32 devices in a mesh: batch: 8 (over z, x), mp: 4 (over y, core).
Axes of the slice: x: 2, y: 2, z: 4, core: 2. Of those that a mesh axis runs over, the one named last changes fastest.
Arguments:
- tokens: bfloat16 [2048, 2048], P('batch'), may hold values from -6 to 6
- lengths: int32 [8], P('batch'), may hold values from 64 to 256, as said below
- cotangent: bfloat16 [2048, 2048], P('batch'), may hold values from -6 to 6
- norm1_gain: float32 [2048], replicated, may hold values from 0.25 to 1.75
- norm1_shift: float32 [2048], replicated, may hold values from -1 to 1
- qkv_weight: bfloat16 [2048, 3, 2048], P(None, None, 'mp'), may hold values from -0.125 to 0.125
- qkv_bias: float32 [3, 32, 64], P(None, 'mp'), may hold values from -1 to 1
- sub1_gain: float32 [32, 64], P('mp'), may hold values from 0.25 to 1.75
- sub1_shift: float32 [32, 64], P('mp'), may hold values from -1 to 1
- out_weight: bfloat16 [2048, 2048], P('mp'), may hold values from -0.125 to 0.125
- out_bias: float32 [2048], replicated, may hold values from -1 to 1
- norm2_gain: float32 [2048], replicated, may hold values from 0.25 to 1.75
- norm2_shift: float32 [2048], replicated, may hold values from -1 to 1
- up_weight: bfloat16 [2048, 8192], P(None, 'mp'), may hold values from -0.125 to 0.125
- up_bias: float32 [8192], P('mp'), may hold values from -1 to 1
- sub2_gain: float32 [8192], P('mp'), may hold values from 0.25 to 1.75
- sub2_shift: float32 [8192], P('mp'), may hold values from -1 to 1
- down_weight: bfloat16 [8192, 2048], P('mp'), may hold values from -0.0625 to 0.0625
- down_bias: float32 [2048], replicated, may hold values from -1 to 1
Outputs:
- result: bfloat16 [2048, 2048], P('batch')
- tokens_grad: bfloat16 [2048, 2048], P('batch')
- norm1_gain_grad: float32 [2048], P('batch')
- norm1_shift_grad: float32 [2048], P('batch')
- qkv_weight_grad: float32 [2048, 3, 2048], P('batch', None, 'mp')
- qkv_bias_grad: float32 [3, 32, 64], P(None, 'mp', 'batch')
- sub1_gain_grad: float32 [32, 64], P('mp', 'batch')
- sub1_shift_grad: float32 [32, 64], P('mp', 'batch')
- out_weight_grad: float32 [2048, 2048], P('mp', 'batch')
- out_bias_grad: float32 [2048], P('batch')
- norm2_gain_grad: float32 [2048], P('batch')
- norm2_shift_grad: float32 [2048], P('batch')
- up_weight_grad: float32 [2048, 8192], P('batch', 'mp')
- up_bias_grad: float32 [64, 128], P('mp', 'batch')
- sub2_gain_grad: float32 [64, 128], P('mp', 'batch')
- sub2_shift_grad: float32 [64, 128], P('mp', 'batch')
- down_weight_grad: float32 [8192, 2048], P('mp', 'batch')
- down_bias_grad: float32 [2048], P('batch')
The draws below stay inside these ranges and needn't reach their ends.
Inputs may be any that keep to these rules, and one draw needn't show every extreme that they name: lengths[r] counts the valid leading tokens of sequence r; some sequence has exactly 256.
All inputs are finite; a program needn't handle non-finite values.
Results may differ from the reference program's by a relative error of at most 0.015.
Values sent between devices are 32-bit elements; how exact they have to be, the bound alone decides.
No kernel may reach another device: no remote copies, remote signals or barrier semaphores. Data moves between devices by JAX's collectives and lax.ppermute only.
A program may use at most 256 MiB of HBM per device.

```python
import math
import jax
import jax.numpy as jnp
from jax import lax

D = 2048
HEADS = 32
HD = 64
FF = 8192
SLOTS = 256
ROWS = 8
QBLOCK = 256


def draw_lengths(key, part):
    lowest = min(100, SLOTS // 4)
    counts = jax.random.randint(jax.random.fold_in(key, 11), (ROWS,), lowest, SLOTS + 1)
    longest = jax.random.randint(jax.random.fold_in(key, 12), (), 0, ROWS)
    return jnp.where(jnp.arange(ROWS) == longest, SLOTS, counts).astype(jnp.int32)


def block_levels(own_key, extent, shards, smallest, top_value):
    loudness = 1.0
    for axis_at, parts in shards:
        steps = jax.random.uniform(jax.random.fold_in(jax.random.fold_in(own_key, 6), axis_at), (parts,), jnp.float32, smallest / len(shards), top_value / len(shards))
        loudness = loudness * jnp.repeat(jnp.exp(steps), extent[axis_at] // parts).reshape((-1,) + (1,) * (len(extent) - 1 - axis_at))
    return loudness


def bell_draw(own_key, extent, scale, reach, cuts=(), kind=jnp.bfloat16):
    entries = jax.random.normal(own_key, extent, jnp.float32) * scale
    if len(cuts) > 0:
        entries = block_levels(own_key, extent, cuts, -0.22, 0.18) * entries
    return jnp.clip(entries, min=-reach, max=reach).astype(kind)


def setup_inputs(seed: int = 0) -> dict:
    seeds = jax.random.split(jax.random.key(seed), 20)
    return {
        "tokens": bell_draw(seeds[0], (ROWS * SLOTS, D), 1.0, 6.0, ((0, 8),)),
        "lengths": draw_lengths(jax.random.fold_in(seeds[19], 71), 0),
        "cotangent": bell_draw(seeds[2], (ROWS * SLOTS, D), 1.0, 6.0, ((0, 8),)),
        "norm1_gain": jnp.clip(1.0 + 0.15 * jax.random.normal(seeds[3], (D,), jnp.float32), 0.25, 1.75),
        "norm1_shift": bell_draw(seeds[4], (D,), 0.2, 1.0, (), jnp.float32),
        "qkv_weight": bell_draw(seeds[5], (D, 3, HEADS * HD), D ** -0.5, 0.125, ((2, 4),)),
        "qkv_bias": bell_draw(seeds[6], (3, HEADS, HD), 0.2, 1.0, ((1, 4),), jnp.float32),
        "sub1_gain": jnp.clip(1.0 + 0.15 * jax.random.normal(seeds[7], (HEADS, HD), jnp.float32), 0.25, 1.75),
        "sub1_shift": bell_draw(seeds[8], (HEADS, HD), 0.2, 1.0, ((0, 4),), jnp.float32),
        "out_weight": bell_draw(seeds[9], (HEADS * HD, D), (HEADS * HD) ** -0.5, 0.125, ((0, 4),)),
        "out_bias": bell_draw(seeds[10], (D,), 0.2, 1.0, (), jnp.float32),
        "norm2_gain": jnp.clip(1.0 + 0.15 * jax.random.normal(seeds[11], (D,), jnp.float32), 0.25, 1.75),
        "norm2_shift": bell_draw(seeds[12], (D,), 0.2, 1.0, (), jnp.float32),
        "up_weight": bell_draw(seeds[13], (D, FF), D ** -0.5, 0.125, ((1, 4),)),
        "up_bias": bell_draw(seeds[14], (FF,), 0.2, 1.0, ((0, 4),), jnp.float32),
        "sub2_gain": jnp.clip(1.0 + 0.15 * jax.random.normal(seeds[15], (FF,), jnp.float32), 0.25, 1.75),
        "sub2_shift": bell_draw(seeds[16], (FF,), 0.2, 1.0, ((0, 4),), jnp.float32),
        "down_weight": bell_draw(seeds[17], (FF, D), FF ** -0.5, 0.0625, ((0, 4),)),
        "down_bias": bell_draw(seeds[18], (D,), 0.2, 1.0, (), jnp.float32),
    }


norm_eps = 1e-05
rope_base = 10000.0
xpos_base = 512.0
masked_score = -1e+30
highest = lax.Precision.HIGHEST

@jax.custom_vjp
def low(v):
    return lax.optimization_barrier(v.astype(jnp.bfloat16)).astype(jnp.float32)

@jax.custom_vjp
def low_back(v):
    return v

def low_keep(v):
    return (low(v), None)

def low_pass(kept, grad):
    return (grad,)

def back_keep(v):
    return (v, None)

def back_low(kept, grad):
    return (low(grad),)
low.defvjp(low_keep, low_pass)
low_back.defvjp(back_keep, back_low)

def normalize(values, gain_row, shift_row):
    center = values - lax.optimization_barrier(jnp.mean(values, axis=-1, keepdims=True))
    spread = lax.optimization_barrier(jnp.mean(center * center, axis=-1, keepdims=True))
    return center * lax.rsqrt(spread + norm_eps) * gain_row + shift_row

def xpos_tables(count_rows, head_width):
    half_width = head_width // 2
    places = jnp.arange(count_rows, dtype=jnp.float32)
    pair_index = jnp.arange(half_width, dtype=jnp.float32)
    frequency = jnp.exp(-math.log(rope_base) * pair_index / half_width)
    angles = places[:, None] * frequency[None, :]
    zeta_base = (2.0 * pair_index + 0.4 * head_width) / (1.4 * head_width)
    powers = (places[:, None] - count_rows // 2) / xpos_base
    factor = jnp.exp(powers * jnp.log(zeta_base)[None, :])
    return (jnp.cos(angles), jnp.sin(angles), factor)

def rotate(values, cosine, sine_table, factor):
    half_width = values.shape[-1] // 2
    first_half = values[..., :half_width]
    second_half = values[..., half_width:]
    cos_rows = cosine[:, None, :]
    sin_rows = sine_table[:, None, :]
    scale_rows = factor[:, None, :]
    return jnp.concatenate([(first_half * cos_rows - second_half * sin_rows) * scale_rows, (second_half * cos_rows + first_half * sin_rows) * scale_rows], axis=-1)

def layer_forward(params, tokens_seq, length_one):
    norm1_gain, norm1_shift, qkv_weight, qkv_bias, sub1_gain, sub1_shift, out_weight, out_bias, norm2_gain, norm2_shift, up_weight, up_bias, sub2_gain, sub2_shift, down_weight, down_bias = params
    attn_width = HEADS * HD
    inv_root = 1.0 / math.sqrt(HD)
    normed = low(normalize(tokens_seq, norm1_gain, norm1_shift))
    mixed_qkv = jnp.dot(normed, qkv_weight.reshape(D, 3 * attn_width), precision=highest) + qkv_bias.reshape(3 * attn_width)
    mixed_qkv = low_back(mixed_qkv).reshape(SLOTS, 3, HEADS, HD)
    cosine, sine_table, factor = xpos_tables(SLOTS, HD)
    queries = low(rotate(mixed_qkv[:, 0], cosine, sine_table, factor))
    key_rows = low(rotate(mixed_qkv[:, 1], cosine, sine_table, 1.0 / factor))
    value_rows = low(mixed_qkv[:, 2])
    places = jnp.arange(SLOTS, dtype=jnp.int32)
    key_valid = places < length_one

    def attend_block(block_start):
        block_q = lax.dynamic_slice_in_dim(queries, block_start.astype(jnp.int32), QBLOCK, 0)
        scores = jnp.einsum('qhd,khd->hqk', block_q, key_rows, precision=highest) * inv_root
        scores = low_back(scores)
        rows_here = block_start.astype(jnp.int32) + jnp.arange(QBLOCK, dtype=jnp.int32)
        allowed = (places[None, :] <= rows_here[:, None]) & key_valid[None, :]
        scores = jnp.where(allowed[None], scores, masked_score)
        attn_probs = jax.nn.softmax(scores, axis=-1)
        return jnp.einsum('hqk,khd->qhd', low(attn_probs), value_rows, precision=highest)
    starts = (jnp.arange(SLOTS // QBLOCK, dtype=jnp.int32) * QBLOCK).astype(jnp.int32)
    attended = lax.map(jax.checkpoint(attend_block), starts).reshape(SLOTS, attn_width)
    attended = low_back(attended)
    sub1_out = low(normalize(attended, sub1_gain.reshape(attn_width), sub1_shift.reshape(attn_width)))
    branch_one = low_back(jnp.dot(sub1_out, out_weight, precision=highest))
    middle = tokens_seq + branch_one + out_bias
    normed2 = low(normalize(middle, norm2_gain, norm2_shift))
    upper_pre = low_back(jnp.dot(normed2, up_weight, precision=highest) + up_bias)
    active = jax.nn.gelu(upper_pre, approximate=False)
    sub2_out = low(normalize(active, sub2_gain, sub2_shift))
    branch_two = low_back(jnp.dot(sub2_out, down_weight, precision=highest))
    return middle + branch_two + down_bias

def reference(tokens, lengths, cotangent, norm1_gain, norm1_shift, qkv_weight, qkv_bias, sub1_gain, sub1_shift, out_weight, out_bias, norm2_gain, norm2_shift, up_weight, up_bias, sub2_gain, sub2_shift, down_weight, down_bias):
    params = tuple((member.astype(jnp.float32) for member in (norm1_gain, norm1_shift, qkv_weight, qkv_bias, sub1_gain, sub1_shift, out_weight, out_bias, norm2_gain, norm2_shift, up_weight, up_bias, sub2_gain, sub2_shift, down_weight, down_bias)))
    seq_tokens = tokens.astype(jnp.float32).reshape(ROWS, SLOTS, D)
    seq_cot = cotangent.astype(jnp.float32).reshape(ROWS, SLOTS, D)

    def per_sequence(totals, member):
        tokens_seq, cot_seq, length_one = member

        def forward(weights_all, tokens_in):
            return layer_forward(weights_all, tokens_in, length_one)
        output_seq, pullback = jax.vjp(forward, params, tokens_seq)
        keep_rows = (jnp.arange(SLOTS, dtype=jnp.int32) < length_one).astype(jnp.float32)[:, None]
        weight_grads, token_grad = pullback(cot_seq * keep_rows)
        totals = jax.tree.map(jnp.add, totals, weight_grads)
        return (totals, (output_seq, token_grad))
    zero_totals = jax.tree.map(jnp.zeros_like, params)
    totals, (outputs, token_grads) = lax.scan(per_sequence, zero_totals, (seq_tokens, seq_cot, lengths))
    return (outputs.reshape(ROWS * SLOTS, D).astype(jnp.bfloat16), token_grads.reshape(ROWS * SLOTS, D).astype(jnp.bfloat16), totals[0], totals[1], totals[2], totals[3], totals[4], totals[5], totals[6], totals[7], totals[8], totals[9], totals[10], totals[11].reshape(FF // 128, 128), totals[12].reshape(FF // 128, 128), totals[13].reshape(FF // 128, 128), totals[14], totals[15])
```

```python
import math

import jax
import jax.numpy as jnp
from jax import lax
from jax.sharding import PartitionSpec as P

D = 2048
HEADS = 32
HD = 64
FF = 8192

norm_eps = 1e-05
rope_base = 10000.0
xpos_base = 512.0
masked_score = -1e30
f32 = jnp.float32
bf16 = jnp.bfloat16
highest = lax.Precision.HIGHEST


def dot(a, b, dims):
    return lax.dot_general(a, b, (dims, ((), ())), preferred_element_type=f32)


def mm(a, b):
    return dot(a, b, ((1,), (0,)))


def mm_nt(a, b):
    return dot(a, b, ((1,), (1,)))


def mm_tn(a, b):
    return dot(a, b, ((0,), (0,)))


def norm_stats(values):
    mean = jnp.mean(values, axis=-1, keepdims=True)
    center = values - mean
    inverse = lax.rsqrt(jnp.mean(center * center, axis=-1, keepdims=True) + norm_eps)
    return center * inverse, inverse


def norm_back(grad, unit, inverse, gain):
    scaled = grad * gain
    return inverse * (
        scaled
        - jnp.mean(scaled, axis=-1, keepdims=True)
        - unit * jnp.mean(scaled * unit, axis=-1, keepdims=True)
    )


def hold(value):
    return lax.optimization_barrier(value)


def swap(axis, value, perm):
    return lax.ppermute(value, axis, perm)


def xpos_tables(places, head_width, center):
    half_width = head_width // 2
    pair_index = jnp.arange(half_width, dtype=f32)
    frequency = jnp.exp(-math.log(rope_base) * pair_index / half_width)
    angles = places[:, None] * frequency[None, :]
    zeta_base = (2.0 * pair_index + 0.4 * head_width) / (1.4 * head_width)
    powers = (places[:, None] - center) / xpos_base
    factor = jnp.exp(powers * jnp.log(zeta_base)[None, :])
    return (jnp.cos(angles), jnp.sin(angles), factor)


def turn(values, cosine, sine, factor):
    half = values.shape[-1] // 2
    one, two = values[..., :half], values[..., half:]
    c, s, e = cosine[:, None, :], sine[:, None, :], factor[:, None, :]
    return jnp.concatenate([(one * c - two * s) * e, (two * c + one * s) * e], axis=-1)


def turn_back(grads, cosine, sine, factor):
    half = grads.shape[-1] // 2
    c, s, e = cosine[:, None, :], sine[:, None, :], factor[:, None, :]
    one, two = grads[..., :half] * e, grads[..., half:] * e
    return jnp.concatenate([one * c + two * s, two * c - one * s], axis=-1)


def gelu_parts(values):
    cdf = 0.5 * (1.0 + lax.erf(values * (2.0**-0.5)))
    density = jnp.exp(-0.5 * values * values) * (1.0 / math.sqrt(2.0 * math.pi))
    return values * cdf, cdf + values * density


def make_local(nb, nm):
    pair = [(i, i ^ 1) for i in range(nm)]
    cross = [(i, i ^ 2) for i in range(nm)]
    full = nb == 8 and nm == 4
    zs = nb // 2

    def zx(moves):
        return [(s * 2 + x, d * 2 + x) for s, d in moves for x in range(2)]

    x_flip = [(i, i ^ 1) for i in range(nb)]
    z_flip = [(i, i ^ 2) for i in range(nb)]
    z_half = [(i, i ^ 4) for i in range(nb)]
    up = zx([(z, z + 1) for z in range(zs - 1)])
    down = zx([(z + 1, z) for z in range(zs - 1)])

    def local(
        tokens,
        lengths,
        cotangent,
        norm1_gain,
        norm1_shift,
        qkv_weight,
        qkv_bias,
        sub1_gain,
        sub1_shift,
        out_weight,
        out_bias,
        norm2_gain,
        norm2_shift,
        up_weight,
        up_bias,
        sub2_gain,
        sub2_shift,
        down_weight,
        down_bias,
    ):
        length = lengths[0]
        rows = tokens.shape[0]
        half = rows // 2
        width = out_weight.shape[0]
        heads = width // HD
        hidden = up_weight.shape[1]
        attn_width = width * nm
        ff_width = hidden * nm
        inv_root = 1.0 / math.sqrt(HD)
        block = D // nb
        index = lax.axis_index("batch")
        odd = lax.axis_index("mp") % 2

        def roll(value):
            return jnp.concatenate(
                [
                    lax.dynamic_slice_in_dim(value, odd * half, half, 0),
                    lax.dynamic_slice_in_dim(value, (1 - odd) * half, half, 0),
                ],
                axis=0,
            )

        def unroll(mine, other):
            return jnp.concatenate(
                [jnp.where(odd == 0, mine, other), jnp.where(odd == 0, other, mine)], axis=0
            )

        def reduce_half(value):
            total = value[:half] + swap("mp", value[half:], pair)
            return total + swap("mp", total, cross)

        def pair_join(value):
            return jnp.concatenate([value, swap("mp", value, pair)], axis=0)

        def mp_sum(value):
            value = value + swap("mp", value, pair)
            return value + swap("mp", value, cross)

        places = (jnp.arange(rows, dtype=jnp.int32) + odd * half) % rows
        keep = (places < length).astype(f32)[:, None]
        x = roll(tokens).astype(f32)
        dy = roll(cotangent).astype(f32) * keep
        dyl = dy.astype(bf16)

        one = jnp.where(length < 0, 2.0, 1.0).astype(f32)

        def narrow(value):
            return (value * one).astype(bf16)

        g1 = sub1_gain.reshape(width)
        c1 = sub1_shift.reshape(width)
        vecs = jnp.stack([g1, c1])
        own_vecs = lax.dot_general(
            vecs, out_weight.astype(f32), (((1,), (0,)), ((), ())), precision=highest
        )
        w_vecs = mp_sum(own_vecs)
        gain_out, shift_out = w_vecs[0], w_vecs[1]

        a_unit, a_inverse = norm_stats(x)
        a_wide = a_unit * norm1_gain + norm1_shift
        a = a_wide.astype(bf16)
        mixed = [
            mm(a, qkv_weight[:, j, :]) + qkv_bias[j].reshape(width) for j in range(3)
        ]
        cosine, sine, factor = xpos_tables(places.astype(f32), HD, rows // 2)
        q = turn(mixed[0].reshape(rows, heads, HD), cosine, sine, factor).astype(bf16)
        k = turn(mixed[1].reshape(rows, heads, HD), cosine, sine, 1.0 / factor).astype(bf16)
        v = mixed[2].reshape(rows, heads, HD).astype(bf16)
        allowed = (places[None, :] <= places[:, None]) & (places < length)[None, :]
        scores = jnp.einsum("qhd,khd->hqk", q, k, preferred_element_type=f32) * inv_root
        scores = jnp.where(allowed[None], scores, masked_score)
        peak = jnp.max(scores, axis=-1, keepdims=True)
        weights = jnp.exp(scores - peak)
        probs = weights / jnp.sum(weights, axis=-1, keepdims=True)
        probs_low = probs.astype(bf16)
        o = jnp.einsum("hqk,khd->qhd", probs_low, v, preferred_element_type=f32).reshape(
            rows, width
        )
        mean_loc = jnp.mean(o, axis=-1, keepdims=True)
        o_center = o - mean_loc
        stats = jnp.concatenate(
            [mean_loc, jnp.sum(o_center * o_center, axis=-1, keepdims=True)], axis=1
        )

        def flip(value):
            return jnp.concatenate([value[half:], value[:half]], axis=0)

        def join_o(stats, other, count):
            gap = stats[:, 0:1] - other[:, 0:1]
            return jnp.concatenate(
                [
                    0.5 * (stats[:, 0:1] + other[:, 0:1]),
                    stats[:, 1:2] + other[:, 1:2] + (0.5 * count) * gap * gap,
                ],
                axis=1,
            )

        stats = join_o(stats, swap("mp", flip(stats), pair), width)
        stats = join_o(stats, swap("mp", stats, cross), 2 * width)
        mu1 = stats[:, 0:1]
        inv1 = lax.rsqrt(stats[:, 1:2] / attn_width + norm_eps)
        partial = mm((o_center * g1).astype(bf16), out_weight) + mean_loc * own_vecs[0]
        branch = inv1[:half] * (reduce_half(partial) - mu1[:half] * gain_out)
        h1 = x[:half] + (branch + shift_out) + out_bias
        z_unit = (o - mu1) * inv1
        z_wide = z_unit * g1 + c1
        z = z_wide.astype(bf16)
        b_unit, b_inverse = norm_stats(h1)
        b_half = b_unit * norm2_gain + norm2_shift

        def first_pass(b_rows, dyl_rows):
            u = mm(b_rows, up_weight) + up_bias
            g, slope = gelu_parts(u)
            dw = mm_nt(dyl_rows, down_weight)
            scaled = dw * sub2_gain
            mean = jnp.mean(g, axis=-1)
            center = g - mean[:, None]
            stats = jnp.stack(
                [
                    mean,
                    jnp.sum(center * center, axis=-1),
                    jnp.sum(scaled, axis=-1),
                    jnp.sum(scaled * center, axis=-1),
                ]
            )
            return g, slope, dw, stats

        def join_g(one, two, count):
            mean = 0.5 * (one[0] + two[0])
            gap = one[0] - two[0]
            return jnp.stack(
                [
                    mean,
                    one[1] + two[1] + (0.5 * count) * gap * gap,
                    one[2] + two[2],
                    one[3] + two[3] + one[2] * (one[0] - mean) + two[2] * (two[0] - mean),
                ]
            )

        def all_stats(stats):
            turned = stats.reshape(4, -1, 2, half)[:, :, ::-1, :].reshape(stats.shape)
            stats = join_g(stats, swap("mp", turned, pair), hidden)
            return join_g(stats, swap("mp", stats, cross), 2 * hidden)

        def second_pass(g, slope, dw, stats):
            inverse = lax.rsqrt(stats[1] / ff_width + norm_eps)[:, None]
            unit = (g - stats[0][:, None]) * inverse
            w = (unit * sub2_gain + sub2_shift).astype(bf16)
            dg = inverse * (
                dw * sub2_gain
                - stats[2][:, None] / ff_width
                - unit * (inverse * (stats[3][:, None] / ff_width))
            )
            du = (dg * slope).astype(bf16)
            return w, du, jnp.sum(dw * unit, axis=0), jnp.sum(dw, axis=0)

        def gather_rows(mine):
            near_x = swap("batch", mine, x_flip)
            u0 = swap("batch", mine, up)
            d0 = swap("batch", mine, down)
            at = index // 2
            got_a = jnp.where(at == 0, d0, u0)
            far_a = swap("batch", got_a, x_flip)
            u1 = swap("batch", u0, [p for p in up if p[0] >= 2])
            d1 = swap("batch", d0, [p for p in down if p[0] < 2 * zs - 2])
            got_b = jnp.where(at >= 2, u1, d1)
            far_b = swap("batch", got_b, x_flip)
            u2 = swap("batch", u1, [p for p in up if p[0] >= 4])
            d2 = swap("batch", d1, [p for p in down if p[0] < 2 * zs - 4])
            got_c = jnp.where(at == 0, d2, jnp.where(at == 3, u2, d0))
            far_c = swap("batch", got_c, x_flip)
            parts = []
            for piece in (near_x, got_a, far_a, got_b, far_b, got_c, far_c):
                parts += [piece, swap("mp", piece, pair)]
            return narrow(jnp.concatenate(parts, axis=0))

        if full:
            dyl_far = gather_rows(dy[:half])
            b_far = gather_rows(b_half)
        b = narrow(pair_join(b_half))
        g, slope, dw, stats = first_pass(b, dyl)
        w, du, sub2_gain_sum, sub2_shift_sum = second_pass(g, slope, dw, all_stats(stats))

        db = reduce_half(mm_nt(du, up_weight))
        dh1_half = dy[:half] + norm_back(db, b_unit, b_inverse, norm2_gain)
        sums = [
            jnp.sum(db * b_unit, axis=0),
            jnp.sum(db, axis=0),
            jnp.sum(dh1_half, axis=0),
        ]
        dhl_half = dh1_half.astype(bf16).astype(f32)
        row_sums = pair_join(
            jnp.concatenate(
                [
                    jnp.sum(dhl_half * gain_out, axis=-1, keepdims=True),
                    jnp.sum(dhl_half * branch, axis=-1, keepdims=True),
                ],
                axis=1,
            )
        )
        dh1 = pair_join(dh1_half)
        dhl = narrow(dh1)
        dz = mm_nt(dhl, out_weight)
        do = inv1 * (
            dz * g1
            - row_sums[:, 0:1] / attn_width
            - z_unit * (row_sums[:, 1:2] / attn_width)
        )
        sub1_gain_sum = jnp.sum(dz * z_unit, axis=0)
        sub1_shift_sum = jnp.sum(dz, axis=0)
        do = do.astype(bf16).reshape(rows, heads, HD)

        dprobs = jnp.einsum("qhd,khd->hqk", do, v, preferred_element_type=f32)
        dv = jnp.einsum("hqk,qhd->khd", probs_low, do, preferred_element_type=f32)
        inner = jnp.sum(probs * dprobs, axis=-1, keepdims=True)
        dscores = (probs * (dprobs - inner)).astype(bf16)
        dq = jnp.einsum("hqk,khd->qhd", dscores, k, preferred_element_type=f32) * inv_root
        dk = jnp.einsum("hqk,qhd->khd", dscores, q, preferred_element_type=f32) * inv_root
        dm = [
            turn_back(dq, cosine, sine, factor).reshape(rows, width),
            turn_back(dk, cosine, sine, 1.0 / factor).reshape(rows, width),
            dv.reshape(rows, width),
        ]
        dm_low = [member.astype(bf16) for member in dm]
        bias_sum = jnp.concatenate([jnp.sum(member.astype(f32), axis=0) for member in dm_low])
        da = reduce_half(sum(mm_nt(dm_low[j], qkv_weight[:, j, :]) for j in range(3)))
        sums += [jnp.sum(da * a_unit[:half], axis=0), jnp.sum(da, axis=0)]
        tokens_half = dh1_half + norm_back(da, a_unit[:half], a_inverse[:half], norm1_gain)
        tokens_grad = narrow(unroll(tokens_half, swap("mp", tokens_half, pair)))

        result_half = h1 + reduce_half(mm(w, down_weight)) + down_bias
        result = narrow(unroll(result_half, swap("mp", result_half, pair)))

        lanes = hidden // 128
        d_sums = jnp.stack(sums)
        d_sums = d_sums + swap("mp", d_sums, pair)
        h_sums = jnp.concatenate([sub1_gain_sum, sub1_shift_sum, bias_sum])
        if not full:

            def scatter(value, axis):
                return lax.psum_scatter(value, "batch", scatter_dimension=axis, tiled=True)

            d_sums = scatter(d_sums, 1)
            down_bias_sum = scatter(jnp.sum(dy, axis=0), 0)
            h_sums = lax.psum(h_sums, "batch")
            wide = jnp.stack(
                [jnp.sum(du.astype(f32), axis=0), sub2_gain_sum, sub2_shift_sum]
            ).reshape(3, lanes, 128)
            wide = scatter(wide, 2)
            grad_qkv = scatter(jnp.stack([mm_tn(a, m) for m in dm_low], axis=1), 0)
            grad_out = scatter(mm_tn(z, dhl), 1)
            grad_up = scatter(mm_tn(b, du), 0)
            grad_down = scatter(mm_tn(w, dyl), 1)
        else:

            def column(value, at):
                return lax.dynamic_slice_in_dim(value, at * block, block, 1)

            for perm in (x_flip, z_flip, z_half):
                h_sums = h_sums + swap("batch", h_sums, perm)
                d_sums = d_sums + swap("batch", d_sums, perm)
            d_sums = column(d_sums, index)
            b_all = jnp.concatenate([b, b_far], axis=0)
            dyl_all = jnp.concatenate([dyl, dyl_far], axis=0)
            g2, slope2, dw2, stats2 = first_pass(b_far, dyl_far)
            w2, du2, gain2, shift2 = second_pass(g2, slope2, dw2, all_stats(stats2))
            w_all = jnp.concatenate([w, w2], axis=0)
            du_all = jnp.concatenate([du, du2], axis=0)
            wide = jnp.stack(
                [
                    jnp.sum(du_all.astype(f32), axis=0),
                    sub2_gain_sum + gain2,
                    sub2_shift_sum + shift2,
                ]
            ).reshape(3, lanes, 128)
            wide = lax.dynamic_slice_in_dim(wide, index * (128 // nb), 128 // nb, 2)
            dyl_mine = column(dyl_all, index)
            down_bias_sum = jnp.sum(dyl_mine.astype(f32), axis=0)
            grad_up = mm_tn(column(b_all, index), du_all)
            grad_down = mm_tn(w_all, dyl_mine)

            def square_rows(value):
                near = swap("batch", value, z_flip)
                return [value, swap("batch", value, x_flip), near, swap("batch", near, x_flip)]

            def square_pieces(value):
                def both(at):
                    return jnp.concatenate([column(value, at), column(value, at ^ 4)], axis=1)

                sent = jnp.concatenate(
                    [
                        swap("batch", both(index ^ s)[:half], [(i, i ^ s) for i in range(nb)])
                        for s in (1, 2, 3)
                    ],
                    axis=1,
                )
                other = swap("mp", sent, pair)
                out = [both(index)]
                for s in range(3):
                    cols = slice(s * 2 * block, (s + 1) * 2 * block)
                    out += [sent[:, cols], other[:, cols]]
                return narrow(jnp.concatenate(out, axis=0))

            a_sq = square_pieces(a_wide)
            z_sq = narrow(jnp.concatenate(square_rows(z_wide), axis=0))
            dhl_sq = square_pieces(dh1)
            grad_out = mm_tn(z_sq, dhl_sq[:, :block]) + swap(
                "batch", mm_tn(z_sq, dhl_sq[:, block:]), z_half
            )
            grads = []
            for j in (2, 0, 1):
                m_sq = narrow(jnp.concatenate(square_rows(dm[j]), axis=0))
                grads.append(
                    mm_tn(a_sq[:, :block], m_sq)
                    + swap("batch", mm_tn(a_sq[:, block:], m_sq), z_half)
                )
            grad_qkv = jnp.stack([grads[1], grads[2], grads[0]], axis=1)
        per = HD // nb

        def own_part(value, shape):
            return lax.dynamic_slice_in_dim(value.reshape(shape), index * per, per, len(shape) - 1)

        return (
            result,
            tokens_grad,
            d_sums[3],
            d_sums[4],
            grad_qkv,
            own_part(h_sums[2 * width :], (3, heads, HD)),
            own_part(h_sums[:width], (heads, HD)),
            own_part(h_sums[width : 2 * width], (heads, HD)),
            grad_out,
            d_sums[2],
            d_sums[0],
            d_sums[1],
            grad_up,
            wide[0],
            wide[1],
            wide[2],
            grad_down,
            down_bias_sum,
        )

    return local


def solution(mesh):
    in_specs = (
        P("batch", None),
        P("batch"),
        P("batch", None),
        P(),
        P(),
        P(None, None, "mp"),
        P(None, "mp", None),
        P("mp", None),
        P("mp", None),
        P("mp", None),
        P(),
        P(),
        P(),
        P(None, "mp"),
        P("mp"),
        P("mp"),
        P("mp"),
        P("mp", None),
        P(),
    )
    out_specs = (
        P("batch", None),
        P("batch", None),
        P("batch"),
        P("batch"),
        P("batch", None, "mp"),
        P(None, "mp", "batch"),
        P("mp", "batch"),
        P("mp", "batch"),
        P("mp", "batch"),
        P("batch"),
        P("batch"),
        P("batch"),
        P("batch", "mp"),
        P("mp", "batch"),
        P("mp", "batch"),
        P("mp", "batch"),
        P("mp", "batch"),
        P("batch"),
    )
    local = make_local(mesh.shape["batch"], mesh.shape["mp"])
    return jax.shard_map(local, mesh=mesh, in_specs=in_specs, out_specs=out_specs, check_vma=False)
```

```python
import functools
import math

import jax
import jax.numpy as jnp
import numpy as np
from jax import lax
from jax.experimental import pallas as pl
from jax.experimental.pallas import tpu as pltpu
from jax.sharding import PartitionSpec as P

HD = 64
QUAD = 4 * HD
PAIR = 2 * HD

norm_eps = 1e-05
rope_base = 10000.0
xpos_base = 512.0
masked_score = -1e30
root_half = 2.0**-0.5
density_scale = 1.0 / math.sqrt(2.0 * math.pi)
f32 = jnp.float32
bf16 = jnp.bfloat16
MIB = 1 << 20


def dot(a, b, dims):
    return lax.dot_general(a, b, (dims, ((), ())), preferred_element_type=f32)


def mm(a, b):
    return dot(a, b, ((1,), (0,)))


def mm_nt(a, b):
    return dot(a, b, ((1,), (1,)))


def mm_tn(a, b):
    return dot(a, b, ((0,), (0,)))


def row_mean(value):
    return jnp.mean(value, axis=-1, keepdims=True)


def row_sum(value):
    return jnp.sum(value, axis=-1, keepdims=True)


def unit_rows(value):
    center = value - row_mean(value)
    inverse = lax.rsqrt(row_mean(center * center) + norm_eps)
    return center * inverse, inverse


def unit_back(grad, unit, inverse, gain):
    scaled = grad * gain
    return inverse * (scaled - row_mean(scaled) - unit * row_mean(scaled * unit))


def turn_tables(count):
    half = HD // 2
    places = np.arange(count, dtype=np.float64)[:, None]
    pair = np.arange(half, dtype=np.float64)[None, :]
    angles = places * rope_base ** (-2.0 * pair / HD)
    zeta = (2.0 * pair + 0.4 * HD) / (1.4 * HD)
    factor = zeta ** ((places - count // 2) / xpos_base)
    tables = []
    for scale in (factor, 1.0 / factor):
        tables.append(np.tile(np.cos(angles) * scale, (1, 4)))
        tables.append(np.tile(np.concatenate([-np.sin(angles), np.sin(angles)], 1), (1, 2))
                      * np.tile(scale, (1, 4)))
    return np.stack(tables).astype(np.float32)


def half_swap(value):
    lane = lax.broadcasted_iota(jnp.int32, value.shape, 1)
    return jnp.where(
        (lane & 32) == 0,
        pltpu.roll(value, value.shape[1] - 32, 1),
        pltpu.roll(value, 32, 1),
    )


def whole(shape):
    return pl.BlockSpec(shape, lambda *_: (0,) * len(shape))


def shape_of(shape, dtype=f32):
    return jax.ShapeDtypeStruct(shape, dtype)


def call(body, grid, ins, outs, shapes, scratch=(), tokens=0, aliases=None):
    count = len(ins)

    def kernel(meta, *refs):
        body(meta, *refs[:count], *refs[count + tokens :])

    return pl.pallas_call(
        kernel,
        grid_spec=pltpu.PrefetchScalarGridSpec(
            num_scalar_prefetch=1,
            grid=grid,
            in_specs=list(ins) + [pl.BlockSpec(memory_space=pl.ANY)] * tokens,
            out_specs=outs,
            scratch_shapes=list(scratch),
        ),
        out_shape=shapes,
        compiler_params=pltpu.CompilerParams(
            dimension_semantics=("arbitrary",) * len(grid), vmem_limit_bytes=64 * MIB
        ),
        input_output_aliases=aliases or {},
    )


class Order:
    def __init__(self, meta):
        self.meta = meta
        self.last = []

    def run(self, body, grid, ins, outs, shapes, args, scratch=(), wait=(), aliases=None):
        extra = list(wait) + self.last
        made = call(body, grid, ins, outs, shapes, scratch, len(extra), aliases)(
            self.meta, *args, *extra
        )
        self.last = [made[0] if isinstance(made, (list, tuple)) else made]
        return made


def half_at(meta, which, half):
    return pl.ds(pl.multiple_of(((meta[0] + which) % 2) * half, half), half)


def spread(ref, count, first=0):
    return jnp.concatenate([ref[pl.ds(first + i, 1), :] for i in range(count)], axis=1)


def mask_kernel(meta, cot_mine, cot_other, mine, other):
    size = mine.shape[0]
    tiles = pl.num_programs(0)
    for which, ref, out in ((0, cot_mine, mine), (1, cot_other, other)):
        first = (((meta[0] + which) % 2) * tiles + pl.program_id(0)) * size
        place = first + lax.broadcasted_iota(jnp.int32, (size, 1), 0)
        out[...] = ref[...].astype(f32) * jnp.where(place < meta[1], 1.0, 0.0)


def send_pieces(meta, first, second, outs, nb, block):
    for s, out in enumerate(outs):
        at = meta[2] ^ (s + 1)
        for part, where in ((0, at), (1, at ^ 4)):
            cols = pl.ds(pl.multiple_of(where * block, block), block)
            out[:, part * block : (part + 1) * block] = first[:, cols].astype(f32)
            out[:, (part + 2) * block : (part + 3) * block] = second[:, cols]


def flip_rows(value, half):
    return jnp.concatenate(
        [
            value[(i ^ 1) * half : ((i ^ 1) + 1) * half]
            for i in range(value.shape[0] // half)
        ],
        axis=0,
    )


def join_two(one, two, count):
    mean = 0.5 * (one[0] + two[0])
    gap = one[0] - two[0]
    joined = [mean, one[1] + two[1] + (0.5 * count) * gap * gap]
    if len(one) > 2:
        joined += [
            one[2] + two[2],
            one[3] + two[3] + one[2] * (one[0] - mean) + two[2] * (two[0] - mean),
        ]
    return joined


def join_all(ref, odd, count):
    cols = []
    for i in range(ref.shape[0]):
        value = ref[i]
        half = value.shape[0] // 2
        value = jnp.where(odd == i % 2, value, flip_rows(value, half))
        cols.append([value[:, c : c + 1] for c in range(4)])
    while len(cols) > 1:
        cols = [join_two(cols[i], cols[i + 1], count) for i in range(0, len(cols), 2)]
        count *= 2
    return cols[0]


def diagonal(count):
    return lax.broadcasted_iota(jnp.int32, (count, count), 0) == lax.broadcasted_iota(
        jnp.int32, (count, count), 1
    )


def as_row(column):
    return jnp.sum(jnp.where(diagonal(column.shape[0]), column, 0.0), axis=0, keepdims=True)


def as_column(row):
    return row_sum(jnp.where(diagonal(row.shape[1]), row, 0.0))


def attend_kernel(meta, tok, gain, shift, weight, bias, sub_gain, sub_shift, out_w, table,
                  a_out, q_out, k_out, v_out, p_out, o_out, y_mine, y_other,
                  a_low, o_all):
    rows, width = o_all.shape
    half = rows // 2
    step = pl.program_id(0)
    places = lax.broadcasted_iota(jnp.int32, (rows, 1), 0) ^ (meta[0] * half)
    keys = lax.broadcasted_iota(jnp.int32, (1, rows), 1) ^ (meta[0] * half)
    allowed = (keys <= places) & (keys < meta[1])

    @pl.when(step == 0)
    def _():
        for which in range(2):
            unit, _ = unit_rows(tok[half_at(meta, which, half), :].astype(f32))
            wide = unit * gain[...] + shift[...]
            a_low[which * half : (which + 1) * half, :] = wide.astype(bf16)
        a_out[...] = a_low[...]

    turned = []
    for j in range(3):
        m = mm(a_low[...], weight[j])
        m = m + jnp.concatenate(
            [bias[j, pl.ds(step * 4 + i, 1), :] for i in range(4)], axis=1
        )
        if j < 2:
            flipped = half_swap(m)
            parts = []
            for which in range(2):
                at = half_at(meta, which, half)
                here = slice(which * half, (which + 1) * half)
                c = jnp.concatenate([table[2 * j, at, :]] * 2, axis=1)
                s = jnp.concatenate([table[2 * j + 1, at, :]] * 2, axis=1)
                parts.append(m[here] * c + flipped[here] * s)
            m = jnp.concatenate(parts, axis=0)
        turned.append(m.astype(bf16))
    q, k, v = turned
    q = q * jnp.asarray(1.0 / math.sqrt(HD), bf16)
    q_out[...] = q
    k_out[...] = k
    v_out[...] = v
    lane = lax.broadcasted_iota(jnp.int32, (1, PAIR), 1)
    for p in range(2):
        here = slice(p * PAIR, (p + 1) * PAIR)
        total = None
        for h in range(2):
            mask = (lane // HD) == h
            scores = mm_nt(jnp.where(mask, q[:, here], jnp.zeros_like(q[:, here])), k[:, here])
            scores = jnp.where(allowed, scores, masked_score)
            weights = jnp.exp(scores - jnp.max(scores, axis=-1, keepdims=True))
            probs = weights / row_sum(weights)
            p_out[p * 2 + h] = probs
            part = mm(
                probs.astype(bf16), jnp.where(mask, v[:, here], jnp.zeros_like(v[:, here]))
            )
            total = part if total is None else total + part
        o_all[:, pl.ds(pl.multiple_of(step * QUAD + p * PAIR, PAIR), PAIR)] = total

    @pl.when(step == pl.num_programs(0) - 1)
    def _():
        o = o_all[...]
        o_out[...] = o
        mean = row_mean(o)
        center = o - mean
        stat_rows = jnp.concatenate([as_row(mean), as_row(row_sum(center * center))], axis=0)
        heads = width // HD
        gain_row, shift_row = spread(sub_gain, heads), spread(sub_shift, heads)
        pieces = []
        for row in (gain_row, shift_row):
            for _ in range(3):
                low = row.astype(bf16)
                pieces.append(low)
                row = row - low.astype(f32)
        vecs = mm(jnp.concatenate(pieces + [jnp.zeros((2, width), bf16)], axis=0), out_w[...])
        gain_out = vecs[0:1] + vecs[1:2] + vecs[2:3]
        shift_out = vecs[3:4] + vecs[4:5] + vecs[5:6]
        extra = jnp.concatenate([gain_out, shift_out, jnp.zeros((6, vecs.shape[1]), f32)], axis=0)
        low = (center * gain_row).astype(bf16)
        for which, out in ((1, y_other), (0, y_mine)):
            here = slice(which * half, (which + 1) * half)
            out[0:half, :] = mm(low[here], out_w[...]) + mean[here] * gain_out
            out[half : half + 8, :] = extra
            out[half + 2 : half + 4, 0:rows] = stat_rows


def stat_rows_of(ref):
    half = ref.shape[1] // 2
    return [ref[i : i + 1, :] for i in (2, 3)], [
        jnp.concatenate([ref[i : i + 1, half:], ref[i : i + 1, 0:half]], axis=1) for i in (2, 3)
    ]


def pair_kernel(width, meta, mine, other, out):
    half = out.shape[0] - 8
    rows = 2 * half
    out[...] = mine[...] + other[...]
    here, _ = stat_rows_of(mine.at[half : half + 8, 0:rows])
    _, there = stat_rows_of(other.at[half : half + 8, 0:rows])
    joined = join_two(here, there, width)
    out[half + 2 : half + 4, 0:rows] = jnp.concatenate(joined, axis=0)


def middle_kernel(attn_width, meta, one, two, one_extra, two_extra, tok, bias, gain, shift,
                   h_out, branch_out, b_out, vec_out, stats):
    size = h_out.shape[0]
    step = pl.program_id(0)

    @pl.when(step == 0)
    def _():
        rows = stats.shape[0]
        here, _ = stat_rows_of(one_extra.at[:, 0:rows])
        there, _ = stat_rows_of(two_extra.at[:, 0:rows])
        mean, m2 = join_two(here, there, attn_width // 2)
        inverse = lax.rsqrt(m2 * (1.0 / attn_width) + norm_eps)
        stats[...] = jnp.concatenate([as_column(mean), as_column(inverse)], axis=1)
        vec_out[...] = one_extra[...] + two_extra[...]

    at = pl.ds(pl.multiple_of(step * size, size), size)
    branch = stats[at, 1:2] * ((one[...] + two[...]) - stats[at, 0:1] * vec_out[0:1, :])
    branch_out[...] = branch
    h1 = tok[...].astype(f32) + (branch + vec_out[1:2, :]) + bias[...]
    h_out[...] = h1
    unit, _ = unit_rows(h1)
    b_out[...] = unit * gain[...] + shift[...]


def unit_kernel(meta, o_all, stats, sub_gain, sub_shift, z_out):
    heads = o_all.shape[1] // HD
    unit = (o_all[...] - stats[:, 0:1]) * stats[:, 1:2]
    z_out[...] = unit * spread(sub_gain, heads) + spread(sub_shift, heads)


def dw_kernel(meta, mine, other, weight, out, low):
    half = mine.shape[0]

    @pl.when(pl.program_id(0) == 0)
    def _():
        low[0:half, :] = mine[...].astype(bf16)
        low[half:, :] = other[...].astype(bf16)

    out[...] = mm_nt(low[...], weight[...]).astype(bf16)


def first_kernel(meta, mine, other, weight, bias, gain, dw, g_out, slope_out, stat_out, low,
                 mean_s, m2_s, s1_s, s2_s):
    half = mine.shape[0]
    step = pl.program_id(0)
    span = weight.shape[1]

    @pl.when(step == 0)
    def _():
        low[0:half, :] = mine[...].astype(bf16)
        low[half:, :] = other[...].astype(bf16)
        for ref in (mean_s, m2_s, s1_s, s2_s):
            ref[...] = jnp.zeros_like(ref)

    done = step.astype(f32)
    share = 1.0 / (done + 1.0)
    u = mm(low[...], weight[...]) + bias[...]
    cdf = 0.5 + 0.5 * lax.erf(u * root_half)
    density = jnp.exp(-0.5 * (u * u)) * density_scale
    g = u * cdf
    slope_out[...] = (cdf + u * density).astype(bf16)
    g_out[...] = g.astype(bf16)
    scaled = dw[...].astype(f32) * gain[...]
    mean_c = row_mean(g)
    center = g - mean_c
    s1_c = row_sum(scaled)
    s2_c = row_sum(scaled * center)
    gap = mean_c - mean_s[...]
    mean_new = mean_s[...] + gap * share
    m2_s[...] += row_sum(center * center) + gap * gap * (span * done * share)
    s2_s[...] += s2_c + s1_s[...] * (mean_s[...] - mean_new) + s1_c * (mean_c - mean_new)
    s1_s[...] += s1_c
    mean_s[...] = mean_new

    @pl.when(step == pl.num_programs(0) - 1)
    def _():
        stat_out[...] = jnp.concatenate([mean_s[...], m2_s[...], s1_s[...], s2_s[...]], axis=1)


def hidden_stats(ref, odd, out, count, ff_width):
    mean, m2, s1, s2 = join_all(ref, odd, count)
    inverse = lax.rsqrt(m2 * (1.0 / ff_width) + norm_eps)
    out[...] = jnp.concatenate(
        [mean, inverse, s1 * (1.0 / ff_width), inverse * s2 * (1.0 / ff_width)], axis=1
    )


def hidden_rows(g, slope, dw, stats, gain, shift):
    inverse = stats[:, 1:2]
    unit = (g.astype(f32) - stats[:, 0:1]) * inverse
    w = (unit * gain + shift).astype(bf16)
    dw = dw.astype(f32)
    dg = inverse * (dw * gain - stats[:, 2:3] - unit * stats[:, 3:4])
    return w, (dg * slope.astype(f32)).astype(bf16), dw * unit, dw


def back_kernel(ff_width, span, meta, g, slope, dw, parts, gain, shift, weight, w_out, du_out, stats,
                sum_out, db_mine, db_other):
    half = db_mine.shape[0]

    @pl.when(pl.program_id(0) == 0)
    def _():
        hidden_stats(parts, meta[0], stats, ff_width // parts.shape[0], ff_width)
        for c in range(g.shape[1] // span):
            at = slice(c * span, (c + 1) * span)
            w, du, gain_part, dw_wide = hidden_rows(
                g[:, at], slope[:, at], dw[:, at], stats[...], gain[:, at], shift[:, at]
            )
            w_out[:, at] = w
            du_out[:, at] = du
            sum_out[:, at] = hidden_sums(du, gain_part, dw_wide)

    part = mm_nt(du_out[...], weight[...])
    db_mine[...] = part[0:half, :]
    db_other[...] = part[half:, :]


def hidden_sums(du, gain_part, dw_wide):
    return jnp.concatenate(
        [
            jnp.sum(du.astype(f32), axis=0, keepdims=True),
            jnp.sum(gain_part, axis=0, keepdims=True),
            jnp.sum(dw_wide, axis=0, keepdims=True),
            jnp.zeros((5, du.shape[1]), f32),
        ],
        axis=0,
    )


def pack_kernel(meta, *refs):
    sources, (out, buffer, sems) = refs[:8], refs[8:]
    where = meta[2] // 2
    inner = (where == 1) | (where == 2)
    half = buffer.shape[1]

    def loads(first):
        return [
            pltpu.make_async_copy(sources[2 * i + first], buffer.at[i], sems.at[i])
            for i in range(4)
        ]

    @pl.when(inner)
    def _():
        for copy in loads(0):
            copy.start()

    @pl.when(jnp.logical_not(inner))
    def _():
        for copy in loads(1):
            copy.start()

    stores = []
    for i, copy in enumerate(loads(0)):
        copy.wait()
        store = pltpu.make_async_copy(
            buffer.at[i], out.at[i * half : (i + 1) * half, :], sems.at[4 + i]
        )
        store.start()
        stores.append(store)
    for store in stores:
        store.wait()


def far_kernel(starts, lower, own, meta, *refs):
    groups = len(starts)
    count = 1 + max(source for pair in starts for source, _ in pair)
    b_src, d_src, refs = refs[:count], refs[count : 2 * count], refs[2 * count :]
    stat_refs, rest = refs[: 2 * groups], refs[2 * groups :]
    up_w, up_b, gain, shift, down_w = rest[:5]
    rest = rest[5:]
    if own:
        w_own, du_own, sum_own, *cols = rest[:7]
        rest = rest[7:]
        ins = ()
    else:
        ins, rest = rest[:3], rest[3:]
    (up_out, down_out, near_out), (b_low, d_low, stats, buffer, sem) = rest[:3], rest[3:]
    half = buffer.shape[1]
    rows = 2 * half
    block = up_out.shape[0]
    where = meta[2] // 2
    inner = (where == 1) | (where == 2)
    mine = pl.ds(pl.multiple_of(meta[2] * block, block), block)
    near = pl.ds(pl.multiple_of((meta[2] ^ 1) * block, block), block)

    @pl.when(pl.program_id(0) == 0)
    def _():
        copies = []
        for n, pair in enumerate(starts):
            for k, (refs_k, low) in enumerate(((b_src, b_low), (d_src, d_low))):
                for i, (source, first) in enumerate(pair):
                    slot = 4 * n + 2 * k + i
                    copy = pltpu.make_async_copy(
                        refs_k[source].at[first + k * lower : first + k * lower + half, :], buffer.at[slot], sem.at[slot]
                    )
                    copy.start()
                    copies.append((copy, low, n * rows + i * half, slot))
        for n in range(groups):
            value = jnp.where(inner, stat_refs[2 * n][...], stat_refs[2 * n + 1][...])
            if lower == 0:
                value = jnp.where(meta[0] == 0, value, flip_rows(value, half))
            stats[n * rows : (n + 1) * rows, :] = value
        for copy, low, at, slot in copies:
            copy.wait()
            low[at : at + half, :] = buffer[slot].astype(bf16)

    for n in range(groups):
        at = slice(n * rows, (n + 1) * rows)
        u = mm(b_low[at, :], up_w[...]) + up_b[...]
        cdf = 0.5 + 0.5 * lax.erf(u * root_half)
        density = jnp.exp(-0.5 * (u * u)) * density_scale
        dw = mm_nt(d_low[at, :], down_w[...])
        w, du, gain_part, dw_wide = hidden_rows(
            u * cdf, cdf + u * density, dw, stats[at, :], gain[...], shift[...]
        )
        terms = [
            mm_tn(b_low[at, mine], du),
            mm_tn(d_low[at, mine], w),
            mm_tn(b_low[at, near], du),
            mm_tn(d_low[at, near], w),
            hidden_sums(du, gain_part, dw_wide),
        ]
        totals = terms if n == 0 else [t + s for t, s in zip(totals, terms)]
    if own:
        terms = [
            mm_tn(cols[0][...], du_own[...]),
            mm_tn(cols[2][...], w_own[...]),
            mm_tn(cols[1][...], du_own[...]),
            mm_tn(cols[3][...], w_own[...]),
            sum_own[...],
        ]
    else:
        low, high = ins[2][0:block, :], ins[2][block : 2 * block, :]
        terms = [ins[0][...], ins[1][...], low, high, ins[2][2 * block :, :]]
    totals = [t + s for t, s in zip(totals, terms)]
    up_out[...] = totals[0]
    down_out[...] = totals[1]
    near_out[0:block, :] = totals[2]
    near_out[block : 2 * block, :] = totals[3]
    near_out[2 * block :, :] = totals[4]


def norm2_kernel(meta, one, two, h1, dy, branch, vecs, gain, dh_out, sum_out):
    size, full = h1.shape
    db = one[...] + two[...]
    unit, inverse = unit_rows(h1[...])
    dh1 = dy[...] + unit_back(db, unit, inverse, gain[...])
    low = dh1.astype(bf16).astype(f32)
    dh_out[:, 0:full] = dh1
    lane = lax.broadcasted_iota(jnp.int32, (size, 128), 1)
    dh_out[:, full : full + 128] = jnp.where(
        lane == 0, row_sum(low * vecs[0:1]), row_sum(low * branch[...])
    )
    sums = jnp.concatenate(
        [
            jnp.sum(db * unit, axis=0, keepdims=True),
            jnp.sum(db, axis=0, keepdims=True),
            jnp.sum(dh1, axis=0, keepdims=True),
            jnp.sum(dy[...], axis=0, keepdims=True),
            jnp.zeros((4, full), f32),
        ],
        axis=0,
    )

    @pl.when(pl.program_id(0) == 0)
    def _():
        sum_out[...] = sums

    @pl.when(pl.program_id(0) > 0)
    def _():
        sum_out[...] += sums


def send_kernel(nb, meta, a_all, dh, *outs):
    send_pieces(meta, a_all, dh, outs, nb, a_all.shape[1] // nb)


def attend_back_kernel(attn_width, meta, dh_mine, dh_other, o_all, stats, sub_gain, out_w, q_all,
                       k_all, v_all, probs_all, table, dm_out, sum_out, dhl_out, do_all):
    rows, width = o_all.shape
    half = rows // 2
    full = out_w.shape[1]
    heads = width // HD
    step = pl.program_id(0)

    @pl.when(step == 0)
    def _():
        gain_row = spread(sub_gain, heads)
        dhl = jnp.concatenate(
            [dh_mine[:, 0:full].astype(bf16), dh_other[:, 0:full].astype(bf16)], axis=0
        )
        dhl_out[...] = dhl
        sums = jnp.concatenate([dh_mine[:, full:], dh_other[:, full:]], axis=0)
        dz = mm_nt(dhl, out_w[...])
        inverse = stats[:, 1:2]
        unit = (o_all[...] - stats[:, 0:1]) * inverse
        do = inverse * (
            dz * gain_row
            - sums[:, 0:1] * (1.0 / attn_width)
            - unit * (sums[:, 1:2] * (1.0 / attn_width))
        )
        do_all[...] = do.astype(bf16)
        sum_out[0:1, :] = jnp.sum(dz * unit, axis=0, keepdims=True)
        sum_out[1:2, :] = jnp.sum(dz, axis=0, keepdims=True)
        sum_out[5:8, :] = jnp.zeros((3, width), f32)

    quad = pl.ds(pl.multiple_of(step * QUAD, QUAD), QUAD)
    do = do_all[:, quad]
    q, k, v = q_all[...], k_all[...], v_all[...]
    lane = lax.broadcasted_iota(jnp.int32, (1, PAIR), 1)
    grads = [[], [], []]
    for p in range(2):
        here = slice(p * PAIR, (p + 1) * PAIR)
        total = [None] * 3
        for h in range(2):
            mask = (lane // HD) == h

            def only(value):
                return jnp.where(mask, value[:, here], jnp.zeros_like(value[:, here]))

            probs = probs_all[p * 2 + h]
            do_h = only(do)
            dprobs = mm_nt(do_h, v[:, here])
            inner = row_sum(probs * dprobs)
            dscores = (probs * (dprobs - inner)).astype(bf16)
            parts = (
                mm(dscores, only(k)),
                mm_tn(dscores, only(q)),
                mm_tn(probs.astype(bf16), do_h),
            )
            total = [part if t is None else t + part for t, part in zip(total, parts)]
        for j in range(3):
            grads[j].append(total[j])
    for j in range(3):
        grad = jnp.concatenate(grads[j], axis=1)
        if j == 0:
            grad = grad * (1.0 / math.sqrt(HD))
        if j < 2:
            flipped = half_swap(grad)
            parts = []
            for which in range(2):
                at = half_at(meta, which, half)
                here = slice(which * half, (which + 1) * half)
                c = jnp.concatenate([table[2 * j, at, :]] * 2, axis=1)
                s = jnp.concatenate([table[2 * j + 1, at, :]] * 2, axis=1)
                parts.append(grad[here] * c - flipped[here] * s)
            grad = jnp.concatenate(parts, axis=0)
        dm_out[:, pl.ds(pl.multiple_of(j * width + step * QUAD, QUAD), QUAD)] = grad
        sum_out[2 + j : 3 + j, quad] = jnp.sum(
            grad.astype(bf16).astype(f32), axis=0, keepdims=True
        )


def tail_kernel(meta, dm, weight, w, down_w, mine, other, low):
    half = mine.shape[0] // 2
    width = weight.shape[2]

    @pl.when(pl.program_id(0) == 0)
    def _():
        low[...] = dm[...].astype(bf16)

    total = mm_nt(low[:, 0:width], weight[0])
    for j in (1, 2):
        total = total + mm_nt(low[:, j * width : (j + 1) * width], weight[j])
    part = mm(w[...], down_w[...])
    mine[0:half, :] = total[0:half, :]
    mine[half:, :] = part[0:half, :]
    other[0:half, :] = total[half:, :]
    other[half:, :] = part[half:, :]


def norm1_kernel(meta, one, two, res_one, res_two, h1, tok, dh, gain, bias, sum_in, out, res_out,
                 sum_out):
    full = out.shape[1]
    da = one[...] + two[...]
    unit, inverse = unit_rows(tok[...].astype(f32))
    out[...] = dh[:, 0:full] + unit_back(da, unit, inverse, gain[...])
    res_out[...] = h1[...] + (res_one[...] + res_two[...]) + bias[...]
    sums = jnp.concatenate(
        [
            jnp.zeros((4, full), f32),
            jnp.sum(da * unit, axis=0, keepdims=True),
            jnp.sum(da, axis=0, keepdims=True),
            jnp.zeros((2, full), f32),
        ],
        axis=0,
    )

    @pl.when(pl.program_id(0) == 0)
    def _():
        sum_out[...] = sum_in[...] + sums

    @pl.when(pl.program_id(0) > 0)
    def _():
        sum_out[...] += sums


def place_kernel(meta, mine, other, out):
    tiles = pl.num_programs(0) // 2
    local = (pl.program_id(0) // tiles) == meta[0]
    out[...] = jnp.where(local, mine[...], other[...]).astype(bf16)


def add_kernel(count, meta, *refs):
    total = refs[0][...]
    for ref in refs[1:count]:
        total = total + ref[...]
    refs[count][...] = total


def square_kernel(nb, meta, a_all, dhl, *refs):
    pieces, sides, (own_out, mirror_out, a_low, d_low, right) = refs[:3], refs[3:11], refs[11:]
    rows, full = a_all.shape
    half, block = rows // 2, full // nb
    split = sides[0].shape[1]
    for part, at in ((0, meta[2]), (1, meta[2] ^ 4)):
        cols = pl.ds(pl.multiple_of(at * block, block), block)
        a_low[0:rows, part * block : (part + 1) * block] = a_all[:, cols]
        d_low[0:rows, part * block : (part + 1) * block] = dhl[:, cols]
    for s in range(4):
        at = rows * s
        if s > 0:
            for which in range(2):
                here = at + which * half
                rows_here = half_at(meta, which, half)
                a_low[here : here + half, :] = pieces[s - 1][rows_here, 0 : 2 * block].astype(bf16)
                d_low[here : here + half, :] = pieces[s - 1][rows_here, 2 * block :].astype(bf16)
        right[at : at + rows, 0:split] = sides[s][...].astype(bf16)
        right[at : at + rows, split:] = sides[4 + s][...].astype(bf16)
    for out, part in ((mirror_out, block), (own_out, 0)):
        out[:, 0:split] = mm_tn(a_low[:, part : part + block], right[:, 0:split])
        out[:, split:] = mm_tn(d_low[:, part : part + block], right[:, split:])


def final_square_kernel(meta, own, got, m_out, o_out):
    width = m_out.shape[2]
    for j in range(3):
        cols = slice(j * width, (j + 1) * width)
        m_out[j] = own[:, cols] + got[:, cols]
    o_out[...] = (own[:, 3 * width :] + got[:, 3 * width :]).T


def final_hidden_kernel(meta, up_own, up_got, down_own, down_got, up_out, down_out):
    up_out[...] = up_own[...] + up_got[...]
    down_out[...] = (down_own[...] + down_got[...]).T


def make_local(nb, nm):
    pair = [(i, i ^ 1) for i in range(nm)]
    cross = [(i, i ^ 2) for i in range(nm)]
    pairs = [[i, i + 1] for i in range(0, nm, 2)]
    full = nb == 8
    middle_link = [(2, 4), (3, 5), (4, 2), (5, 3)]
    outward_link = [(2, 0), (3, 1), (4, 6), (5, 7)]

    def to_core(value):
        return lax.ppermute(value, "mp", pair)

    def to_y(value):
        return lax.ppermute(value, "mp", cross)

    def to_batch(value, s):
        return lax.ppermute(value, "batch", [(i, i ^ s) for i in range(nb)])

    def to_middle(value):
        return lax.ppermute(value, "batch", middle_link)

    def outward(value):
        return lax.ppermute(value, "batch", outward_link)

    def local(
        tokens,
        lengths,
        cotangent,
        norm1_gain,
        norm1_shift,
        qkv_weight,
        qkv_bias,
        sub1_gain,
        sub1_shift,
        out_weight,
        out_bias,
        norm2_gain,
        norm2_shift,
        up_weight,
        up_bias,
        sub2_gain,
        sub2_shift,
        down_weight,
        down_bias,
    ):
        rows, D = tokens.shape
        half = rows // 2
        width = out_weight.shape[0]
        heads = width // HD
        hidden = up_weight.shape[1]
        attn_width = width * nm
        ff_width = hidden * nm
        block = D // nb
        span = 512
        chunks = hidden // span
        parts = D // span
        quads = heads // 4
        tiles = 4
        index = lax.axis_index("batch")
        meta = jnp.stack([lax.axis_index("mp") % 2, lengths[0], index]).astype(jnp.int32)
        always = lengths[0] >= 0
        table = jnp.asarray(turn_tables(rows))
        weight = jnp.transpose(qkv_weight, (1, 0, 2))

        def segment(stage):
            def skip():
                return jax.tree.map(
                    lambda s: jnp.zeros(s.shape, s.dtype), jax.eval_shape(stage)
                )

            return lax.cond(always, stage, skip)

        def meet(*values):
            return lax.optimization_barrier(values)

        def line(vec):
            return vec.reshape(1, -1)

        def rolled(step):
            return lambda i, *_: (0, i) if step == 1 else (i, 0)

        half_shape = shape_of((half, D))
        half_tile = pl.BlockSpec((half // tiles, D), rolled(0))
        tok_mine = pl.BlockSpec((half // tiles, D), lambda i, m: (m[0] * tiles + i, 0))
        tok_other = pl.BlockSpec((half // tiles, D), lambda i, m: ((1 - m[0]) * tiles + i, 0))
        ext_spec, ext_shape = whole((half + 8, D)), shape_of((half + 8, D))
        dh_spec, dh_shape = whole((half, D + 128)), shape_of((half, D + 128))
        dh_tile = pl.BlockSpec((half // tiles, D + 128), rolled(0))
        row_spec = whole((1, D))
        wide_spec, wide_shape = whole((rows, width)), shape_of((rows, width))
        quad = pl.BlockSpec((rows, QUAD), rolled(1))
        quad_weight = pl.BlockSpec((3, D, QUAD), lambda i, *_: (0, 0, i))
        probs_spec = pl.BlockSpec((4, rows, rows), lambda i, *_: (i, 0, 0))
        table_spec = whole((4, rows, PAIR))
        wide = pl.BlockSpec((1, span), rolled(1))
        tall = pl.BlockSpec((D, span), rolled(1))
        flat = pl.BlockSpec((span, D), rolled(0))
        half_part = pl.BlockSpec((half, span), rolled(1))
        many = pl.BlockSpec((rows, span), rolled(1))
        low_hidden = shape_of((rows, hidden), bf16)
        low_rows = shape_of((rows, D), bf16)
        tiny2, tiny4 = shape_of((rows, 2)), shape_of((rows, 4))
        tile = pl.BlockSpec((block, span), rolled(1))
        sum_tile = pl.BlockSpec((8, span), rolled(1))
        gain2, shift2, bias2 = line(sub2_gain), line(sub2_shift), line(up_bias)

        def add(order, *terms):
            shape = terms[0].shape
            tall_tile = pl.BlockSpec((shape[0] // tiles, shape[1]), rolled(0))
            return order.run(
                functools.partial(add_kernel, len(terms)),
                (tiles,),
                [tall_tile] * len(terms),
                tall_tile,
                shape_of(shape),
                terms,
            )

        def pair_join(value):
            return lax.all_gather(value, "mp", axis_index_groups=pairs, axis=0, tiled=True)

        dy, dy_other = Order(meta).run(
            mask_kernel, (tiles,), [tok_mine, tok_other], [half_tile] * 2, [half_shape] * 2,
            (cotangent, cotangent),
        )
        if full:
            dy_e1, dy_m1 = to_batch(dy, 2), to_middle(dy)

        def attention():
            order = Order(meta)
            low_shape = shape_of((rows, width), bf16)
            a, q, k, v, probs, o, y_mine, y_other = order.run(
                attend_kernel,
                (quads,),
                [whole((rows, D)), row_spec, row_spec, quad_weight, whole((3, heads, HD)),
                 whole((heads, HD)), whole((heads, HD)), whole((width, D)), table_spec],
                [whole((rows, D)), quad, quad, quad, probs_spec, wide_spec, ext_spec, ext_spec],
                [low_rows, low_shape, low_shape, low_shape,
                 shape_of((heads, rows, rows)), wide_shape, ext_shape, ext_shape],
                (tokens, line(norm1_gain), line(norm1_shift), weight, qkv_bias, sub1_gain,
                 sub1_shift, out_weight, table),
                [pltpu.VMEM((rows, D), bf16), pltpu.VMEM((rows, width), f32)],
            )
            y_pair = order.run(
                functools.partial(pair_kernel, width),
                (1,),
                [ext_spec] * 2,
                ext_spec,
                ext_shape,
                (y_mine, to_core(y_other)),
            )
            return a, q, k, v, probs, o, y_pair

        a, q, k, v, probs, o, y_pair = segment(attention)
        if full:
            dy_e1, dy_m1, y_pair = meet(dy_e1, dy_m1, y_pair)
            dy_f1, dy_m2 = outward(dy_m1), to_middle(dy_e1)

        def after_attention():
            order = Order(meta)
            y_cross = to_y(y_pair)
            dw, dyl = order.run(
                dw_kernel,
                (chunks,),
                [whole((half, D))] * 2 + [flat],
                [many, whole((rows, D))],
                [low_hidden, low_rows],
                (dy, dy_other, down_weight),
            )
            return dw, dyl, order.run(
                functools.partial(middle_kernel, attn_width),
                (tiles,),
                [half_tile, half_tile] + [pl.BlockSpec((8, D), lambda i, *_: (half // 8, 0))] * 2
                + [tok_mine] + [row_spec] * 3,
                [half_tile] * 3 + [whole((8, D)), whole((rows, 2))],
                [half_shape] * 3 + [shape_of((8, D)), tiny2],
                (y_pair, y_cross, y_pair, y_cross, tokens, line(out_bias), line(norm2_gain),
                 line(norm2_shift)),
            )

        dw, dyl, (h1, branch, b_mine, vecs, stats) = segment(after_attention)
        if full:
            dy_f1, dy_m2, b_mine = meet(dy_f1, dy_m2, b_mine)
            b_e1, b_m1 = to_batch(b_mine, 2), to_middle(b_mine)

        def hidden_first():
            order = Order(meta)
            dy_near = pair_join(dy_e1) if full else ()
            g, slope, stats_g, b = order.run(
                first_kernel,
                (chunks,),
                [whole((half, D))] * 2 + [tall, wide, wide, many],
                [many, many, whole((rows, 4)), whole((rows, D))],
                [low_hidden, low_hidden, tiny4, low_rows],
                (b_mine, to_core(b_mine), up_weight, bias2, gain2, dw),
                [pltpu.VMEM((rows, 1), f32)] * 4,
            )
            return g, slope, lax.all_gather(stats_g, "mp"), b, dy_near

        g, slope, g_stats, b, dy_near = segment(hidden_first)
        if full:
            b_e1, b_m1, g, dy_near = meet(b_e1, b_m1, g, dy_near)
            b_f1, b_m2 = outward(b_m1), to_middle(b_e1)

        def hidden_back():
            order = Order(meta)
            b_near = pair_join(b_e1) if full else ()
            w, du, st, h_sum, db_mine, db_other = order.run(
                functools.partial(back_kernel, ff_width, span),
                (parts,),
                [whole((rows, hidden))] * 3 + [whole((nm, rows, 4))]
                + [whole((1, hidden))] * 2 + [pl.BlockSpec((span, hidden), rolled(0))],
                [whole((rows, hidden))] * 2 + [whole((rows, 4)), whole((8, hidden))]
                + [half_part] * 2,
                [low_hidden, low_hidden, tiny4, shape_of((8, hidden)), half_shape, half_shape],
                (g, slope, dw, g_stats, gain2, shift2, up_weight),
            )
            return w, du, st, h_sum, add(order, db_mine, to_core(db_other)), b_near

        w, du, st, h_sum, db_pair, b_near = segment(hidden_back)
        if full:
            b_f1, b_m2, db_pair, b_near = meet(b_f1, b_m2, db_pair, b_near)
            st_near, st_far = to_batch(st, 2), (to_batch(st, 6), to_batch(st, 4))
            st_near, b_m2 = meet(st_near, b_m2)
            b_f2, dy_f2 = outward(b_m2), outward(dy_m2)

        def far_pass(order, b_src, d_src, starts, lower, stats_in, own, wait=()):
            size = len(starts) * rows
            cols = [
                pl.BlockSpec((rows, block), lambda i, m: (0, m[2])),
                pl.BlockSpec((rows, block), lambda i, m: (0, m[2] ^ 1)),
            ] * 2
            near_tile = pl.BlockSpec((2 * block + 8, span), rolled(1))
            fresh = own[0].dtype == bf16
            if fresh:
                w_own, du_own, sum_own, b_own, d_own = own
                tail = (w_own, du_own, sum_own, b_own, b_own, d_own, d_own)
                specs = [many, many, sum_tile] + cols
            else:
                tail, specs = tuple(own), [tile, tile, near_tile]
            count = 4 * len(starts)
            sources = (*b_src, *d_src)
            return order.run(
                functools.partial(far_kernel, starts, lower, fresh),
                (chunks,),
                [pl.BlockSpec(memory_space=pl.ANY)] * len(sources)
                + [whole((rows, 4))] * len(stats_in)
                + [tall, wide, wide, wide, flat]
                + specs,
                [tile, tile, near_tile],
                [shape_of((block, hidden))] * 2 + [shape_of((2 * block + 8, hidden))],
                (*sources, *stats_in, up_weight, bias2, gain2, shift2, down_weight, *tail),
                [pltpu.VMEM((size, D), bf16)] * 2
                + [pltpu.VMEM((size, 4), f32), pltpu.VMEM((count, half, D), f32),
                   pltpu.SemaphoreType.DMA((count,))],
                wait=wait,
                aliases={} if fresh else {
                    1 + len(sources) + len(stats_in) + 5 + i: i for i in range(3)},
            )

        def middle_norm_back():
            order = Order(meta)
            db_cross = to_y(db_pair)
            sums = ()
            if full:
                sums = far_pass(
                    order, [b_near], [dy_near], (((0, 0), (0, half)),), 0, (st_near, st_near),
                    (w, du, h_sum, b, dyl),
                )
            z = order.run(
                unit_kernel,
                (1,),
                [wide_spec, whole((rows, 2)), whole((heads, HD)), whole((heads, HD))],
                wide_spec,
                wide_shape,
                (o, stats, sub1_gain, sub1_shift),
            )
            dh_mine, d_sums = order.run(
                norm2_kernel,
                (tiles,),
                [half_tile] * 5 + [whole((8, D)), row_spec],
                [dh_tile, whole((8, D))],
                [dh_shape, shape_of((8, D))],
                (db_pair, db_cross, h1, dy, branch, vecs, line(norm2_gain)),
            )
            return dh_mine, d_sums, z, sums

        dh_mine, d_sums, z, sums = segment(middle_norm_back)
        if full:
            b_f2, dy_f2, st_far, dh_mine, z = meet(b_f2, dy_f2, st_far, dh_mine, z)
            z_x, z_z, z_d = to_batch(z, 1), to_batch(z, 2), to_batch(z, 3)

        def attention_back():
            order = Order(meta)
            dh_other = to_core(dh_mine)
            packed = ()
            if full:
                far = order.run(
                    pack_kernel,
                    (1,),
                    [pl.BlockSpec(memory_space=pl.ANY)] * 8,
                    pl.BlockSpec(memory_space=pl.ANY),
                    shape_of((2 * rows, D)),
                    (b_m1, b_f1, b_m2, b_f2, dy_m1, dy_f1, dy_m2, dy_f2),
                    [pltpu.VMEM((4, half, D), f32), pltpu.SemaphoreType.DMA((8,))],
                )
                packed = [far, to_core(far)]
            dm, h_sums, dhl = order.run(
                functools.partial(attend_back_kernel, attn_width),
                (quads,),
                [dh_spec, dh_spec, wide_spec, whole((rows, 2)), whole((heads, HD)),
                 whole((width, D)), quad, quad, quad, probs_spec, table_spec],
                [whole((rows, 3 * width)), whole((8, width)), whole((rows, D))],
                [shape_of((rows, 3 * width)), shape_of((8, width)), low_rows],
                (dh_mine, dh_other, o, stats, sub1_gain, out_weight, q, k, v, probs, table),
                [pltpu.VMEM((rows, width), bf16)],
            )
            sends = ()
            if full:
                sends = order.run(
                    functools.partial(send_kernel, nb),
                    (tiles,),
                    [half_tile, dh_tile],
                    [pl.BlockSpec((half // tiles, 4 * block), rolled(0))] * 3,
                    [shape_of((half, 4 * block))] * 3,
                    (a, dh_mine),
                )
            return packed, dm, h_sums, dhl, sends

        packed, dm, h_sums, dhl, sends = segment(attention_back)
        main = Order(meta)
        if full:
            z_x, z_z, z_d, dm, sends = meet(z_x, z_z, z_d, dm, sends)
            dm_x, dm_z = to_batch(dm, 1), to_batch(dm, 2)
            pieces = [to_batch(sends[s - 1], s) for s in (1, 2, 3)]
            sums = far_pass(
                main, packed, packed, (((0, 0), (1, 0)), ((0, half), (1, half))), rows,
                (st_far[0], st_far[1], st_far[1], st_far[0]), sums,
            )

        both = pl.BlockSpec((rows, span), rolled(1))
        tail_mine, tail_other = main.run(
            tail_kernel,
            (parts,),
            [whole((rows, 3 * width)), pl.BlockSpec((3, span, width), lambda i, *_: (0, i, 0)),
             whole((rows, hidden)), pl.BlockSpec((hidden, span), rolled(1))],
            [both] * 2,
            [shape_of((rows, D))] * 2,
            (dm, weight, w, down_weight),
            [pltpu.VMEM((rows, 3 * width), bf16)],
        )
        if full:
            dm_x, dm_z, pieces, sums, tail_other = meet(dm_x, dm_z, pieces, sums, tail_other)
            near_got, dm_d = to_batch(sums[2], 1), to_batch(dm_x, 2)

        def input_back():
            joined = [pair_join(piece) for piece in pieces] if full else ()
            return add(Order(meta), tail_mine, to_core(tail_other)), joined

        da_pair, pieces = segment(input_back)
        da_cross = to_y(da_pair)
        if full:
            da_pair, pieces = meet(da_pair, pieces)

            sides = [dm, dm_x, dm_z, dm_d, z, z_x, z_z, z_d]
            s_own, s_mirror = main.run(
                functools.partial(square_kernel, nb),
                (1,),
                [whole((rows, D))] * 2 + [whole((rows, 4 * block))] * 3
                + [whole((rows, 3 * width))] * 4 + [wide_spec] * 4,
                [whole((block, 4 * width))] * 2,
                [shape_of((block, 4 * width))] * 2,
                (a, dhl, *pieces, *sides),
                [pltpu.VMEM((4 * rows, 2 * block), bf16)] * 2
                + [pltpu.VMEM((4 * rows, 4 * width), bf16)],
            )
            s_got = to_batch(s_mirror, 4)

        main.last = [s_own] if full else []
        low_tile = pl.BlockSpec((half // tiles, D), lambda i, *_: (tiles + i, 0))
        t_mine, r_mine, d_sums = main.run(
            norm1_kernel,
            (tiles,),
            [half_tile, half_tile, low_tile, low_tile, half_tile, tok_mine, dh_tile, row_spec,
             row_spec, whole((8, D))],
            [half_tile, half_tile, whole((8, D))],
            [half_shape, half_shape, shape_of((8, D))],
            (da_pair, da_cross, da_pair, da_cross, h1, tokens, dh_mine, line(norm1_gain),
             line(down_bias), d_sums),
        )

        def place():
            order = Order(meta)
            sums = d_sums + to_core(d_sums)
            outs = [
                order.run(
                    place_kernel,
                    (2 * tiles,),
                    [pl.BlockSpec((half // tiles, D), lambda i, *_: (i % tiles, 0))] * 2,
                    pl.BlockSpec((half // tiles, D), rolled(0)),
                    low_rows,
                    (mine, to_core(mine)),
                )
                for mine in (r_mine, t_mine)
            ]
            return (*outs, sums)

        result, tokens_grad, d_sums = segment(place)

        def small_sums():
            comb = jnp.concatenate([d_sums, h_sums], axis=1)
            for s in (1, 2, 4):
                comb = comb + to_batch(comb, s)
            return comb

        lanes = hidden // 128
        per = 128 // nb
        if not full:

            def scatter(value, axis):
                return lax.psum_scatter(value, "batch", scatter_dimension=axis, tiled=True)

            d_sums = scatter(d_sums, 1)
            h_sums = lax.psum(h_sums, "batch")
            h_parts = scatter(h_sum[:3].reshape(3, lanes, 128), 2)
            dm_low = dm.astype(bf16)
            grad_qkv = scatter(
                jnp.stack([mm_tn(a, dm_low[:, j * width : (j + 1) * width]) for j in range(3)], 1), 0
            )
            grad_out = scatter(mm_tn(z.astype(bf16), dhl), 1)
            grad_up = scatter(mm_tn(b, du), 0)
            grad_down = scatter(mm_tn(w, dyl), 1)
        else:
            comb = segment(small_sums)
            d_sums = lax.dynamic_slice_in_dim(comb, index * block, block, 1)
            h_sums = comb[:, D:]
            h_parts = (sums[2][2 * block :] + near_got[2 * block :])[:3]
            h_parts = lax.dynamic_slice_in_dim(
                h_parts.reshape(3, lanes, 128), index * per, per, 2
            )
            main.last = [comb]
            cut = hidden // 4
            grad_up, grad_down = main.run(
                final_hidden_kernel,
                (4,),
                [pl.BlockSpec((block, cut), rolled(1))] * 3
                + [pl.BlockSpec((block, cut), lambda i, *_: (1, i))],
                [pl.BlockSpec((block, cut), rolled(1)), pl.BlockSpec((cut, block), rolled(0))],
                [shape_of((block, hidden)), shape_of((hidden, block))],
                (sums[0], near_got, sums[1], near_got),
            )
            grad_qkv, grad_out = main.run(
                final_square_kernel,
                (1,),
                [whole((block, 4 * width))] * 2,
                [whole((3, block, width)), whole((width, block))],
                [shape_of((3, block, width)), shape_of((width, block))],
                (s_own, s_got),
            )
            grad_qkv = jnp.transpose(grad_qkv, (1, 0, 2))
        per = HD // nb

        def own_part(value, shape):
            return lax.dynamic_slice_in_dim(value.reshape(shape), index * per, per, len(shape) - 1)

        return (
            result,
            tokens_grad,
            d_sums[4],
            d_sums[5],
            grad_qkv,
            own_part(h_sums[2:5], (3, heads, HD)),
            own_part(h_sums[0], (heads, HD)),
            own_part(h_sums[1], (heads, HD)),
            grad_out,
            d_sums[2],
            d_sums[0],
            d_sums[1],
            grad_up,
            h_parts[0],
            h_parts[1],
            h_parts[2],
            grad_down,
            d_sums[3],
        )

    return local


def solution(mesh):
    in_specs = (
        P("batch", None),
        P("batch"),
        P("batch", None),
        P(),
        P(),
        P(None, None, "mp"),
        P(None, "mp", None),
        P("mp", None),
        P("mp", None),
        P("mp", None),
        P(),
        P(),
        P(),
        P(None, "mp"),
        P("mp"),
        P("mp"),
        P("mp"),
        P("mp", None),
        P(),
    )
    out_specs = (
        P("batch", None),
        P("batch", None),
        P("batch"),
        P("batch"),
        P("batch", None, "mp"),
        P(None, "mp", "batch"),
        P("mp", "batch"),
        P("mp", "batch"),
        P("mp", "batch"),
        P("batch"),
        P("batch"),
        P("batch"),
        P("batch", "mp"),
        P("mp", "batch"),
        P("mp", "batch"),
        P("mp", "batch"),
        P("mp", "batch"),
        P("batch"),
    )
    local = make_local(mesh.shape["batch"], mesh.shape["mp"])
    return jax.shard_map(local, mesh=mesh, in_specs=in_specs, out_specs=out_specs, check_vma=False)
```

```python
import functools
import math

import jax
import jax.numpy as jnp
import numpy as np
from jax import lax
from jax.experimental import pallas as pl
from jax.experimental.pallas import tpu as pltpu
from jax.sharding import PartitionSpec as P

HD = 64
QUAD = 4 * HD
PAIR = 2 * HD

norm_eps = 1e-05
rope_base = 10000.0
xpos_base = 512.0
masked_score = -1e30
root_half = 2.0**-0.5
density_scale = 1.0 / math.sqrt(2.0 * math.pi)
f32 = jnp.float32
bf16 = jnp.bfloat16
MIB = 1 << 20


def dot(a, b, dims):
    return lax.dot_general(a, b, (dims, ((), ())), preferred_element_type=f32)


def mm(a, b):
    return dot(a, b, ((1,), (0,)))


def mm_nt(a, b):
    return dot(a, b, ((1,), (1,)))


def mm_tn(a, b):
    return dot(a, b, ((0,), (0,)))


def row_mean(value):
    return jnp.mean(value, axis=-1, keepdims=True)


def row_sum(value):
    return jnp.sum(value, axis=-1, keepdims=True)


def unit_rows(value):
    center = value - row_mean(value)
    inverse = lax.rsqrt(row_mean(center * center) + norm_eps)
    return center * inverse, inverse


def unit_back(grad, unit, inverse, gain):
    scaled = grad * gain
    return inverse * (scaled - row_mean(scaled) - unit * row_mean(scaled * unit))


def turn_tables(count):
    half = HD // 2
    places = np.arange(count, dtype=np.float64)[:, None]
    pair = np.arange(half, dtype=np.float64)[None, :]
    angles = places * rope_base ** (-2.0 * pair / HD)
    zeta = (2.0 * pair + 0.4 * HD) / (1.4 * HD)
    factor = zeta ** ((places - count // 2) / xpos_base)
    tables = []
    for scale in (factor, 1.0 / factor):
        tables.append(np.tile(np.cos(angles) * scale, (1, 4)))
        tables.append(np.tile(np.concatenate([-np.sin(angles), np.sin(angles)], 1), (1, 2))
                      * np.tile(scale, (1, 4)))
    return np.stack(tables).astype(np.float32)


def half_swap(value):
    lane = lax.broadcasted_iota(jnp.int32, value.shape, 1)
    return jnp.where(
        (lane & 32) == 0,
        pltpu.roll(value, value.shape[1] - 32, 1),
        pltpu.roll(value, 32, 1),
    )


def whole(shape):
    return pl.BlockSpec(shape, lambda *_: (0,) * len(shape))


def shape_of(shape, dtype=f32):
    return jax.ShapeDtypeStruct(shape, dtype)


def call(body, grid, ins, outs, shapes, scratch=(), tokens=0, aliases=None, cover=0):
    count = len(ins)

    def kernel(meta, *refs):
        body(meta, *refs[:count], *refs[count + tokens :])

    return pl.pallas_call(
        kernel,
        grid_spec=pltpu.PrefetchScalarGridSpec(
            num_scalar_prefetch=1,
            grid=grid,
            in_specs=list(ins) + [pl.BlockSpec(memory_space=pl.ANY)] * tokens,
            out_specs=outs,
            scratch_shapes=list(scratch),
        ),
        out_shape=shapes,
        compiler_params=pltpu.CompilerParams(
            dimension_semantics=("arbitrary",) * len(grid), vmem_limit_bytes=64 * MIB
        ),
        input_output_aliases=aliases or {},
        cost_estimate=pl.CostEstimate(flops=cover, bytes_accessed=0, transcendentals=0)
        if cover
        else None,
    )


class Order:
    def __init__(self, meta, cover=0):
        self.meta = meta
        self.last = []
        self.cover = cover

    def run(self, body, grid, ins, outs, shapes, args, scratch=(), wait=(), aliases=None):
        extra = list(wait) + self.last
        made = call(body, grid, ins, outs, shapes, scratch, len(extra), aliases, self.cover)(
            self.meta, *args, *extra
        )
        self.last = [made[0] if isinstance(made, (list, tuple)) else made]
        return made


def half_at(meta, which, half):
    return pl.ds(pl.multiple_of(((meta[0] + which) % 2) * half, half), half)


def spread(ref, count, first=0):
    return jnp.concatenate([ref[pl.ds(first + i, 1), :] for i in range(count)], axis=1)


def mask_kernel(meta, cot, mine):
    size = mine.shape[0]
    first = (meta[0] * pl.num_programs(0) + pl.program_id(0)) * size
    place = first + lax.broadcasted_iota(jnp.int32, (size, 1), 0)
    mine[...] = cot[...].astype(f32) * jnp.where(place < meta[1], 1.0, 0.0)


def send_pieces(meta, value, outs, block):
    for s, out in enumerate(outs):
        at = meta[2] ^ (s + 1)
        for part, where in ((0, at), (1, at ^ 4)):
            cols = pl.ds(pl.multiple_of(where * block, block), block)
            out[:, part * block : (part + 1) * block] = value[:, cols].astype(f32)


def flip_rows(value, half):
    return jnp.concatenate(
        [
            value[(i ^ 1) * half : ((i ^ 1) + 1) * half]
            for i in range(value.shape[0] // half)
        ],
        axis=0,
    )


def join_two(one, two, count):
    mean = 0.5 * (one[0] + two[0])
    gap = one[0] - two[0]
    joined = [mean, one[1] + two[1] + (0.5 * count) * gap * gap]
    if len(one) > 2:
        joined += [
            one[2] + two[2],
            one[3] + two[3] + one[2] * (one[0] - mean) + two[2] * (two[0] - mean),
        ]
    return joined


def join_all(ref, odd, count):
    cols = []
    for i in range(ref.shape[0]):
        value = ref[i]
        half = value.shape[0] // 2
        value = jnp.where(odd == i % 2, value, flip_rows(value, half))
        cols.append([value[:, c : c + 1] for c in range(4)])
    while len(cols) > 1:
        cols = [join_two(cols[i], cols[i + 1], count) for i in range(0, len(cols), 2)]
        count *= 2
    return cols[0]


def diagonal(count):
    return lax.broadcasted_iota(jnp.int32, (count, count), 0) == lax.broadcasted_iota(
        jnp.int32, (count, count), 1
    )


def as_row(column):
    return jnp.sum(jnp.where(diagonal(column.shape[0]), column, 0.0), axis=0, keepdims=True)


def as_column(row):
    return row_sum(jnp.where(diagonal(row.shape[1]), row, 0.0))


def attend_kernel(nb, meta, tok, gain, shift, weight, bias, sub_gain, sub_shift, out_w, table,
                  a_out, q_out, k_out, v_out, p_out, o_out, y_mine, y_other,
                  *rest):
    sends, (a_low, o_all) = rest[:-2], rest[-2:]
    rows, width = o_all.shape
    half = rows // 2
    step = pl.program_id(0)
    places = lax.broadcasted_iota(jnp.int32, (rows, 1), 0) ^ (meta[0] * half)
    keys = lax.broadcasted_iota(jnp.int32, (1, rows), 1) ^ (meta[0] * half)
    allowed = (keys <= places) & (keys < meta[1])

    @pl.when(step == 0)
    def _():
        for which in range(2):
            unit, _ = unit_rows(tok[half_at(meta, which, half), :].astype(f32))
            wide = unit * gain[...] + shift[...]
            a_low[which * half : (which + 1) * half, :] = wide.astype(bf16)
        a_out[...] = a_low[...]
        if sends:
            send_pieces(meta, a_low.at[0:half, :], sends, tok.shape[1] // nb)

    turned = []
    for j in range(3):
        m = mm(a_low[...], weight[j])
        m = m + jnp.concatenate(
            [bias[j, pl.ds(step * 4 + i, 1), :] for i in range(4)], axis=1
        )
        if j < 2:
            flipped = half_swap(m)
            parts = []
            for which in range(2):
                at = half_at(meta, which, half)
                here = slice(which * half, (which + 1) * half)
                c = jnp.concatenate([table[2 * j, at, :]] * 2, axis=1)
                s = jnp.concatenate([table[2 * j + 1, at, :]] * 2, axis=1)
                parts.append(m[here] * c + flipped[here] * s)
            m = jnp.concatenate(parts, axis=0)
        turned.append(m.astype(bf16))
    q, k, v = turned
    q = q * jnp.asarray(1.0 / math.sqrt(HD), bf16)
    q_out[...] = q
    k_out[...] = k
    v_out[...] = v
    lane = lax.broadcasted_iota(jnp.int32, (1, PAIR), 1)
    for p in range(2):
        here = slice(p * PAIR, (p + 1) * PAIR)
        total = None
        for h in range(2):
            mask = (lane // HD) == h
            scores = mm_nt(jnp.where(mask, q[:, here], jnp.zeros_like(q[:, here])), k[:, here])
            scores = jnp.where(allowed, scores, masked_score)
            weights = jnp.exp(scores - jnp.max(scores, axis=-1, keepdims=True))
            probs = weights / row_sum(weights)
            p_out[p * 2 + h] = probs
            part = mm(
                probs.astype(bf16), jnp.where(mask, v[:, here], jnp.zeros_like(v[:, here]))
            )
            total = part if total is None else total + part
        o_all[:, pl.ds(pl.multiple_of(step * QUAD + p * PAIR, PAIR), PAIR)] = total

    @pl.when(step == pl.num_programs(0) - 1)
    def _():
        o = o_all[...]
        o_out[...] = o
        mean = row_mean(o)
        center = o - mean
        stat_rows = jnp.concatenate([as_row(mean), as_row(row_sum(center * center))], axis=0)
        heads = width // HD
        gain_row, shift_row = spread(sub_gain, heads), spread(sub_shift, heads)
        pieces = []
        for row in (gain_row, shift_row):
            for _ in range(3):
                low = row.astype(bf16)
                pieces.append(low)
                row = row - low.astype(f32)
        vecs = mm(jnp.concatenate(pieces + [jnp.zeros((2, width), bf16)], axis=0), out_w[...])
        gain_out = vecs[0:1] + vecs[1:2] + vecs[2:3]
        shift_out = vecs[3:4] + vecs[4:5] + vecs[5:6]
        extra = jnp.concatenate([gain_out, shift_out, jnp.zeros((6, vecs.shape[1]), f32)], axis=0)
        low = (center * gain_row).astype(bf16)
        for which, out in ((1, y_other), (0, y_mine)):
            here = slice(which * half, (which + 1) * half)
            out[0:half, :] = mm(low[here], out_w[...]) + mean[here] * gain_out
            out[half : half + 8, :] = extra
            for p in range(2):
                out[half + 2 + 2 * p : half + 4 + 2 * p, 0:rows] = jnp.where(
                    meta[0] == p, stat_rows, jnp.zeros_like(stat_rows)
                )


def join_rows(refs, odd, count):
    cols = []
    for ref in refs:
        half = ref.shape[1] // 2
        for p in range(2):
            rows = ref[2 + 2 * p : 4 + 2 * p, :]
            swapped = jnp.concatenate([rows[:, half:], rows[:, :half]], axis=1)
            rows = jnp.where(odd == p, rows, swapped)
            cols.append([rows[0:1], rows[1:2]])
    near = join_two(cols[0], cols[1], count)
    far = join_two(cols[2], cols[3], count)
    return join_two(near, far, 2 * count)


def middle_kernel(attn_width, meta, one, two, one_extra, two_extra, tok, bias, gain, shift,
                   h_out, branch_out, b_out, vec_out, stats):
    size = h_out.shape[0]
    step = pl.program_id(0)

    @pl.when(step == 0)
    def _():
        rows = stats.shape[0]
        extras = (one_extra.at[:, 0:rows], two_extra.at[:, 0:rows])
        mean, m2 = join_rows(extras, meta[0], attn_width // 4)
        inverse = lax.rsqrt(m2 * (1.0 / attn_width) + norm_eps)
        stats[...] = jnp.concatenate([as_column(mean), as_column(inverse)], axis=1)
        vec_out[...] = one_extra[...] + two_extra[...]

    at = pl.ds(pl.multiple_of(step * size, size), size)
    branch = stats[at, 1:2] * ((one[...] + two[...]) - stats[at, 0:1] * vec_out[0:1, :])
    branch_out[...] = branch
    h1 = tok[...].astype(f32) + (branch + vec_out[1:2, :]) + bias[...]
    h_out[...] = h1
    unit, _ = unit_rows(h1)
    b_out[...] = unit * gain[...] + shift[...]


def dw_kernel(meta, cot, weight, out, low):
    half = cot.shape[0] // 2

    @pl.when(pl.program_id(0) == 0)
    def _():
        for which in range(2):
            first = ((meta[0] + which) % 2) * half
            place = first + lax.broadcasted_iota(jnp.int32, (half, 1), 0)
            rows = cot[half_at(meta, which, half), :]
            low[which * half : (which + 1) * half, :] = jnp.where(
                place < meta[1], rows, jnp.zeros_like(rows)
            )

    out[...] = mm_nt(low[...], weight[...]).astype(bf16)


def first_kernel(meta, mine, other, weight, bias, gain, dw, g_out, slope_out, stat_out, low,
                 mean_s, m2_s, s1_s, s2_s):
    half = mine.shape[0]
    step = pl.program_id(0)
    span = weight.shape[1]

    @pl.when(step == 0)
    def _():
        low[0:half, :] = mine[...].astype(bf16)
        low[half:, :] = other[...].astype(bf16)
        for ref in (mean_s, m2_s, s1_s, s2_s):
            ref[...] = jnp.zeros_like(ref)

    done = step.astype(f32)
    share = 1.0 / (done + 1.0)
    u = mm(low[...], weight[...]) + bias[...]
    cdf = 0.5 + 0.5 * lax.erf(u * root_half)
    density = jnp.exp(-0.5 * (u * u)) * density_scale
    g = u * cdf
    slope_out[...] = (cdf + u * density).astype(bf16)
    g_out[...] = g.astype(bf16)
    scaled = dw[...].astype(f32) * gain[...]
    mean_c = row_mean(g)
    center = g - mean_c
    s1_c = row_sum(scaled)
    s2_c = row_sum(scaled * center)
    gap = mean_c - mean_s[...]
    mean_new = mean_s[...] + gap * share
    m2_s[...] += row_sum(center * center) + gap * gap * (span * done * share)
    s2_s[...] += s2_c + s1_s[...] * (mean_s[...] - mean_new) + s1_c * (mean_c - mean_new)
    s1_s[...] += s1_c
    mean_s[...] = mean_new

    @pl.when(step == pl.num_programs(0) - 1)
    def _():
        stat_out[...] = jnp.concatenate([mean_s[...], m2_s[...], s1_s[...], s2_s[...]], axis=1)


def hidden_stats(ref, odd, out, count, ff_width):
    mean, m2, s1, s2 = join_all(ref, odd, count)
    inverse = lax.rsqrt(m2 * (1.0 / ff_width) + norm_eps)
    out[...] = jnp.concatenate(
        [mean, inverse, s1 * (1.0 / ff_width), inverse * s2 * (1.0 / ff_width)], axis=1
    )


def hidden_rows(g, slope, dw, stats, gain, shift):
    inverse = stats[:, 1:2]
    unit = (g.astype(f32) - stats[:, 0:1]) * inverse
    w = (unit * gain + shift).astype(bf16)
    dw = dw.astype(f32)
    dg = inverse * (dw * gain - stats[:, 2:3] - unit * stats[:, 3:4])
    return w, (dg * slope.astype(f32)).astype(bf16), dw * unit, dw


def back_kernel(ff_width, span, meta, g, slope, dw, parts, gain, shift, weight, w_out, du_out, stats,
                sum_out, db_mine, db_other):
    half = db_mine.shape[0]

    @pl.when(pl.program_id(0) == 0)
    def _():
        hidden_stats(parts, meta[0], stats, ff_width // parts.shape[0], ff_width)
        for c in range(g.shape[1] // span):
            at = slice(c * span, (c + 1) * span)
            w, du, gain_part, dw_wide = hidden_rows(
                g[:, at], slope[:, at], dw[:, at], stats[...], gain[:, at], shift[:, at]
            )
            w_out[:, at] = w
            du_out[:, at] = du
            sum_out[:, at] = hidden_sums(du, gain_part, dw_wide)

    part = mm_nt(du_out[...], weight[...])
    db_mine[...] = part[0:half, :]
    db_other[...] = part[half:, :]


def hidden_sums(du, gain_part, dw_wide):
    return jnp.concatenate(
        [
            jnp.sum(du.astype(f32), axis=0, keepdims=True),
            jnp.sum(gain_part, axis=0, keepdims=True),
            jnp.sum(dw_wide, axis=0, keepdims=True),
            jnp.zeros((5, du.shape[1]), f32),
        ],
        axis=0,
    )


def pack_kernel(meta, *refs):
    sources, (out, buffer, sems) = refs[:8], refs[8:]
    where = meta[2] // 2
    inner = (where == 1) | (where == 2)
    half = buffer.shape[1]

    def loads(first):
        return [
            pltpu.make_async_copy(sources[2 * i + first], buffer.at[i], sems.at[i])
            for i in range(4)
        ]

    @pl.when(inner)
    def _():
        for copy in loads(0):
            copy.start()

    @pl.when(jnp.logical_not(inner))
    def _():
        for copy in loads(1):
            copy.start()

    stores = []
    for i, copy in enumerate(loads(0)):
        copy.wait()
        store = pltpu.make_async_copy(
            buffer.at[i], out.at[i * half : (i + 1) * half, :], sems.at[4 + i]
        )
        store.start()
        stores.append(store)
    for store in stores:
        store.wait()


def far_kernel(starts, lower, own, meta, *refs):
    groups = len(starts)
    count = 1 + max(source for pair in starts for source, _ in pair)
    b_src, d_src, refs = refs[:count], refs[count : 2 * count], refs[2 * count :]
    stat_refs, rest = refs[: 2 * groups], refs[2 * groups :]
    up_w, up_b, gain, shift, down_w = rest[:5]
    rest = rest[5:]
    if own:
        w_own, du_own, sum_own, *cols = rest[:7]
        rest = rest[7:]
        ins = ()
    else:
        ins, rest = rest[:3], rest[3:]
    (up_out, down_out, near_out), (b_low, d_low, stats, buffer, sem) = rest[:3], rest[3:]
    half = buffer.shape[1]
    rows = 2 * half
    block = up_out.shape[0]
    where = meta[2] // 2
    inner = (where == 1) | (where == 2)
    mine = pl.ds(pl.multiple_of(meta[2] * block, block), block)
    near = pl.ds(pl.multiple_of((meta[2] ^ 1) * block, block), block)

    @pl.when(pl.program_id(0) == 0)
    def _():
        copies = []
        for n, pair in enumerate(starts):
            for k, (refs_k, low) in enumerate(((b_src, b_low), (d_src, d_low))):
                for i, (source, first) in enumerate(pair):
                    slot = 4 * n + 2 * k + i
                    copy = pltpu.make_async_copy(
                        refs_k[source].at[first + k * lower : first + k * lower + half, :], buffer.at[slot], sem.at[slot]
                    )
                    copy.start()
                    copies.append((copy, low, n * rows + i * half, slot))
        for n in range(groups):
            value = jnp.where(inner, stat_refs[2 * n][...], stat_refs[2 * n + 1][...])
            if lower == 0:
                value = jnp.where(meta[0] == 0, value, flip_rows(value, half))
            stats[n * rows : (n + 1) * rows, :] = value
        for copy, low, at, slot in copies:
            copy.wait()
            low[at : at + half, :] = buffer[slot].astype(bf16)

    for n in range(groups):
        at = slice(n * rows, (n + 1) * rows)
        u = mm(b_low[at, :], up_w[...]) + up_b[...]
        cdf = 0.5 + 0.5 * lax.erf(u * root_half)
        density = jnp.exp(-0.5 * (u * u)) * density_scale
        dw = mm_nt(d_low[at, :], down_w[...])
        w, du, gain_part, dw_wide = hidden_rows(
            u * cdf, cdf + u * density, dw, stats[at, :], gain[...], shift[...]
        )
        terms = [
            mm_tn(b_low[at, mine], du),
            mm_tn(d_low[at, mine], w),
            mm_tn(b_low[at, near], du),
            mm_tn(d_low[at, near], w),
            hidden_sums(du, gain_part, dw_wide),
        ]
        totals = terms if n == 0 else [t + s for t, s in zip(totals, terms)]
    if own:
        terms = [
            mm_tn(cols[0][...], du_own[...]),
            mm_tn(cols[2][...], w_own[...]),
            mm_tn(cols[1][...], du_own[...]),
            mm_tn(cols[3][...], w_own[...]),
            sum_own[...],
        ]
    else:
        low, high = ins[2][0:block, :], ins[2][block : 2 * block, :]
        terms = [ins[0][...], ins[1][...], low, high, ins[2][2 * block :, :]]
    totals = [t + s for t, s in zip(totals, terms)]
    up_out[...] = totals[0]
    down_out[...] = totals[1]
    near_out[0:block, :] = totals[2]
    near_out[block : 2 * block, :] = totals[3]
    near_out[2 * block :, :] = totals[4]


def norm2_kernel(nb, meta, one, two, h1, dy, branch, vecs, gain, dh_out, sum_out, *sends):
    size, full = h1.shape
    db = one[...] + two[...]
    unit, inverse = unit_rows(h1[...])
    dh1 = dy[...] + unit_back(db, unit, inverse, gain[...])
    low = dh1.astype(bf16).astype(f32)
    dh_out[:, 0:full] = dh1
    lane = lax.broadcasted_iota(jnp.int32, (size, 128), 1)
    dh_out[:, full : full + 128] = jnp.where(
        lane == 0, row_sum(low * vecs[0:1]), row_sum(low * branch[...])
    )
    sums = jnp.concatenate(
        [
            jnp.sum(db * unit, axis=0, keepdims=True),
            jnp.sum(db, axis=0, keepdims=True),
            jnp.sum(dh1, axis=0, keepdims=True),
            jnp.sum(dy[...], axis=0, keepdims=True),
            jnp.zeros((4, full), f32),
        ],
        axis=0,
    )

    @pl.when(pl.program_id(0) == 0)
    def _():
        sum_out[...] = sums

    @pl.when(pl.program_id(0) > 0)
    def _():
        sum_out[...] += sums
    if sends:
        send_pieces(meta, dh_out, sends, full // nb)


def attend_back_kernel(attn_width, meta, dh_mine, dh_other, o_all, stats, sub_gain, sub_shift, out_w, q_all,
                       k_all, v_all, probs_all, table, dm_out, dv_out, sum_out, dhl_out, do_all):
    rows, width = o_all.shape
    half = rows // 2
    full = out_w.shape[1]
    heads = width // HD
    step = pl.program_id(0)

    @pl.when(step == 0)
    def _():
        gain_row = spread(sub_gain, heads)
        dhl = jnp.concatenate(
            [dh_mine[:, 0:full].astype(bf16), dh_other[:, 0:full].astype(bf16)], axis=0
        )
        dhl_out[...] = dhl
        sums = jnp.concatenate([dh_mine[:, full:], dh_other[:, full:]], axis=0)
        dz = mm_nt(dhl, out_w[...])
        inverse = stats[:, 1:2]
        unit = (o_all[...] - stats[:, 0:1]) * inverse
        do = inverse * (
            dz * gain_row
            - sums[:, 0:1] * (1.0 / attn_width)
            - unit * (sums[:, 1:2] * (1.0 / attn_width))
        )
        do_all[...] = do.astype(bf16)
        dv_out[:, width:] = unit * gain_row + spread(sub_shift, heads)
        sum_out[0:1, :] = jnp.sum(dz * unit, axis=0, keepdims=True)
        sum_out[1:2, :] = jnp.sum(dz, axis=0, keepdims=True)
        sum_out[5:8, :] = jnp.zeros((3, width), f32)

    quad = pl.ds(pl.multiple_of(step * QUAD, QUAD), QUAD)
    do = do_all[:, quad]
    q, k, v = q_all[...], k_all[...], v_all[...]
    lane = lax.broadcasted_iota(jnp.int32, (1, PAIR), 1)
    grads = [[], [], []]
    for p in range(2):
        here = slice(p * PAIR, (p + 1) * PAIR)
        total = [None] * 3
        for h in range(2):
            mask = (lane // HD) == h

            def only(value):
                return jnp.where(mask, value[:, here], jnp.zeros_like(value[:, here]))

            probs = probs_all[p * 2 + h]
            do_h = only(do)
            dprobs = mm_nt(do_h, v[:, here])
            inner = row_sum(probs * dprobs)
            dscores = (probs * (dprobs - inner)).astype(bf16)
            parts = (
                mm(dscores, only(k)),
                mm_tn(dscores, only(q)),
                mm_tn(probs.astype(bf16), do_h),
            )
            total = [part if t is None else t + part for t, part in zip(total, parts)]
        for j in range(3):
            grads[j].append(total[j])
    for j in range(3):
        grad = jnp.concatenate(grads[j], axis=1)
        if j == 0:
            grad = grad * (1.0 / math.sqrt(HD))
        if j < 2:
            flipped = half_swap(grad)
            parts = []
            for which in range(2):
                at = half_at(meta, which, half)
                here = slice(which * half, (which + 1) * half)
                c = jnp.concatenate([table[2 * j, at, :]] * 2, axis=1)
                s = jnp.concatenate([table[2 * j + 1, at, :]] * 2, axis=1)
                parts.append(grad[here] * c - flipped[here] * s)
            grad = jnp.concatenate(parts, axis=0)
        if j < 2:
            dm_out[:, pl.ds(pl.multiple_of(j * width + step * QUAD, QUAD), QUAD)] = grad
        else:
            dv_out[:, quad] = grad
        sum_out[2 + j : 3 + j, quad] = jnp.sum(
            grad.astype(bf16).astype(f32), axis=0, keepdims=True
        )


def tail_kernel(meta, dm, dv, weight, w, down_w, mine, other, low):
    half = mine.shape[0] // 2
    width = weight.shape[2]

    @pl.when(pl.program_id(0) == 0)
    def _():
        low[:, 0 : 2 * width] = dm[...].astype(bf16)
        low[:, 2 * width :] = dv[...].astype(bf16)

    total = mm_nt(low[:, 0:width], weight[0])
    for j in (1, 2):
        total = total + mm_nt(low[:, j * width : (j + 1) * width], weight[j])
    part = mm(w[...], down_w[...])
    mine[0:half, :] = total[0:half, :]
    mine[half:, :] = part[0:half, :]
    other[0:half, :] = total[half:, :]
    other[half:, :] = part[half:, :]


def norm1_kernel(meta, one, two, h1, tok, dh, gain, bias, sum_in, out, sum_out):
    full = out.shape[1]
    step = pl.program_id(0)
    total = one[...] + two[...]

    @pl.when(step == 0)
    def _():
        sum_out[...] = sum_in[...]

    @pl.when(step < pl.num_programs(0) // 2)
    def _():
        unit, inverse = unit_rows(tok[...].astype(f32))
        out[...] = dh[:, 0:full] + unit_back(total, unit, inverse, gain[...])
        sum_out[4:5, :] += jnp.sum(total * unit, axis=0, keepdims=True)
        sum_out[5:6, :] += jnp.sum(total, axis=0, keepdims=True)

    @pl.when(step >= pl.num_programs(0) // 2)
    def _():
        out[...] = h1[...] + total + bias[...]


def place_kernel(meta, mine, other, out):
    tiles = pl.num_programs(0) // 2
    local = (pl.program_id(0) // tiles) == meta[0]
    out[...] = jnp.where(local, mine[...], other[...]).astype(bf16)


def add_kernel(count, meta, *refs):
    total = refs[0][...]
    for ref in refs[1:count]:
        total = total + ref[...]
    refs[count][...] = total


def join_kernel(meta, *refs):
    pieces, (out, buffer, sems) = refs[:3], refs[3:]
    half = buffer.shape[1]
    loads = [pltpu.make_async_copy(pieces[i], buffer.at[i], sems.at[i]) for i in range(3)]
    for copy in loads:
        copy.start()
    stores = []
    for i, copy in enumerate(loads):
        copy.wait()
        store = pltpu.make_async_copy(
            buffer.at[i], out.at[i * half : (i + 1) * half, :], sems.at[3 + i]
        )
        store.start()
        stores.append(store)
    for store in stores:
        store.wait()


def square_kernel(nb, part, meta, *refs):
    lists, rest = refs[: 7 * (part + 1)], refs[7 * (part + 1) :]
    sides, (own_out, mirror_out), lows = rest[:4], rest[4:6], rest[6:]
    right = lows[-1]
    rows, full = lists[0].shape
    half, block = rows // 2, full // nb
    width = own_out.shape[1] // 2
    for n, low in enumerate(lows[:-1]):
        own, mine, other = lists[7 * n], lists[7 * n + 1 : 7 * n + 4], lists[7 * n + 4 : 7 * n + 7]
        for which, at in ((0, meta[2]), (1, meta[2] ^ 4)):
            cols = pl.ds(pl.multiple_of(at * block, block), block)
            low[0:rows, which * block : (which + 1) * block] = own[:, cols]
        for s in range(3):
            here = rows * (s + 1)
            low[here : here + half, :] = mine[s][...].astype(bf16)
            low[here + half : here + rows, :] = other[s][...].astype(bf16)
    for s in range(4):
        right[rows * s : rows * (s + 1), :] = sides[s][...].astype(bf16)
    for out, first in ((mirror_out, block), (own_out, 0)):
        left = lows[0][:, first : first + block]
        if part == 0:
            out[...] = mm_tn(left, right[...])
        else:
            out[:, 0:width] = mm_tn(left, right[:, 0:width])
            out[:, width:] = mm_tn(lows[1][:, first : first + block], right[:, width:])


def final_square_kernel(meta, one_own, one_got, two_own, two_got, m_out, o_out):
    width = m_out.shape[2]
    for j in range(2):
        cols = slice(j * width, (j + 1) * width)
        m_out[j] = one_own[:, cols] + one_got[:, cols]
    m_out[2] = two_own[:, 0:width] + two_got[:, 0:width]
    o_out[...] = (two_own[:, width:] + two_got[:, width:]).T


def final_hidden_kernel(meta, up_own, up_got, down_own, down_got, up_out, down_out):
    up_out[...] = up_own[...] + up_got[...]
    down_out[...] = (down_own[...] + down_got[...]).T


def make_local(nb, nm):
    pair = [(i, i ^ 1) for i in range(nm)]
    cross = [(i, i ^ 2) for i in range(nm)]
    pairs = [[i, i + 1] for i in range(0, nm, 2)]
    full = nb == 8
    middle_link = [(2, 4), (3, 5), (4, 2), (5, 3)]
    outward_link = [(2, 0), (3, 1), (4, 6), (5, 7)]

    def to_core(value):
        return lax.ppermute(value, "mp", pair)

    def to_y(value):
        return lax.ppermute(value, "mp", cross)

    def to_batch(value, s):
        return lax.ppermute(value, "batch", [(i, i ^ s) for i in range(nb)])

    def to_middle(value):
        return lax.ppermute(value, "batch", middle_link)

    def outward(value):
        return lax.ppermute(value, "batch", outward_link)

    def local(
        tokens,
        lengths,
        cotangent,
        norm1_gain,
        norm1_shift,
        qkv_weight,
        qkv_bias,
        sub1_gain,
        sub1_shift,
        out_weight,
        out_bias,
        norm2_gain,
        norm2_shift,
        up_weight,
        up_bias,
        sub2_gain,
        sub2_shift,
        down_weight,
        down_bias,
    ):
        rows, D = tokens.shape
        half = rows // 2
        width = out_weight.shape[0]
        heads = width // HD
        hidden = up_weight.shape[1]
        attn_width = width * nm
        ff_width = hidden * nm
        block = D // nb
        span = 512
        chunks = hidden // span
        parts = D // span
        quads = heads // 4
        sends = 3 if full else 0
        tiles = 4
        index = lax.axis_index("batch")
        meta = jnp.stack([lax.axis_index("mp") % 2, lengths[0], index]).astype(jnp.int32)
        always = lengths[0] >= 0
        table = jnp.asarray(turn_tables(rows))
        weight = jnp.transpose(qkv_weight, (1, 0, 2))

        def segment(stage):
            def skip():
                return jax.tree.map(
                    lambda s: jnp.zeros(s.shape, s.dtype), jax.eval_shape(stage)
                )

            return lax.cond(always, stage, skip)

        def meet(*values):
            return lax.optimization_barrier(values)

        def line(vec):
            return vec.reshape(1, -1)

        def rolled(step):
            return lambda i, *_: (0, i) if step == 1 else (i, 0)

        half_shape = shape_of((half, D))
        half_tile = pl.BlockSpec((half // tiles, D), rolled(0))
        tok_mine = pl.BlockSpec((half // tiles, D), lambda i, m: (m[0] * tiles + i, 0))
        ext_spec, ext_shape = whole((half + 8, D)), shape_of((half + 8, D))
        dh_spec, dh_shape = whole((half, D + 128)), shape_of((half, D + 128))
        dh_tile = pl.BlockSpec((half // tiles, D + 128), rolled(0))
        row_spec = whole((1, D))
        wide_spec, wide_shape = whole((rows, width)), shape_of((rows, width))
        quad = pl.BlockSpec((rows, QUAD), rolled(1))
        quad_weight = pl.BlockSpec((3, D, QUAD), lambda i, *_: (0, 0, i))
        probs_spec = pl.BlockSpec((4, rows, rows), lambda i, *_: (i, 0, 0))
        table_spec = whole((4, rows, PAIR))
        wide = pl.BlockSpec((1, span), rolled(1))
        tall = pl.BlockSpec((D, span), rolled(1))
        flat = pl.BlockSpec((span, D), rolled(0))
        half_part = pl.BlockSpec((half, span), rolled(1))
        many = pl.BlockSpec((rows, span), rolled(1))
        low_hidden = shape_of((rows, hidden), bf16)
        low_rows = shape_of((rows, D), bf16)
        tiny2, tiny4 = shape_of((rows, 2)), shape_of((rows, 4))
        tile = pl.BlockSpec((block, span), rolled(1))
        sum_tile = pl.BlockSpec((8, span), rolled(1))
        gain2, shift2, bias2 = line(sub2_gain), line(sub2_shift), line(up_bias)

        def pair_join(value):
            return lax.all_gather(value, "mp", axis_index_groups=pairs, axis=0, tiled=True)

        dy = Order(meta).run(
            mask_kernel, (tiles,), [tok_mine], half_tile, half_shape, (cotangent,)
        )
        if full:
            dy_e1, dy_m1 = to_batch(dy, 2), to_middle(dy)

        def attention():
            order = Order(meta)
            low_shape = shape_of((rows, width), bf16)
            a, q, k, v, probs, o, y_mine, y_other, *a_sent = order.run(
                functools.partial(attend_kernel, nb),
                (quads,),
                [whole((rows, D)), row_spec, row_spec, quad_weight, whole((3, heads, HD)),
                 whole((heads, HD)), whole((heads, HD)), whole((width, D)), table_spec],
                    [whole((rows, D)), quad, quad, quad, probs_spec, wide_spec, ext_spec, ext_spec]
                + [whole((half, 2 * block))] * sends,
                [low_rows, low_shape, low_shape, low_shape,
                 shape_of((heads, rows, rows)), wide_shape, ext_shape, ext_shape]
                + [shape_of((half, 2 * block))] * sends,
                (tokens, line(norm1_gain), line(norm1_shift), weight, qkv_bias, sub1_gain,
                 sub1_shift, out_weight, table),
                [pltpu.VMEM((rows, D), bf16), pltpu.VMEM((rows, width), f32)],
            )
            y_pair = y_mine + to_core(y_other)
            return a, q, k, v, probs, o, y_pair, a_sent

        a, q, k, v, probs, o, y_pair, a_sent = segment(attention)
        if full:
            dy_e1, dy_m1, y_pair, a_sent = meet(dy_e1, dy_m1, y_pair, a_sent)
            a_got = [None, to_batch(a_sent[1], 2), to_batch(a_sent[2], 3)]
            dy_f1, dy_m2 = outward(dy_m1), to_middle(dy_e1)

        def after_attention():
            order = Order(meta)
            y_cross = to_y(y_pair)
            dw, dyl = order.run(
                dw_kernel,
                (chunks,),
                [whole((rows, D)), flat],
                [many, whole((rows, D))],
                [low_hidden, low_rows],
                (cotangent, down_weight),
            )
            return dw, dyl, order.run(
                functools.partial(middle_kernel, attn_width),
                (tiles,),
                [half_tile, half_tile] + [pl.BlockSpec((8, D), lambda i, *_: (half // 8, 0))] * 2
                + [tok_mine] + [row_spec] * 3,
                [half_tile] * 3 + [whole((8, D)), whole((rows, 2))],
                [half_shape] * 3 + [shape_of((8, D)), tiny2],
                (y_pair, y_cross, y_pair, y_cross, tokens, line(out_bias), line(norm2_gain),
                 line(norm2_shift)),
            )

        dw, dyl, (h1, branch, b_mine, vecs, stats) = segment(after_attention)
        if full:
            dy_f1, dy_m2, b_mine, a_sent, a_got[1], a_got[2] = meet(
                dy_f1, dy_m2, b_mine, a_sent, a_got[1], a_got[2]
            )
            a_got[0] = to_batch(a_sent[0], 1)
            b_e1, b_m1 = to_batch(b_mine, 2), to_middle(b_mine)

        def hidden_first():
            order = Order(meta)
            dy_near = pair_join(dy_e1) if full else ()
            g, slope, stats_g, b = order.run(
                first_kernel,
                (chunks,),
                [whole((half, D))] * 2 + [tall, wide, wide, many],
                [many, many, whole((rows, 4)), whole((rows, D))],
                [low_hidden, low_hidden, tiny4, low_rows],
                (b_mine, to_core(b_mine), up_weight, bias2, gain2, dw),
                [pltpu.VMEM((rows, 1), f32)] * 4,
            )
            return g, slope, lax.all_gather(stats_g, "mp"), b, dy_near

        g, slope, g_stats, b, dy_near = segment(hidden_first)
        if full:
            b_e1, b_m1, a_got, g, dy_near = meet(b_e1, b_m1, a_got, g, dy_near)
            b_f1, b_m2 = outward(b_m1), to_middle(b_e1)

        def hidden_back():
            order = Order(meta)
            b_near = pair_join(b_e1) if full else ()
            a_core = [to_core(piece) for piece in a_got[1:]] if full else ()
            w, du, st, h_sum, db_mine, db_other = order.run(
                functools.partial(back_kernel, ff_width, span),
                (parts,),
                [whole((rows, hidden))] * 3 + [whole((nm, rows, 4))]
                + [whole((1, hidden))] * 2 + [pl.BlockSpec((span, hidden), rolled(0))],
                [whole((rows, hidden))] * 2 + [whole((rows, 4)), whole((8, hidden))]
                + [half_part] * 2,
                [low_hidden, low_hidden, tiny4, shape_of((8, hidden)), half_shape, half_shape],
                (g, slope, dw, g_stats, gain2, shift2, up_weight),
            )
            return w, du, st, h_sum, db_mine + to_core(db_other), b_near, a_core

        w, du, st, h_sum, db_pair, b_near, a_core = segment(hidden_back)
        if full:
            b_f1, b_m2, db_pair, b_near = meet(b_f1, b_m2, db_pair, b_near)
            st_near, st_far = to_batch(st, 2), (to_batch(st, 6), to_batch(st, 4))
            st_near, dy_m2 = meet(st_near, dy_m2)
            dy_f2, b_f2 = outward(dy_m2), outward(b_m2)

        def far_pass(order, b_src, d_src, starts, lower, stats_in, own, wait=()):
            size = len(starts) * rows
            cols = [
                pl.BlockSpec((rows, block), lambda i, m: (0, m[2])),
                pl.BlockSpec((rows, block), lambda i, m: (0, m[2] ^ 1)),
            ] * 2
            near_tile = pl.BlockSpec((2 * block + 8, span), rolled(1))
            fresh = own[0].dtype == bf16
            if fresh:
                w_own, du_own, sum_own, b_own, d_own = own
                tail = (w_own, du_own, sum_own, b_own, b_own, d_own, d_own)
                specs = [many, many, sum_tile] + cols
            else:
                tail, specs = tuple(own), [tile, tile, near_tile]
            count = 4 * len(starts)
            sources = (*b_src, *d_src)
            return order.run(
                functools.partial(far_kernel, starts, lower, fresh),
                (chunks,),
                [pl.BlockSpec(memory_space=pl.ANY)] * len(sources)
                + [whole((rows, 4))] * len(stats_in)
                + [tall, wide, wide, wide, flat]
                + specs,
                [tile, tile, near_tile],
                [shape_of((block, hidden))] * 2 + [shape_of((2 * block + 8, hidden))],
                (*sources, *stats_in, up_weight, bias2, gain2, shift2, down_weight, *tail),
                [pltpu.VMEM((size, D), bf16)] * 2
                + [pltpu.VMEM((size, 4), f32), pltpu.VMEM((count, half, D), f32),
                   pltpu.SemaphoreType.DMA((count,))],
                wait=wait,
                aliases={} if fresh else {
                    1 + len(sources) + len(stats_in) + 5 + i: i for i in range(3)},
            )

        def middle_norm_back():
            order = Order(meta)
            db_cross = to_y(db_pair)
            sums = ()
            if full:
                sums = far_pass(
                    order, [b_near], [dy_near], (((0, 0), (0, half)),), 0, (st_near, st_near),
                    (w, du, h_sum, b, dyl),
                )
            outs = order.run(
                functools.partial(norm2_kernel, nb),
                (tiles,),
                [half_tile] * 5 + [whole((8, D)), row_spec],
                [dh_tile, whole((8, D))]
                + [pl.BlockSpec((half // tiles, 2 * block), rolled(0))] * sends,
                [dh_shape, shape_of((8, D))] + [shape_of((half, 2 * block))] * sends,
                (db_pair, db_cross, h1, dy, branch, vecs, line(norm2_gain)),
            )
            return outs, sums

        (dh_mine, d_sums, *dh_sent), sums = segment(middle_norm_back)
        if full:
            st_far, dy_f2, dh_mine, dh_sent = meet(st_far, dy_f2, dh_mine, dh_sent)
            dh_got = [to_batch(dh_sent[0], 1), None, None]

        def attention_back():
            order = Order(meta)
            dh_other = to_core(dh_mine)
            a_first = to_core(a_got[0]) if full else ()
            dm, dv, h_sums, dhl = order.run(
                functools.partial(attend_back_kernel, attn_width),
                (quads,),
                [dh_spec, dh_spec, wide_spec, whole((rows, 2)), whole((heads, HD)),
                 whole((heads, HD)), whole((width, D)), quad, quad, quad, probs_spec, table_spec],
                [whole((rows, 2 * width))] * 2 + [whole((8, width)), whole((rows, D))],
                [shape_of((rows, 2 * width))] * 2 + [shape_of((8, width)), low_rows],
                (dh_mine, dh_other, o, stats, sub1_gain, sub1_shift, out_weight, q, k, v, probs,
                 table),
                [pltpu.VMEM((rows, width), bf16)],
            )
            return dm, dv, h_sums, dhl, a_first

        dm, dv, h_sums, dhl, a_first = segment(attention_back)
        main = Order(meta, 10**11)
        if full:
            b_f2, dh_got[0], dm, dv, dh_sent = meet(b_f2, dh_got[0], dm, dv, dh_sent)
            dm_x, dm_z = to_batch(dm, 1), to_batch(dm, 2)
            dh_got[1] = to_batch(dh_sent[1], 2)

        both = pl.BlockSpec((rows, span), rolled(1))

        def prepare():
            order = Order(meta)
            packed = ()
            if full:
                far = order.run(
                    pack_kernel,
                    (1,),
                    [pl.BlockSpec(memory_space=pl.ANY)] * 8,
                    pl.BlockSpec(memory_space=pl.ANY),
                    shape_of((2 * rows, D)),
                    (b_m1, b_f1, b_m2, b_f2, dy_m1, dy_f1, dy_m2, dy_f2),
                    [pltpu.VMEM((4, half, D), f32), pltpu.SemaphoreType.DMA((8,))],
                )
                packed = [far, to_core(far)]
            tail_mine, tail_other = order.run(
                tail_kernel,
                (parts,),
                [whole((rows, 2 * width)), pl.BlockSpec((rows, width), lambda i, *_: (0, 0)),
                 pl.BlockSpec((3, span, width), lambda i, *_: (0, i, 0)),
                 whole((rows, hidden)), pl.BlockSpec((hidden, span), rolled(1))],
                [both] * 2,
                [shape_of((rows, D))] * 2,
                (dm, dv, weight, w, down_weight),
                [pltpu.VMEM((rows, 3 * width), bf16)],
            )
            return packed, tail_mine + to_core(tail_other)

        packed, da_pair = segment(prepare)
        if full:
            dm_x, dm_z, dh_got[1], packed, dv, dh_sent, da_pair = meet(
                dm_x, dm_z, dh_got[1], packed, dv, dh_sent, da_pair
            )
            dv_x = to_batch(dv, 1)
            dm_d = to_batch(dm_x, 2)
            dh_got[2] = to_batch(dh_sent[2], 3)
            da_cross = to_y(da_pair)
            sums = far_pass(
                main, packed, packed, (((0, 0), (1, 0)), ((0, half), (1, half))), rows,
                (st_far[0], st_far[1], st_far[1], st_far[0]), sums,
            )

        if full:
            dv_x, dm_d, dh_got[2], sums, dm, dv = meet(dv_x, dm_d, dh_got[2], sums, dm, dv)
            near_got, dv_z, dv_d = to_batch(sums[2], 1), to_batch(dv, 2), to_batch(dv_x, 2)
            cut = 2 * width
            a_join = [*a_got, a_first, *a_core]

            def square(part, lefts, sides):
                def piece(array, s):
                    at = s if array.shape[0] > half else 0
                    return pl.BlockSpec((half, 2 * block), lambda i, *_: (at, 0))

                specs = []
                for _, got in lefts:
                    specs += [whole((rows, D))] + [piece(got[i], i % 3) for i in range(6)]
                lists = [array for own, got in lefts for array in (own, *got)]
                return main.run(
                    functools.partial(square_kernel, nb, part),
                    (1,),
                    specs + [whole((rows, cut))] * 4,
                    [whole((block, cut))] * 2,
                    [shape_of((block, cut))] * 2,
                    (*lists, *sides),
                    [pltpu.VMEM((4 * rows, 2 * block), bf16)] * len(lefts)
                    + [pltpu.VMEM((4 * rows, cut), bf16)],
                )

            one_own, one_mirror = square(0, [(a, a_join)], [dm, dm_x, dm_z, dm_d])
            one_got = to_batch(one_mirror, 4)
        else:
            da_cross = to_y(da_pair)
        row_tile = pl.BlockSpec((half // tiles, D), rolled(0))
        row_mod = pl.BlockSpec((half // tiles, D), lambda i, *_: (i % tiles, 0))
        last = main.last

        def input_norm_back():
            order = Order(meta)
            order.last = last
            joined = ()
            if full:
                dh_all = Order(meta).run(
                    join_kernel,
                    (1,),
                    [pl.BlockSpec(memory_space=pl.ANY)] * 3,
                    pl.BlockSpec(memory_space=pl.ANY),
                    shape_of((3 * half, 2 * block)),
                    dh_got,
                    [pltpu.VMEM((3, half, 2 * block), f32), pltpu.SemaphoreType.DMA((6,))],
                )
                joined = [dh_all] * 3 + [to_core(dh_all)] * 3
            outs = order.run(
                norm1_kernel,
                (2 * tiles,),
                [row_tile, row_tile, row_mod,
                 pl.BlockSpec((half // tiles, D), lambda i, m: (m[0] * tiles + i % tiles, 0)),
                 pl.BlockSpec((half // tiles, D + 128), lambda i, *_: (i % tiles, 0)), row_spec,
                 row_spec, whole((8, D))],
                [row_tile, whole((8, D))],
                [shape_of((rows, D)), shape_of((8, D))],
                (da_pair, da_cross, h1, tokens, dh_mine, line(norm1_gain),
                 line(down_bias), d_sums),
            )
            return outs, joined

        (mine, d_sums), dh_join = segment(input_norm_back)
        if full:
            dv_z, dv_d, dh_join = meet(dv_z, dv_d, dh_join)
            two_own, two_mirror = square(
                1, [(a, a_join), (dhl, dh_join)], [dv, dv_x, dv_z, dv_d]
            )
            two_got = to_batch(two_mirror, 4)

        def place():
            order = Order(meta)
            sums = d_sums + to_core(d_sums)
            other = to_core(mine)
            outs = [
                order.run(
                    place_kernel,
                    (2 * tiles,),
                    [pl.BlockSpec((half // tiles, D), functools.partial(
                        lambda first, i, *_: (first + i % tiles, 0), first))] * 2,
                    row_tile,
                    low_rows,
                    (mine, other),
                )
                for first in (tiles, 0)
            ]
            return (*outs, sums)

        result, tokens_grad, d_sums = segment(place)

        def small_sums():
            comb = jnp.concatenate([d_sums, h_sums], axis=1)
            for s in (1, 2, 4):
                comb = comb + to_batch(comb, s)
            return comb

        lanes = hidden // 128
        per = 128 // nb
        if not full:

            def scatter(value, axis):
                return lax.psum_scatter(value, "batch", scatter_dimension=axis, tiled=True)

            d_sums = scatter(d_sums, 1)
            h_sums = lax.psum(h_sums, "batch")
            h_parts = scatter(h_sum[:3].reshape(3, lanes, 128), 2)
            dm_low = jnp.concatenate([dm, dv[:, :width]], axis=1).astype(bf16)
            z = dv[:, width:]
            grad_qkv = scatter(
                jnp.stack([mm_tn(a, dm_low[:, j * width : (j + 1) * width]) for j in range(3)], 1), 0
            )
            grad_out = scatter(mm_tn(z.astype(bf16), dhl), 1)
            grad_up = scatter(mm_tn(b, du), 0)
            grad_down = scatter(mm_tn(w, dyl), 1)
        else:
            near_got, sums, d_sums = meet(near_got, sums, d_sums)
            h_parts = (sums[2][2 * block :] + near_got[2 * block :])[:3]
            h_parts = lax.dynamic_slice_in_dim(
                h_parts.reshape(3, lanes, 128), index * per, per, 2
            )
            strip = hidden // 4
            grad_up, grad_down = main.run(
                final_hidden_kernel,
                (4,),
                [pl.BlockSpec((block, strip), rolled(1))] * 3
                + [pl.BlockSpec((block, strip), lambda i, *_: (1, i))],
                [pl.BlockSpec((block, strip), rolled(1)), pl.BlockSpec((strip, block), rolled(0))],
                [shape_of((block, hidden)), shape_of((hidden, block))],
                (sums[0], near_got, sums[1], near_got),
            )
            d_sums, grad_up = meet(d_sums, grad_up)
            comb = segment(small_sums)
            d_sums = lax.dynamic_slice_in_dim(comb, index * block, block, 1)
            h_sums = comb[:, D:]
            grad_qkv, grad_out = main.run(
                final_square_kernel,
                (1,),
                [whole((block, cut))] * 4,
                [whole((3, block, width)), whole((width, block))],
                [shape_of((3, block, width)), shape_of((width, block))],
                (one_own, one_got, two_own, two_got),
            )
            grad_qkv = jnp.transpose(grad_qkv, (1, 0, 2))
        per = HD // nb

        def own_part(value, shape):
            return lax.dynamic_slice_in_dim(value.reshape(shape), index * per, per, len(shape) - 1)

        return (
            result,
            tokens_grad,
            d_sums[4],
            d_sums[5],
            grad_qkv,
            own_part(h_sums[2:5], (3, heads, HD)),
            own_part(h_sums[0], (heads, HD)),
            own_part(h_sums[1], (heads, HD)),
            grad_out,
            d_sums[2],
            d_sums[0],
            d_sums[1],
            grad_up,
            h_parts[0],
            h_parts[1],
            h_parts[2],
            grad_down,
            d_sums[3],
        )

    return local


def solution(mesh):
    in_specs = (
        P("batch", None),
        P("batch"),
        P("batch", None),
        P(),
        P(),
        P(None, None, "mp"),
        P(None, "mp", None),
        P("mp", None),
        P("mp", None),
        P("mp", None),
        P(),
        P(),
        P(),
        P(None, "mp"),
        P("mp"),
        P("mp"),
        P("mp"),
        P("mp", None),
        P(),
    )
    out_specs = (
        P("batch", None),
        P("batch", None),
        P("batch"),
        P("batch"),
        P("batch", None, "mp"),
        P(None, "mp", "batch"),
        P("mp", "batch"),
        P("mp", "batch"),
        P("mp", "batch"),
        P("batch"),
        P("batch"),
        P("batch"),
        P("batch", "mp"),
        P("mp", "batch"),
        P("mp", "batch"),
        P("mp", "batch"),
        P("mp", "batch"),
        P("batch"),
    )
    local = make_local(mesh.shape["batch"], mesh.shape["mp"])
    return jax.shard_map(local, mesh=mesh, in_specs=in_specs, out_specs=out_specs, check_vma=False)
```

```python
import functools
import math

import jax
import jax.numpy as jnp
import numpy as np
from jax import lax
from jax.experimental import pallas as pl
from jax.experimental.pallas import tpu as pltpu
from jax.sharding import PartitionSpec as P

HD = 64
QUAD = 4 * HD
PAIR = 2 * HD

norm_eps = 1e-05
rope_base = 10000.0
xpos_base = 512.0
masked_score = -1e30
root_half = 2.0**-0.5
density_scale = 1.0 / math.sqrt(2.0 * math.pi)
f32 = jnp.float32
bf16 = jnp.bfloat16
MIB = 1 << 20
COVER = 10**11


def dot(a, b, dims):
    return lax.dot_general(a, b, (dims, ((), ())), preferred_element_type=f32)


def mm(a, b):
    return dot(a, b, ((1,), (0,)))


def mm_nt(a, b):
    return dot(a, b, ((1,), (1,)))


def mm_tn(a, b):
    return dot(a, b, ((0,), (0,)))


def row_mean(value):
    return jnp.mean(value, axis=-1, keepdims=True)


def row_sum(value):
    return jnp.sum(value, axis=-1, keepdims=True)


def unit_rows(value):
    center = value - row_mean(value)
    inverse = lax.rsqrt(row_mean(center * center) + norm_eps)
    return center * inverse, inverse


def unit_back(grad, unit, inverse, gain):
    scaled = grad * gain
    return inverse * (scaled - row_mean(scaled) - unit * row_mean(scaled * unit))


def turn_tables(count):
    half = HD // 2
    places = np.arange(count, dtype=np.float64)[:, None]
    pair = np.arange(half, dtype=np.float64)[None, :]
    angles = places * rope_base ** (-2.0 * pair / HD)
    zeta = (2.0 * pair + 0.4 * HD) / (1.4 * HD)
    factor = zeta ** ((places - count // 2) / xpos_base)
    tables = []
    for scale in (factor, 1.0 / factor):
        tables.append(np.tile(np.cos(angles) * scale, (1, 4)))
        tables.append(np.tile(np.concatenate([-np.sin(angles), np.sin(angles)], 1), (1, 2))
                      * np.tile(scale, (1, 4)))
    return np.stack(tables).astype(np.float32)


def half_swap(value):
    lane = lax.broadcasted_iota(jnp.int32, value.shape, 1)
    return jnp.where(
        (lane & 32) == 0,
        pltpu.roll(value, value.shape[1] - 32, 1),
        pltpu.roll(value, 32, 1),
    )


def whole(shape):
    return pl.BlockSpec(shape, lambda *_: (0,) * len(shape))


def shape_of(shape, dtype=f32):
    return jax.ShapeDtypeStruct(shape, dtype)


def call(body, grid, ins, outs, shapes, scratch=(), tokens=0, cover=0):
    count = len(ins)

    def kernel(meta, *refs):
        body(meta, *refs[:count], *refs[count + tokens :])

    return pl.pallas_call(
        kernel,
        grid_spec=pltpu.PrefetchScalarGridSpec(
            num_scalar_prefetch=1,
            grid=grid,
            in_specs=list(ins) + [pl.BlockSpec(memory_space=pl.ANY)] * tokens,
            out_specs=outs,
            scratch_shapes=list(scratch),
        ),
        out_shape=shapes,
        compiler_params=pltpu.CompilerParams(
            dimension_semantics=("arbitrary",) * len(grid), vmem_limit_bytes=64 * MIB
        ),
        cost_estimate=pl.CostEstimate(flops=cover, bytes_accessed=0, transcendentals=0)
        if cover
        else None,
    )


class Order:
    def __init__(self, meta, cover=0):
        self.meta = meta
        self.last = []
        self.cover = cover

    def run(self, body, grid, ins, outs, shapes, args, scratch=(), wait=()):
        extra = list(wait) + self.last
        made = call(body, grid, ins, outs, shapes, scratch, len(extra), self.cover)(
            self.meta, *args, *extra
        )
        self.last = [made[0] if isinstance(made, (list, tuple)) else made]
        return made


def half_at(meta, which, half):
    return pl.ds(pl.multiple_of(((meta[0] + which) % 2) * half, half), half)


def spread(ref, count, first=0):
    return jnp.concatenate([ref[pl.ds(first + i, 1), :] for i in range(count)], axis=1)


def mask_kernel(meta, cot, mine):
    size = mine.shape[0]
    first = (meta[0] * pl.num_programs(0) + pl.program_id(0)) * size
    place = first + lax.broadcasted_iota(jnp.int32, (size, 1), 0)
    mine[...] = cot[...].astype(f32) * jnp.where(place < meta[1], 1.0, 0.0)


def send_pieces(meta, value, outs, block):
    for s, out in enumerate(outs):
        at = meta[2] ^ (s + 1)
        for part, where in ((0, at), (1, at ^ 4)):
            cols = pl.ds(pl.multiple_of(where * block, block), block)
            out[:, part * block : (part + 1) * block] = value[:, cols].astype(f32)


def flip_rows(value, half):
    return jnp.concatenate(
        [
            value[(i ^ 1) * half : ((i ^ 1) + 1) * half]
            for i in range(value.shape[0] // half)
        ],
        axis=0,
    )


def join_two(one, two, count):
    mean = 0.5 * (one[0] + two[0])
    gap = one[0] - two[0]
    joined = [mean, one[1] + two[1] + (0.5 * count) * gap * gap]
    if len(one) > 2:
        joined += [
            one[2] + two[2],
            one[3] + two[3] + one[2] * (one[0] - mean) + two[2] * (two[0] - mean),
        ]
    return joined


def join_all(ref, odd, count):
    cols = []
    for i in range(ref.shape[0]):
        value = ref[i]
        half = value.shape[0] // 2
        value = jnp.where(odd == i % 2, value, flip_rows(value, half))
        cols.append([value[:, c : c + 1] for c in range(4)])
    while len(cols) > 1:
        cols = [join_two(cols[i], cols[i + 1], count) for i in range(0, len(cols), 2)]
        count *= 2
    return cols[0]


def diagonal(count):
    return lax.broadcasted_iota(jnp.int32, (count, count), 0) == lax.broadcasted_iota(
        jnp.int32, (count, count), 1
    )


def as_row(column):
    return jnp.sum(jnp.where(diagonal(column.shape[0]), column, 0.0), axis=0, keepdims=True)


def as_column(row):
    return row_sum(jnp.where(diagonal(row.shape[1]), row, 0.0))


def attend_kernel(nb, meta, tok, gain, shift, weight, bias, sub_gain, sub_shift, out_w, table,
                  a_out, q_out, k_out, v_out, p_out, o_out, y_mine, y_other,
                  *rest):
    sends, (a_low, o_all) = rest[:-2], rest[-2:]
    rows, width = o_all.shape
    half = rows // 2
    step = pl.program_id(0)
    places = lax.broadcasted_iota(jnp.int32, (rows, 1), 0) ^ (meta[0] * half)
    keys = lax.broadcasted_iota(jnp.int32, (1, rows), 1) ^ (meta[0] * half)
    allowed = (keys <= places) & (keys < meta[1])

    @pl.when(step == 0)
    def _():
        for which in range(2):
            unit, _ = unit_rows(tok[half_at(meta, which, half), :].astype(f32))
            wide = unit * gain[...] + shift[...]
            a_low[which * half : (which + 1) * half, :] = wide.astype(bf16)
        a_out[...] = a_low[...]
        if sends:
            send_pieces(meta, a_low.at[0:half, :], sends, tok.shape[1] // nb)

    turned = []
    for j in range(3):
        m = mm(a_low[...], weight[j])
        m = m + jnp.concatenate(
            [bias[j, pl.ds(step * 4 + i, 1), :] for i in range(4)], axis=1
        )
        if j < 2:
            flipped = half_swap(m)
            parts = []
            for which in range(2):
                at = half_at(meta, which, half)
                here = slice(which * half, (which + 1) * half)
                c = jnp.concatenate([table[2 * j, at, :]] * 2, axis=1)
                s = jnp.concatenate([table[2 * j + 1, at, :]] * 2, axis=1)
                parts.append(m[here] * c + flipped[here] * s)
            m = jnp.concatenate(parts, axis=0)
        turned.append(m.astype(bf16))
    q, k, v = turned
    q = q * jnp.asarray(1.0 / math.sqrt(HD), bf16)
    q_out[...] = q
    k_out[...] = k
    v_out[...] = v
    lane = lax.broadcasted_iota(jnp.int32, (1, PAIR), 1)
    for p in range(2):
        here = slice(p * PAIR, (p + 1) * PAIR)
        total = None
        for h in range(2):
            mask = (lane // HD) == h
            scores = mm_nt(jnp.where(mask, q[:, here], jnp.zeros_like(q[:, here])), k[:, here])
            scores = jnp.where(allowed, scores, masked_score)
            weights = jnp.exp(scores - jnp.max(scores, axis=-1, keepdims=True))
            probs = weights * (1.0 / row_sum(weights))
            p_out[p * 2 + h] = probs
            part = mm(
                probs.astype(bf16), jnp.where(mask, v[:, here], jnp.zeros_like(v[:, here]))
            )
            total = part if total is None else total + part
        o_all[:, pl.ds(pl.multiple_of(step * QUAD + p * PAIR, PAIR), PAIR)] = total

    @pl.when(step == pl.num_programs(0) - 1)
    def _():
        o = o_all[...]
        o_out[...] = o
        mean = row_mean(o)
        center = o - mean
        stat_rows = jnp.concatenate([as_row(mean), as_row(row_sum(center * center))], axis=0)
        heads = width // HD
        gain_row, shift_row = spread(sub_gain, heads), spread(sub_shift, heads)
        pieces = []
        for row in (gain_row, shift_row):
            for _ in range(3):
                low = row.astype(bf16)
                pieces.append(low)
                row = row - low.astype(f32)
        vecs = mm(jnp.concatenate(pieces + [jnp.zeros((2, width), bf16)], axis=0), out_w[...])
        gain_out = vecs[0:1] + vecs[1:2] + vecs[2:3]
        shift_out = vecs[3:4] + vecs[4:5] + vecs[5:6]
        extra = jnp.concatenate([gain_out, shift_out, jnp.zeros((6, vecs.shape[1]), f32)], axis=0)
        low = (center * gain_row).astype(bf16)
        for which, out in ((1, y_other), (0, y_mine)):
            here = slice(which * half, (which + 1) * half)
            out[0:half, :] = mm(low[here], out_w[...]) + mean[here] * gain_out
            out[half : half + 8, :] = extra
            for p in range(2):
                out[half + 2 + 2 * p : half + 4 + 2 * p, 0:rows] = jnp.where(
                    meta[0] == p, stat_rows, jnp.zeros_like(stat_rows)
                )


def join_rows(refs, odd, count):
    cols = []
    for ref in refs:
        half = ref.shape[1] // 2
        for p in range(2):
            rows = ref[2 + 2 * p : 4 + 2 * p, :]
            swapped = jnp.concatenate([rows[:, half:], rows[:, :half]], axis=1)
            rows = jnp.where(odd == p, rows, swapped)
            cols.append([rows[0:1], rows[1:2]])
    near = join_two(cols[0], cols[1], count)
    far = join_two(cols[2], cols[3], count)
    return join_two(near, far, 2 * count)


def middle_kernel(attn_width, meta, one, two, one_extra, two_extra, tok, bias, gain, shift,
                   h_out, branch_out, b_out, vec_out, stats):
    size = h_out.shape[0]
    step = pl.program_id(0)

    @pl.when(step == 0)
    def _():
        rows = stats.shape[0]
        extras = (one_extra.at[:, 0:rows], two_extra.at[:, 0:rows])
        mean, m2 = join_rows(extras, meta[0], attn_width // 4)
        inverse = lax.rsqrt(m2 * (1.0 / attn_width) + norm_eps)
        stats[...] = jnp.concatenate([as_column(mean), as_column(inverse)], axis=1)
        vec_out[...] = one_extra[...] + two_extra[...]

    at = pl.ds(pl.multiple_of(step * size, size), size)
    branch = stats[at, 1:2] * ((one[...] + two[...]) - stats[at, 0:1] * vec_out[0:1, :])
    branch_out[...] = branch
    h1 = tok[...].astype(f32) + (branch + vec_out[1:2, :]) + bias[...]
    h_out[...] = h1
    unit, _ = unit_rows(h1)
    b_out[...] = unit * gain[...] + shift[...]


def dw_kernel(meta, cot, weight, out, low):
    half = cot.shape[0] // 2

    @pl.when(pl.program_id(0) == 0)
    def _():
        for which in range(2):
            first = ((meta[0] + which) % 2) * half
            place = first + lax.broadcasted_iota(jnp.int32, (half, 1), 0)
            rows = cot[half_at(meta, which, half), :]
            low[which * half : (which + 1) * half, :] = jnp.where(
                place < meta[1], rows, jnp.zeros_like(rows)
            )

    out[...] = mm_nt(low[...], weight[...]).astype(bf16)


def first_kernel(meta, mine, other, weight, bias, gain, dw, g_out, slope_out, stat_out, low,
                 mean_s, m2_s, s1_s, s2_s):
    half = mine.shape[0]
    step = pl.program_id(0)
    span = weight.shape[1]

    @pl.when(step == 0)
    def _():
        low[0:half, :] = mine[...].astype(bf16)
        low[half:, :] = other[...].astype(bf16)
        for ref in (mean_s, m2_s, s1_s, s2_s):
            ref[...] = jnp.zeros_like(ref)

    done = step.astype(f32)
    share = 1.0 / (done + 1.0)
    u = mm(low[...], weight[...]) + bias[...]
    cdf = 0.5 + 0.5 * lax.erf(u * root_half)
    density = jnp.exp(-0.5 * (u * u)) * density_scale
    g = u * cdf
    slope_out[...] = (cdf + u * density).astype(bf16)
    g_out[...] = g.astype(bf16)
    scaled = dw[...].astype(f32) * gain[...]
    mean_c = row_mean(g)
    center = g - mean_c
    s1_c = row_sum(scaled)
    s2_c = row_sum(scaled * center)
    gap = mean_c - mean_s[...]
    mean_new = mean_s[...] + gap * share
    m2_s[...] += row_sum(center * center) + gap * gap * (span * done * share)
    s2_s[...] += s2_c + s1_s[...] * (mean_s[...] - mean_new) + s1_c * (mean_c - mean_new)
    s1_s[...] += s1_c
    mean_s[...] = mean_new

    @pl.when(step == pl.num_programs(0) - 1)
    def _():
        stat_out[...] = jnp.concatenate([mean_s[...], m2_s[...], s1_s[...], s2_s[...]], axis=1)


def hidden_stats(ref, odd, out, count, ff_width):
    mean, m2, s1, s2 = join_all(ref, odd, count)
    inverse = lax.rsqrt(m2 * (1.0 / ff_width) + norm_eps)
    out[...] = jnp.concatenate(
        [mean, inverse, s1 * (1.0 / ff_width), inverse * s2 * (1.0 / ff_width)], axis=1
    )


def hidden_rows(g, slope, dw, stats, gain, shift):
    inverse = stats[:, 1:2]
    unit = (g.astype(f32) - stats[:, 0:1]) * inverse
    w = (unit * gain + shift).astype(bf16)
    dw = dw.astype(f32)
    dg = inverse * (dw * gain - stats[:, 2:3] - unit * stats[:, 3:4])
    return w, (dg * slope.astype(f32)).astype(bf16), dw * unit, dw


def back_kernel(ff_width, span, meta, g, slope, dw, parts, gain, shift, weight, w_out, du_out, stats,
                sum_out, db_mine, db_other):
    half = db_mine.shape[0]

    @pl.when(pl.program_id(0) == 0)
    def _():
        hidden_stats(parts, meta[0], stats, ff_width // parts.shape[0], ff_width)
        for c in range(g.shape[1] // span):
            at = slice(c * span, (c + 1) * span)
            w, du, gain_part, dw_wide = hidden_rows(
                g[:, at], slope[:, at], dw[:, at], stats[...], gain[:, at], shift[:, at]
            )
            w_out[:, at] = w
            du_out[:, at] = du
            sum_out[:, at] = hidden_sums(du, gain_part, dw_wide)

    part = mm_nt(du_out[...], weight[...])
    db_mine[...] = part[0:half, :]
    db_other[...] = part[half:, :]


def hidden_sums(du, gain_part, dw_wide):
    return jnp.concatenate(
        [
            jnp.sum(du.astype(f32), axis=0, keepdims=True),
            jnp.sum(gain_part, axis=0, keepdims=True),
            jnp.sum(dw_wide, axis=0, keepdims=True),
            jnp.zeros((5, du.shape[1]), f32),
        ],
        axis=0,
    )


def pack_kernel(meta, *refs):
    sources, (out, buffer, sems) = refs[:8], refs[8:]
    where = meta[2] // 2
    inner = (where == 1) | (where == 2)
    half = buffer.shape[1]

    def loads(first):
        return [
            pltpu.make_async_copy(sources[2 * i + first], buffer.at[i], sems.at[i])
            for i in range(4)
        ]

    @pl.when(inner)
    def _():
        for copy in loads(0):
            copy.start()

    @pl.when(jnp.logical_not(inner))
    def _():
        for copy in loads(1):
            copy.start()

    stores = []
    for i, copy in enumerate(loads(0)):
        copy.wait()
        store = pltpu.make_async_copy(
            buffer.at[i], out.at[i * half : (i + 1) * half, :], sems.at[4 + i]
        )
        store.start()
        stores.append(store)
    for store in stores:
        store.wait()


def far_kernel(starts, lower, own, meta, *refs):
    groups = len(starts)
    count = 1 + max(source for pair in starts for source, _ in pair)
    b_src, d_src, refs = refs[:count], refs[count : 2 * count], refs[2 * count :]
    stat_refs, rest = refs[: 2 * groups], refs[2 * groups :]
    up_w, up_b, gain, shift, down_w = rest[:5]
    rest = rest[5:]
    if own:
        w_own, du_own, sum_own, *cols = rest[:7]
        rest = rest[7:]
        ins = ()
    else:
        ins, rest = rest[:3], rest[3:]
    (up_out, down_out, near_out), (b_low, d_low, stats, buffer, sem) = rest[:3], rest[3:]
    half = buffer.shape[1]
    rows = 2 * half
    block = up_out.shape[0]
    where = meta[2] // 2
    inner = (where == 1) | (where == 2)
    mine = pl.ds(pl.multiple_of(meta[2] * block, block), block)
    near = pl.ds(pl.multiple_of((meta[2] ^ 1) * block, block), block)

    @pl.when(pl.program_id(0) == 0)
    def _():
        copies = []
        for n, pair in enumerate(starts):
            for k, (refs_k, low) in enumerate(((b_src, b_low), (d_src, d_low))):
                for i, (source, first) in enumerate(pair):
                    slot = 4 * n + 2 * k + i
                    copy = pltpu.make_async_copy(
                        refs_k[source].at[first + k * lower : first + k * lower + half, :], buffer.at[slot], sem.at[slot]
                    )
                    copy.start()
                    copies.append((copy, low, n * rows + i * half, slot))
        for n in range(groups):
            stats[n * rows : (n + 1) * rows, :] = jnp.where(
                inner, stat_refs[2 * n][...], stat_refs[2 * n + 1][...]
            )
        for copy, low, at, slot in copies:
            copy.wait()
            low[at : at + half, :] = buffer[slot].astype(bf16)

    for n in range(groups):
        at = slice(n * rows, (n + 1) * rows)
        u = mm(b_low[at, :], up_w[...]) + up_b[...]
        cdf = 0.5 + 0.5 * lax.erf(u * root_half)
        density = jnp.exp(-0.5 * (u * u)) * density_scale
        dw = mm_nt(d_low[at, :], down_w[...])
        w, du, gain_part, dw_wide = hidden_rows(
            u * cdf, cdf + u * density, dw, stats[at, :], gain[...], shift[...]
        )
        terms = [
            mm_tn(b_low[at, mine], du),
            mm_tn(d_low[at, mine], w),
            mm_tn(b_low[at, near], du),
            mm_tn(d_low[at, near], w),
            hidden_sums(du, gain_part, dw_wide),
        ]
        totals = terms if n == 0 else [t + s for t, s in zip(totals, terms)]
    if own:
        terms = [
            mm_tn(cols[0][...], du_own[...]),
            mm_tn(cols[2][...], w_own[...]),
            mm_tn(cols[1][...], du_own[...]),
            mm_tn(cols[3][...], w_own[...]),
            sum_own[...],
        ]
    else:
        low, high = ins[2][0:block, :], ins[2][block : 2 * block, :]
        terms = [ins[0][...], ins[1][...], low, high, ins[2][2 * block :, :]]
    totals = [t + s for t, s in zip(totals, terms)]
    up_out[...] = totals[0]
    down_out[...] = totals[1]
    near_out[0:block, :] = totals[2]
    near_out[block : 2 * block, :] = totals[3]
    near_out[2 * block :, :] = totals[4]


def norm2_kernel(nb, meta, one, two, h1, dy, branch, vecs, gain, dh_out, sum_out, *sends):
    size, full = h1.shape
    db = one[...] + two[...]
    unit, inverse = unit_rows(h1[...])
    dh1 = dy[...] + unit_back(db, unit, inverse, gain[...])
    low = dh1.astype(bf16).astype(f32)
    dh_out[:, 0:full] = dh1
    lane = lax.broadcasted_iota(jnp.int32, (size, 128), 1)
    dh_out[:, full : full + 128] = jnp.where(
        lane == 0, row_sum(low * vecs[0:1]), row_sum(low * branch[...])
    )
    sums = jnp.concatenate(
        [
            jnp.sum(db * unit, axis=0, keepdims=True),
            jnp.sum(db, axis=0, keepdims=True),
            jnp.sum(dh1, axis=0, keepdims=True),
            jnp.sum(dy[...], axis=0, keepdims=True),
            jnp.zeros((4, full), f32),
        ],
        axis=0,
    )

    @pl.when(pl.program_id(0) == 0)
    def _():
        sum_out[...] = sums

    @pl.when(pl.program_id(0) > 0)
    def _():
        sum_out[...] += sums
    if sends:
        send_pieces(meta, dh_out, sends, full // nb)


def attend_back_kernel(attn_width, meta, dh_mine, dh_other, o_all, stats, sub_gain, sub_shift, out_w, q_all,
                       k_all, v_all, probs_all, table, dm_out, dv_out, sum_out, dhl_out, do_all):
    rows, width = o_all.shape
    half = rows // 2
    full = out_w.shape[1]
    heads = width // HD
    step = pl.program_id(0)

    @pl.when(step == 0)
    def _():
        gain_row = spread(sub_gain, heads)
        dhl = jnp.concatenate(
            [dh_mine[:, 0:full].astype(bf16), dh_other[:, 0:full].astype(bf16)], axis=0
        )
        dhl_out[...] = dhl
        sums = jnp.concatenate([dh_mine[:, full:], dh_other[:, full:]], axis=0)
        dz = mm_nt(dhl, out_w[...])
        inverse = stats[:, 1:2]
        unit = (o_all[...] - stats[:, 0:1]) * inverse
        do = inverse * (
            dz * gain_row
            - sums[:, 0:1] * (1.0 / attn_width)
            - unit * (sums[:, 1:2] * (1.0 / attn_width))
        )
        do_all[...] = do.astype(bf16)
        dv_out[:, width:] = unit * gain_row + spread(sub_shift, heads)
        sum_out[0:1, :] = jnp.sum(dz * unit, axis=0, keepdims=True)
        sum_out[1:2, :] = jnp.sum(dz, axis=0, keepdims=True)
        sum_out[5:8, :] = jnp.zeros((3, width), f32)

    quad = pl.ds(pl.multiple_of(step * QUAD, QUAD), QUAD)
    do = do_all[:, quad]
    q, k, v = q_all[...], k_all[...], v_all[...]
    lane = lax.broadcasted_iota(jnp.int32, (1, PAIR), 1)
    grads = [[], [], []]
    for p in range(2):
        here = slice(p * PAIR, (p + 1) * PAIR)
        total = [None] * 3
        for h in range(2):
            mask = (lane // HD) == h

            def only(value):
                return jnp.where(mask, value[:, here], jnp.zeros_like(value[:, here]))

            probs = probs_all[p * 2 + h]
            do_h = only(do)
            dprobs = mm_nt(do_h, v[:, here])
            inner = row_sum(probs * dprobs)
            dscores = (probs * (dprobs - inner)).astype(bf16)
            parts = (
                mm(dscores, only(k)),
                mm_tn(dscores, only(q)),
                mm_tn(probs.astype(bf16), do_h),
            )
            total = [part if t is None else t + part for t, part in zip(total, parts)]
        for j in range(3):
            grads[j].append(total[j])
    for j in range(3):
        grad = jnp.concatenate(grads[j], axis=1)
        if j == 0:
            grad = grad * (1.0 / math.sqrt(HD))
        if j < 2:
            flipped = half_swap(grad)
            parts = []
            for which in range(2):
                at = half_at(meta, which, half)
                here = slice(which * half, (which + 1) * half)
                c = jnp.concatenate([table[2 * j, at, :]] * 2, axis=1)
                s = jnp.concatenate([table[2 * j + 1, at, :]] * 2, axis=1)
                parts.append(grad[here] * c - flipped[here] * s)
            grad = jnp.concatenate(parts, axis=0)
        if j < 2:
            dm_out[:, pl.ds(pl.multiple_of(j * width + step * QUAD, QUAD), QUAD)] = grad
        else:
            dv_out[:, quad] = grad
        sum_out[2 + j : 3 + j, quad] = jnp.sum(
            grad.astype(bf16).astype(f32), axis=0, keepdims=True
        )


def tail_kernel(meta, dm, dv, weight, w, down_w, mine, other, low):
    half = mine.shape[0] // 2
    width = weight.shape[2]

    @pl.when(pl.program_id(0) == 0)
    def _():
        low[:, 0 : 2 * width] = dm[...].astype(bf16)
        low[:, 2 * width :] = dv[...].astype(bf16)

    total = mm_nt(low[:, 0:width], weight[0])
    for j in (1, 2):
        total = total + mm_nt(low[:, j * width : (j + 1) * width], weight[j])
    part = mm(w[...], down_w[...])
    mine[0:half, :] = total[0:half, :]
    mine[half:, :] = part[0:half, :]
    other[0:half, :] = total[half:, :]
    other[half:, :] = part[half:, :]


def norm1_kernel(meta, one, two, h1, tok, dh, gain, bias, sum_in, out, sum_out):
    full = out.shape[1]
    step = pl.program_id(0)
    total = one[...] + two[...]

    @pl.when(step == 0)
    def _():
        sum_out[...] = sum_in[...]

    @pl.when(step < pl.num_programs(0) // 2)
    def _():
        unit, inverse = unit_rows(tok[...].astype(f32))
        out[...] = dh[:, 0:full] + unit_back(total, unit, inverse, gain[...])
        sum_out[4:5, :] += jnp.sum(total * unit, axis=0, keepdims=True)
        sum_out[5:6, :] += jnp.sum(total, axis=0, keepdims=True)

    @pl.when(step >= pl.num_programs(0) // 2)
    def _():
        out[...] = h1[...] + total + bias[...]


def place_kernel(meta, mine, other, out):
    tiles = pl.num_programs(0) // 2
    local = (pl.program_id(0) // tiles) == meta[0]
    out[...] = jnp.where(local, mine[...], other[...]).astype(bf16)


def add_kernel(count, meta, *refs):
    total = refs[0][...]
    for ref in refs[1:count]:
        total = total + ref[...]
    refs[count][...] = total


def join_kernel(meta, *refs):
    pieces, (out, buffer, sems) = refs[:3], refs[3:]
    half = buffer.shape[1]
    loads = [pltpu.make_async_copy(pieces[i], buffer.at[i], sems.at[i]) for i in range(3)]
    for copy in loads:
        copy.start()
    stores = []
    for i, copy in enumerate(loads):
        copy.wait()
        store = pltpu.make_async_copy(
            buffer.at[i], out.at[i * half : (i + 1) * half, :], sems.at[3 + i]
        )
        store.start()
        stores.append(store)
    for store in stores:
        store.wait()


def square_kernel(nb, part, meta, *refs):
    lists, rest = refs[: 7 * (part + 1)], refs[7 * (part + 1) :]
    sides, (own_out, mirror_out), lows = rest[:4], rest[4:6], rest[6:]
    right = lows[-1]
    rows, full = lists[0].shape
    half, block = rows // 2, full // nb
    width = own_out.shape[1] // 2
    for n, low in enumerate(lows[:-1]):
        own, mine, other = lists[7 * n], lists[7 * n + 1 : 7 * n + 4], lists[7 * n + 4 : 7 * n + 7]
        for which, at in ((0, meta[2]), (1, meta[2] ^ 4)):
            cols = pl.ds(pl.multiple_of(at * block, block), block)
            low[0:rows, which * block : (which + 1) * block] = own[:, cols]
        for s in range(3):
            here = rows * (s + 1)
            low[here : here + half, :] = mine[s][...].astype(bf16)
            low[here + half : here + rows, :] = other[s][...].astype(bf16)
    for s in range(4):
        right[rows * s : rows * (s + 1), :] = sides[s][...].astype(bf16)
    for out, first in ((mirror_out, block), (own_out, 0)):
        left = lows[0][:, first : first + block]
        if part == 0:
            out[...] = mm_tn(left, right[...])
        else:
            out[:, 0:width] = mm_tn(left, right[:, 0:width])
            out[:, width:] = mm_tn(lows[1][:, first : first + block], right[:, width:])


def final_square_kernel(meta, one_own, one_got, two_own, two_got, m_out, o_out):
    width = m_out.shape[2]
    for j in range(2):
        cols = slice(j * width, (j + 1) * width)
        m_out[j] = one_own[:, cols] + one_got[:, cols]
    m_out[2] = two_own[:, 0:width] + two_got[:, 0:width]
    o_out[...] = (two_own[:, width:] + two_got[:, width:]).T


def final_hidden_kernel(meta, up_own, up_got, down_own, down_got, up_out, down_out):
    up_out[...] = up_own[...] + up_got[...]
    down_out[...] = (down_own[...] + down_got[...]).T


def make_local(nb, nm):
    pair = [(i, i ^ 1) for i in range(nm)]
    cross = [(i, i ^ 2) for i in range(nm)]
    full = nb == 8
    middle_link = [(2, 4), (3, 5), (4, 2), (5, 3)]
    outward_link = [(2, 0), (3, 1), (4, 6), (5, 7)]

    def to_core(value):
        return lax.ppermute(value, "mp", pair)

    def to_y(value):
        return lax.ppermute(value, "mp", cross)

    def to_batch(value, s):
        return lax.ppermute(value, "batch", [(i, i ^ s) for i in range(nb)])

    def to_middle(value):
        return lax.ppermute(value, "batch", middle_link)

    def outward(value):
        return lax.ppermute(value, "batch", outward_link)

    def local(
        tokens,
        lengths,
        cotangent,
        norm1_gain,
        norm1_shift,
        qkv_weight,
        qkv_bias,
        sub1_gain,
        sub1_shift,
        out_weight,
        out_bias,
        norm2_gain,
        norm2_shift,
        up_weight,
        up_bias,
        sub2_gain,
        sub2_shift,
        down_weight,
        down_bias,
    ):
        rows, D = tokens.shape
        half = rows // 2
        width = out_weight.shape[0]
        heads = width // HD
        hidden = up_weight.shape[1]
        attn_width = width * nm
        ff_width = hidden * nm
        block = D // nb
        span = 512
        chunks = hidden // span
        parts = D // span
        quads = heads // 4
        sends = 3 if full else 0
        tiles = 4
        index = lax.axis_index("batch")
        meta = jnp.stack([lax.axis_index("mp") % 2, lengths[0], index]).astype(jnp.int32)
        always = lengths[0] >= 0
        table = jnp.asarray(turn_tables(rows))
        weight = jnp.transpose(qkv_weight, (1, 0, 2))

        def segment(stage):
            def skip():
                return jax.tree.map(
                    lambda s: jnp.zeros(s.shape, s.dtype), jax.eval_shape(stage)
                )

            return lax.cond(always, stage, skip)

        def meet(*values):
            return lax.optimization_barrier(values)

        def line(vec):
            return vec.reshape(1, -1)

        def rolled(step):
            return lambda i, *_: (0, i) if step == 1 else (i, 0)

        half_shape = shape_of((half, D))
        half_tile = pl.BlockSpec((half // tiles, D), rolled(0))
        tok_mine = pl.BlockSpec((half // tiles, D), lambda i, m: (m[0] * tiles + i, 0))
        ext_spec, ext_shape = whole((half + 8, D)), shape_of((half + 8, D))
        dh_spec, dh_shape = whole((half, D + 128)), shape_of((half, D + 128))
        dh_tile = pl.BlockSpec((half // tiles, D + 128), rolled(0))
        row_spec = whole((1, D))
        wide_spec, wide_shape = whole((rows, width)), shape_of((rows, width))
        quad = pl.BlockSpec((rows, QUAD), rolled(1))
        quad_weight = pl.BlockSpec((3, D, QUAD), lambda i, *_: (0, 0, i))
        probs_spec = pl.BlockSpec((4, rows, rows), lambda i, *_: (i, 0, 0))
        table_spec = whole((4, rows, PAIR))
        wide = pl.BlockSpec((1, span), rolled(1))
        tall = pl.BlockSpec((D, span), rolled(1))
        flat = pl.BlockSpec((span, D), rolled(0))
        half_part = pl.BlockSpec((half, span), rolled(1))
        many = pl.BlockSpec((rows, span), rolled(1))
        low_hidden = shape_of((rows, hidden), bf16)
        low_rows = shape_of((rows, D), bf16)
        tiny2, tiny4 = shape_of((rows, 2)), shape_of((rows, 4))
        tile = pl.BlockSpec((block, span), rolled(1))
        sum_tile = pl.BlockSpec((8, span), rolled(1))
        gain2, shift2, bias2 = line(sub2_gain), line(sub2_shift), line(up_bias)

        dy = Order(meta).run(
            mask_kernel,
            (2,),
            [pl.BlockSpec((half // 2, D), lambda i, m: (m[0] * 2 + i, 0))],
            pl.BlockSpec((half // 2, D), rolled(0)),
            half_shape,
            (cotangent,),
        )
        if full:
            dy_e1, dy_m1 = to_batch(dy, 2), to_middle(dy)

        def attention():
            order = Order(meta)
            low_shape = shape_of((rows, width), bf16)
            a, q, k, v, probs, o, y_mine, y_other, *a_sent = order.run(
                functools.partial(attend_kernel, nb),
                (quads,),
                [whole((rows, D)), row_spec, row_spec, quad_weight, whole((3, heads, HD)),
                 whole((heads, HD)), whole((heads, HD)), whole((width, D)), table_spec],
                    [whole((rows, D)), quad, quad, quad, probs_spec, wide_spec, ext_spec, ext_spec]
                + [whole((half, 2 * block))] * sends,
                [low_rows, low_shape, low_shape, low_shape,
                 shape_of((heads, rows, rows)), wide_shape, ext_shape, ext_shape]
                + [shape_of((half, 2 * block))] * sends,
                (tokens, line(norm1_gain), line(norm1_shift), weight, qkv_bias, sub1_gain,
                 sub1_shift, out_weight, table),
                [pltpu.VMEM((rows, D), bf16), pltpu.VMEM((rows, width), f32)],
            )
            y_pair = y_mine + to_core(y_other)
            return a, q, k, v, probs, o, y_pair, a_sent

        a, q, k, v, probs, o, y_pair, a_sent = segment(attention)
        if full:
            dy_e1, dy_m1, y_pair, a_sent = meet(dy_e1, dy_m1, y_pair, a_sent)
            a_got = [None, to_batch(a_sent[1], 2), to_batch(a_sent[2], 3)]
            dy_f1, dy_m2 = outward(dy_m1), to_middle(dy_e1)

        def after_attention():
            order = Order(meta)
            y_cross = to_y(y_pair)
            dw, dyl = order.run(
                dw_kernel,
                (chunks,),
                [whole((rows, D)), flat],
                [many, whole((rows, D))],
                [low_hidden, low_rows],
                (cotangent, down_weight),
            )
            return dw, dyl, order.run(
                functools.partial(middle_kernel, attn_width),
                (tiles,),
                [half_tile, half_tile] + [pl.BlockSpec((8, D), lambda i, *_: (half // 8, 0))] * 2
                + [tok_mine] + [row_spec] * 3,
                [half_tile] * 3 + [whole((8, D)), whole((rows, 2))],
                [half_shape] * 3 + [shape_of((8, D)), tiny2],
                (y_pair, y_cross, y_pair, y_cross, tokens, line(out_bias), line(norm2_gain),
                 line(norm2_shift)),
            )

        dw, dyl, (h1, branch, b_mine, vecs, stats) = segment(after_attention)
        if full:
            dy_f1, dy_m2, b_mine, a_sent, a_got[1], a_got[2] = meet(
                dy_f1, dy_m2, b_mine, a_sent, a_got[1], a_got[2]
            )
            a_got[0] = to_batch(a_sent[0], 1)
            b_e1, b_m1 = to_batch(b_mine, 2), to_middle(b_mine)

        def hidden_first():
            order = Order(meta)
            dy_core = to_core(dy_e1) if full else ()
            g, slope, stats_g, b = order.run(
                first_kernel,
                (chunks,),
                [whole((half, D))] * 2 + [tall, wide, wide, many],
                [many, many, whole((rows, 4)), whole((rows, D))],
                [low_hidden, low_hidden, tiny4, low_rows],
                (b_mine, to_core(b_mine), up_weight, bias2, gain2, dw),
                [pltpu.VMEM((rows, 1), f32)] * 4,
            )
            return g, slope, lax.all_gather(stats_g, "mp"), b, dy_core

        g, slope, g_stats, b, dy_core = segment(hidden_first)
        if full:
            b_e1, b_m1, a_got, g, dy_core = meet(b_e1, b_m1, a_got, g, dy_core)
            b_f1, b_m2 = outward(b_m1), to_middle(b_e1)

        def hidden_back():
            order = Order(meta)
            b_core, a_core = (to_core(b_e1), [to_core(a_got[1])]) if full else ((), [])
            w, du, st, h_sum, db_mine, db_other = order.run(
                functools.partial(back_kernel, ff_width, span),
                (parts,),
                [whole((rows, hidden))] * 3 + [whole((nm, rows, 4))]
                + [whole((1, hidden))] * 2 + [pl.BlockSpec((span, hidden), rolled(0))],
                [whole((rows, hidden))] * 2 + [whole((rows, 4)), whole((8, hidden))]
                + [half_part] * 2,
                [low_hidden, low_hidden, tiny4, shape_of((8, hidden)), half_shape, half_shape],
                (g, slope, dw, g_stats, gain2, shift2, up_weight),
            )
            return w, du, st, h_sum, db_mine + to_core(db_other), b_core, a_core

        w, du, st, h_sum, db_pair, b_core, a_core = segment(hidden_back)
        if full:
            b_f1, b_m2, db_pair, b_core = meet(b_f1, b_m2, db_pair, b_core)
            st_near = to_batch(st, 2)
            st_near, dy_m2, b_m2, st = meet(st_near, dy_m2, b_m2, st)
            dy_f2, b_f2, st_six = outward(dy_m2), outward(b_m2), to_batch(st, 6)
        db_cross = to_y(db_pair)

        def far_pass(order, b_src, d_src, starts, lower, stats_in, own, wait=()):
            size = len(starts) * rows
            cols = [
                pl.BlockSpec((rows, block), lambda i, m: (0, m[2])),
                pl.BlockSpec((rows, block), lambda i, m: (0, m[2] ^ 1)),
            ] * 2
            near_tile = pl.BlockSpec((2 * block + 8, span), rolled(1))
            fresh = own[0].dtype == bf16
            if fresh:
                w_own, du_own, sum_own, b_own, d_own = own
                tail = (w_own, du_own, sum_own, b_own, b_own, d_own, d_own)
                specs = [many, many, sum_tile] + cols
            else:
                tail, specs = tuple(own), [tile, tile, near_tile]
            count = 4 * len(starts)
            sources = (*b_src, *d_src)
            return order.run(
                functools.partial(far_kernel, starts, lower, fresh),
                (chunks,),
                [pl.BlockSpec(memory_space=pl.ANY)] * len(sources)
                + [whole((rows, 4))] * len(stats_in)
                + [tall, wide, wide, wide, flat]
                + specs,
                [tile, tile, near_tile],
                [shape_of((block, hidden))] * 2 + [shape_of((2 * block + 8, hidden))],
                (*sources, *stats_in, up_weight, bias2, gain2, shift2, down_weight, *tail),
                [pltpu.VMEM((size, D), bf16)] * 2
                + [pltpu.VMEM((size, 4), f32), pltpu.VMEM((count, half, D), f32),
                   pltpu.SemaphoreType.DMA((count,))],
                wait=wait,
            )

        early = Order(meta, COVER)
        if full:
            sums = far_pass(
                early, [b_e1, b_core], [dy_e1, dy_core], (((0, 0), (1, 0)),), 0,
                (st_near, st_near), (w, du, h_sum, b, dyl),
            )
        dh_mine, d_sums, *dh_sent = early.run(
            functools.partial(norm2_kernel, nb),
            (tiles,),
            [half_tile] * 5 + [whole((8, D)), row_spec],
            [dh_tile, whole((8, D))]
            + [pl.BlockSpec((half // tiles, 2 * block), rolled(0))] * sends,
            [dh_shape, shape_of((8, D))] + [shape_of((half, 2 * block))] * sends,
            (db_pair, db_cross, h1, dy, branch, vecs, line(norm2_gain)),
        )
        if full:
            st_six, dy_f2, dh_mine, dh_sent, st = meet(st_six, dy_f2, dh_mine, dh_sent, st)
            st_far = (st_six, to_batch(st, 4))

        def attention_back():
            order = Order(meta)
            dh_other = to_core(dh_mine)
            a_late = [to_core(a_got[0]), to_core(a_got[2])] if full else ()
            dm, dv, h_sums, dhl = order.run(
                functools.partial(attend_back_kernel, attn_width),
                (quads,),
                [dh_spec, dh_spec, wide_spec, whole((rows, 2)), whole((heads, HD)),
                 whole((heads, HD)), whole((width, D)), quad, quad, quad, probs_spec, table_spec],
                [whole((rows, 2 * width))] * 2 + [whole((8, width)), whole((rows, D))],
                [shape_of((rows, 2 * width))] * 2 + [shape_of((8, width)), low_rows],
                (dh_mine, dh_other, o, stats, sub1_gain, sub1_shift, out_weight, q, k, v, probs,
                 table),
                [pltpu.VMEM((rows, width), bf16)],
            )
            return dm, dv, h_sums, dhl, a_late

        dm, dv, h_sums, dhl, a_late = segment(attention_back)
        main = Order(meta, COVER)
        if full:
            b_f2, st_far, dm, dv, dh_sent = meet(b_f2, st_far, dm, dv, dh_sent)
            dm_x, dm_z = to_batch(dm, 1), to_batch(dm, 2)
            dh_got = [None, to_batch(dh_sent[1], 2), None]

        both = pl.BlockSpec((rows, span), rolled(1))

        def prepare():
            order = Order(meta)
            packed = ()
            if full:
                far = order.run(
                    pack_kernel,
                    (1,),
                    [pl.BlockSpec(memory_space=pl.ANY)] * 8,
                    pl.BlockSpec(memory_space=pl.ANY),
                    shape_of((2 * rows, D)),
                    (b_m1, b_f1, b_m2, b_f2, dy_m1, dy_f1, dy_m2, dy_f2),
                    [pltpu.VMEM((4, half, D), f32), pltpu.SemaphoreType.DMA((8,))],
                )
                packed = [far, to_core(far)]
            tail_mine, tail_other = order.run(
                tail_kernel,
                (parts,),
                [whole((rows, 2 * width)), pl.BlockSpec((rows, width), lambda i, *_: (0, 0)),
                 pl.BlockSpec((3, span, width), lambda i, *_: (0, i, 0)),
                 whole((rows, hidden)), pl.BlockSpec((hidden, span), rolled(1))],
                [both] * 2,
                [shape_of((rows, D))] * 2,
                (dm, dv, weight, w, down_weight),
                [pltpu.VMEM((rows, 3 * width), bf16)],
            )
            return packed, tail_mine + to_core(tail_other)

        packed, da_pair = segment(prepare)
        if full:
            dm_x, dm_z, dh_got[1], packed, dv, dh_sent, da_pair = meet(
                dm_x, dm_z, dh_got[1], packed, dv, dh_sent, da_pair
            )
            dv_x = to_batch(dv, 1)
            dm_d = to_batch(dm_x, 2)
            dh_got[0], dh_got[2] = to_batch(dh_sent[0], 1), to_batch(dh_sent[2], 3)
            da_cross = to_y(da_pair)
            sums = far_pass(
                main, packed, packed, (((0, 0), (1, 0)), ((0, half), (1, half))), rows,
                (st_far[0], st_far[1], st_far[1], st_far[0]), sums,
            )

        if full:
            dv_x, dm_d, dh_got, sums, dm, dv = meet(dv_x, dm_d, dh_got, sums, dm, dv)
            near_got, dv_z, dv_d = to_batch(sums[2], 1), to_batch(dv, 2), to_batch(dv_x, 2)
            cut = 2 * width
            a_join = [*a_got, a_late[0], *a_core, a_late[1]]

            def square(part, lefts, sides):
                def piece(array, s):
                    at = s if array.shape[0] > half else 0
                    return pl.BlockSpec((half, 2 * block), lambda i, *_: (at, 0))

                specs = []
                for _, got in lefts:
                    specs += [whole((rows, D))] + [piece(got[i], i % 3) for i in range(6)]
                lists = [array for own, got in lefts for array in (own, *got)]
                return main.run(
                    functools.partial(square_kernel, nb, part),
                    (1,),
                    specs + [whole((rows, cut))] * 4,
                    [whole((block, cut))] * 2,
                    [shape_of((block, cut))] * 2,
                    (*lists, *sides),
                    [pltpu.VMEM((4 * rows, 2 * block), bf16)] * len(lefts)
                    + [pltpu.VMEM((4 * rows, cut), bf16)],
                )

            one_own, one_mirror = square(0, [(a, a_join)], [dm, dm_x, dm_z, dm_d])
            one_got = to_batch(one_mirror, 4)
        else:
            da_cross = to_y(da_pair)
        row_tile = pl.BlockSpec((half // tiles, D), rolled(0))
        row_mod = pl.BlockSpec((half // tiles, D), lambda i, *_: (i % tiles, 0))
        last = main.last

        def input_norm_back():
            order = Order(meta)
            order.last = last
            joined = ()
            if full:
                dh_all = Order(meta).run(
                    join_kernel,
                    (1,),
                    [pl.BlockSpec(memory_space=pl.ANY)] * 3,
                    pl.BlockSpec(memory_space=pl.ANY),
                    shape_of((3 * half, 2 * block)),
                    dh_got,
                    [pltpu.VMEM((3, half, 2 * block), f32), pltpu.SemaphoreType.DMA((6,))],
                )
                joined = [dh_all] * 3 + [to_core(dh_all)] * 3
            outs = order.run(
                norm1_kernel,
                (2 * tiles,),
                [row_tile, row_tile, row_mod,
                 pl.BlockSpec((half // tiles, D), lambda i, m: (m[0] * tiles + i % tiles, 0)),
                 pl.BlockSpec((half // tiles, D + 128), lambda i, *_: (i % tiles, 0)), row_spec,
                 row_spec, whole((8, D))],
                [row_tile, whole((8, D))],
                [shape_of((rows, D)), shape_of((8, D))],
                (da_pair, da_cross, h1, tokens, dh_mine, line(norm1_gain),
                 line(down_bias), d_sums),
            )
            return outs, joined

        (mine, d_sums), dh_join = segment(input_norm_back)
        if full:
            dv_z, dv_d, dh_join = meet(dv_z, dv_d, dh_join)
            two_own, two_mirror = square(
                1, [(a, a_join), (dhl, dh_join)], [dv, dv_x, dv_z, dv_d]
            )
            two_got = to_batch(two_mirror, 4)

        def place():
            order = Order(meta)
            sums = d_sums + to_core(d_sums)
            other = to_core(mine)
            outs = [
                order.run(
                    place_kernel,
                    (2 * tiles,),
                    [pl.BlockSpec((half // tiles, D), functools.partial(
                        lambda first, i, *_: (first + i % tiles, 0), first))] * 2,
                    row_tile,
                    low_rows,
                    (mine, other),
                )
                for first in (tiles, 0)
            ]
            return (*outs, sums)

        result, tokens_grad, d_sums = segment(place)

        def small_sums():
            comb = jnp.concatenate([d_sums, h_sums], axis=1)
            for s in (1, 2):
                comb = comb + to_batch(comb, s)
            return comb

        lanes = hidden // 128
        per = 128 // nb
        if not full:

            def scatter(value, axis):
                return lax.psum_scatter(value, "batch", scatter_dimension=axis, tiled=True)

            d_sums = scatter(d_sums, 1)
            h_sums = lax.psum(h_sums, "batch")
            h_parts = scatter(h_sum[:3].reshape(3, lanes, 128), 2)
            dm_low = jnp.concatenate([dm, dv[:, :width]], axis=1).astype(bf16)
            z = dv[:, width:]
            grad_qkv = scatter(
                jnp.stack([mm_tn(a, dm_low[:, j * width : (j + 1) * width]) for j in range(3)], 1), 0
            )
            grad_out = scatter(mm_tn(z.astype(bf16), dhl), 1)
            grad_up = scatter(mm_tn(b, du), 0)
            grad_down = scatter(mm_tn(w, dyl), 1)
        else:
            near_got, sums, d_sums = meet(near_got, sums, d_sums)
            h_parts = (sums[2][2 * block :] + near_got[2 * block :])[:3]
            h_parts = lax.dynamic_slice_in_dim(
                h_parts.reshape(3, lanes, 128), index * per, per, 2
            )
            strip = hidden // 4
            grad_up, grad_down = main.run(
                final_hidden_kernel,
                (4,),
                [pl.BlockSpec((block, strip), rolled(1))] * 3
                + [pl.BlockSpec((block, strip), lambda i, *_: (1, i))],
                [pl.BlockSpec((block, strip), rolled(1)), pl.BlockSpec((strip, block), rolled(0))],
                [shape_of((block, hidden)), shape_of((hidden, block))],
                (sums[0], near_got, sums[1], near_got),
            )
            d_sums, grad_up = meet(d_sums, grad_up)
            comb = segment(small_sums)
            comb_far = to_batch(comb, 4)
            main.last = [comb]
            grad_qkv, grad_out = main.run(
                final_square_kernel,
                (1,),
                [whole((block, cut))] * 4,
                [whole((3, block, width)), whole((width, block))],
                [shape_of((3, block, width)), shape_of((width, block))],
                (one_own, one_got, two_own, two_got),
            )
            comb = comb + comb_far
            d_sums = lax.dynamic_slice_in_dim(comb, index * block, block, 1)
            h_sums = comb[:, D:]
            grad_qkv = jnp.transpose(grad_qkv, (1, 0, 2))
        per = HD // nb

        def own_part(value, shape):
            return lax.dynamic_slice_in_dim(value.reshape(shape), index * per, per, len(shape) - 1)

        return (
            result,
            tokens_grad,
            d_sums[4],
            d_sums[5],
            grad_qkv,
            own_part(h_sums[2:5], (3, heads, HD)),
            own_part(h_sums[0], (heads, HD)),
            own_part(h_sums[1], (heads, HD)),
            grad_out,
            d_sums[2],
            d_sums[0],
            d_sums[1],
            grad_up,
            h_parts[0],
            h_parts[1],
            h_parts[2],
            grad_down,
            d_sums[3],
        )

    return local


def solution(mesh):
    in_specs = (
        P("batch", None),
        P("batch"),
        P("batch", None),
        P(),
        P(),
        P(None, None, "mp"),
        P(None, "mp", None),
        P("mp", None),
        P("mp", None),
        P("mp", None),
        P(),
        P(),
        P(),
        P(None, "mp"),
        P("mp"),
        P("mp"),
        P("mp"),
        P("mp", None),
        P(),
    )
    out_specs = (
        P("batch", None),
        P("batch", None),
        P("batch"),
        P("batch"),
        P("batch", None, "mp"),
        P(None, "mp", "batch"),
        P("mp", "batch"),
        P("mp", "batch"),
        P("mp", "batch"),
        P("batch"),
        P("batch"),
        P("batch"),
        P("batch", "mp"),
        P("mp", "batch"),
        P("mp", "batch"),
        P("mp", "batch"),
        P("mp", "batch"),
        P("batch"),
    )
    local = make_local(mesh.shape["batch"], mesh.shape["mp"])
    return jax.shard_map(local, mesh=mesh, in_specs=in_specs, out_specs=out_specs, check_vma=False)
```

```python
import functools
import math

import jax
import jax.numpy as jnp
import numpy as np
from jax import lax
from jax.experimental import pallas as pl
from jax.experimental.pallas import tpu as pltpu
from jax.sharding import PartitionSpec as P

HD = 64
QUAD = 4 * HD
PAIR = 2 * HD

norm_eps = 1e-05
rope_base = 10000.0
xpos_base = 512.0
masked_score = -1e30
root_half = 2.0**-0.5
density_scale = 1.0 / math.sqrt(2.0 * math.pi)
f32 = jnp.float32
bf16 = jnp.bfloat16
MIB = 1 << 20
COVER = 10**11


def dot(a, b, dims):
    return lax.dot_general(a, b, (dims, ((), ())), preferred_element_type=f32)


def mm(a, b):
    return dot(a, b, ((1,), (0,)))


def mm_nt(a, b):
    return dot(a, b, ((1,), (1,)))


def mm_tn(a, b):
    return dot(a, b, ((0,), (0,)))


def row_mean(value):
    return jnp.mean(value, axis=-1, keepdims=True)


def row_sum(value):
    return jnp.sum(value, axis=-1, keepdims=True)


def unit_rows(value):
    center = value - row_mean(value)
    inverse = lax.rsqrt(row_mean(center * center) + norm_eps)
    return center * inverse, inverse


def unit_back(grad, unit, inverse, gain):
    scaled = grad * gain
    return inverse * (scaled - row_mean(scaled) - unit * row_mean(scaled * unit))


def turn_tables(count):
    half = HD // 2
    places = np.arange(count, dtype=np.float64)[:, None]
    pair = np.arange(half, dtype=np.float64)[None, :]
    angles = places * rope_base ** (-2.0 * pair / HD)
    zeta = (2.0 * pair + 0.4 * HD) / (1.4 * HD)
    factor = zeta ** ((places - count // 2) / xpos_base)
    tables = []
    for scale in (factor, 1.0 / factor):
        tables.append(np.tile(np.cos(angles) * scale, (1, 4)))
        tables.append(np.tile(np.concatenate([-np.sin(angles), np.sin(angles)], 1), (1, 2))
                      * np.tile(scale, (1, 4)))
    return np.stack(tables).astype(np.float32)


def half_swap(value):
    lane = lax.broadcasted_iota(jnp.int32, value.shape, 1)
    return jnp.where(
        (lane & 32) == 0,
        pltpu.roll(value, value.shape[1] - 32, 1),
        pltpu.roll(value, 32, 1),
    )


def whole(shape):
    return pl.BlockSpec(shape, lambda *_: (0,) * len(shape))


def shape_of(shape, dtype=f32):
    return jax.ShapeDtypeStruct(shape, dtype)


def call(body, grid, ins, outs, shapes, scratch=(), tokens=0, cover=0):
    count = len(ins)

    def kernel(meta, *refs):
        body(meta, *refs[:count], *refs[count + tokens :])

    return pl.pallas_call(
        kernel,
        grid_spec=pltpu.PrefetchScalarGridSpec(
            num_scalar_prefetch=1,
            grid=grid,
            in_specs=list(ins) + [pl.BlockSpec(memory_space=pl.ANY)] * tokens,
            out_specs=outs,
            scratch_shapes=list(scratch),
        ),
        out_shape=shapes,
        compiler_params=pltpu.CompilerParams(
            dimension_semantics=("arbitrary",) * len(grid), vmem_limit_bytes=64 * MIB
        ),
        cost_estimate=pl.CostEstimate(flops=cover, bytes_accessed=0, transcendentals=0)
        if cover
        else None,
    )


class Order:
    def __init__(self, meta, cover=0):
        self.meta = meta
        self.last = []
        self.cover = cover

    def run(self, body, grid, ins, outs, shapes, args, scratch=(), wait=()):
        extra = list(wait) + self.last
        made = call(body, grid, ins, outs, shapes, scratch, len(extra), self.cover)(
            self.meta, *args, *extra
        )
        self.last = [made[0] if isinstance(made, (list, tuple)) else made]
        return made


def half_at(meta, which, half):
    return pl.ds(pl.multiple_of(((meta[0] + which) % 2) * half, half), half)


def spread(ref, count, first=0):
    return jnp.concatenate([ref[pl.ds(first + i, 1), :] for i in range(count)], axis=1)


def mask_kernel(meta, cot, mine):
    size = mine.shape[0]
    first = (meta[0] * pl.num_programs(0) + pl.program_id(0)) * size
    place = first + lax.broadcasted_iota(jnp.int32, (size, 1), 0)
    mine[...] = cot[...].astype(f32) * jnp.where(place < meta[1], 1.0, 0.0)


def send_pieces(meta, value, outs, block):
    for s, out in enumerate(outs):
        at = meta[2] ^ (s + 1)
        for part, where in ((0, at), (1, at ^ 4)):
            cols = pl.ds(pl.multiple_of(where * block, block), block)
            out[:, part * block : (part + 1) * block] = value[:, cols].astype(f32)


def flip_rows(value, half):
    return jnp.concatenate(
        [
            value[(i ^ 1) * half : ((i ^ 1) + 1) * half]
            for i in range(value.shape[0] // half)
        ],
        axis=0,
    )


def join_two(one, two, count):
    mean = 0.5 * (one[0] + two[0])
    gap = one[0] - two[0]
    joined = [mean, one[1] + two[1] + (0.5 * count) * gap * gap]
    if len(one) > 2:
        joined += [
            one[2] + two[2],
            one[3] + two[3] + one[2] * (one[0] - mean) + two[2] * (two[0] - mean),
        ]
    return joined


def join_all(ref, odd, count):
    cols = []
    for i in range(ref.shape[0]):
        value = ref[i]
        half = value.shape[0] // 2
        value = jnp.where(odd == i % 2, value, flip_rows(value, half))
        cols.append([value[:, c : c + 1] for c in range(4)])
    while len(cols) > 1:
        cols = [join_two(cols[i], cols[i + 1], count) for i in range(0, len(cols), 2)]
        count *= 2
    return cols[0]


def diagonal(count):
    return lax.broadcasted_iota(jnp.int32, (count, count), 0) == lax.broadcasted_iota(
        jnp.int32, (count, count), 1
    )


def as_row(column):
    return jnp.sum(jnp.where(diagonal(column.shape[0]), column, 0.0), axis=0, keepdims=True)


def as_column(row):
    return row_sum(jnp.where(diagonal(row.shape[1]), row, 0.0))


def attend_kernel(nb, meta, tok, gain, shift, weight, bias, sub_gain, sub_shift, out_w, table,
                  a_out, q_out, k_out, v_out, p_out, o_out, y_mine, y_other,
                  *rest):
    sends, (a_low, o_all) = rest[:-2], rest[-2:]
    rows, width = o_all.shape
    half = rows // 2
    step = pl.program_id(0)
    places = lax.broadcasted_iota(jnp.int32, (rows, 1), 0) ^ (meta[0] * half)
    keys = lax.broadcasted_iota(jnp.int32, (1, rows), 1) ^ (meta[0] * half)
    allowed = (keys <= places) & (keys < meta[1])

    @pl.when(step == 0)
    def _():
        for which in range(2):
            unit, _ = unit_rows(tok[half_at(meta, which, half), :].astype(f32))
            wide = unit * gain[...] + shift[...]
            a_low[which * half : (which + 1) * half, :] = wide.astype(bf16)
        a_out[...] = a_low[...]
        if sends:
            send_pieces(meta, a_low.at[0:half, :], sends, tok.shape[1] // nb)

    turned = []
    for j in range(3):
        m = mm(a_low[...], weight[j])
        m = m + jnp.concatenate(
            [bias[j, pl.ds(step * 4 + i, 1), :] for i in range(4)], axis=1
        )
        if j < 2:
            flipped = half_swap(m)
            parts = []
            for which in range(2):
                at = half_at(meta, which, half)
                here = slice(which * half, (which + 1) * half)
                c = jnp.concatenate([table[2 * j, at, :]] * 2, axis=1)
                s = jnp.concatenate([table[2 * j + 1, at, :]] * 2, axis=1)
                parts.append(m[here] * c + flipped[here] * s)
            m = jnp.concatenate(parts, axis=0)
        turned.append(m.astype(bf16))
    q, k, v = turned
    q = q * jnp.asarray(1.0 / math.sqrt(HD), bf16)
    q_out[...] = q
    k_out[...] = k
    v_out[...] = v
    lane = lax.broadcasted_iota(jnp.int32, (1, PAIR), 1)
    for p in range(2):
        here = slice(p * PAIR, (p + 1) * PAIR)
        total = None
        for h in range(2):
            mask = (lane // HD) == h
            scores = mm_nt(jnp.where(mask, q[:, here], jnp.zeros_like(q[:, here])), k[:, here])
            scores = jnp.where(allowed, scores, masked_score)
            weights = jnp.exp(scores - jnp.max(scores, axis=-1, keepdims=True))
            probs = weights * (1.0 / row_sum(weights))
            p_out[p * 2 + h] = probs
            part = mm(
                probs.astype(bf16), jnp.where(mask, v[:, here], jnp.zeros_like(v[:, here]))
            )
            total = part if total is None else total + part
        o_all[:, pl.ds(pl.multiple_of(step * QUAD + p * PAIR, PAIR), PAIR)] = total

    @pl.when(step == pl.num_programs(0) - 1)
    def _():
        o = o_all[...]
        o_out[...] = o
        mean = row_mean(o)
        center = o - mean
        stat_rows = jnp.concatenate([as_row(mean), as_row(row_sum(center * center))], axis=0)
        heads = width // HD
        gain_row, shift_row = spread(sub_gain, heads), spread(sub_shift, heads)
        pieces = []
        for row in (gain_row, shift_row):
            for _ in range(3):
                low = row.astype(bf16)
                pieces.append(low)
                row = row - low.astype(f32)
        vecs = mm(jnp.concatenate(pieces + [jnp.zeros((2, width), bf16)], axis=0), out_w[...])
        gain_out = vecs[0:1] + vecs[1:2] + vecs[2:3]
        shift_out = vecs[3:4] + vecs[4:5] + vecs[5:6]
        extra = jnp.concatenate([gain_out, shift_out, jnp.zeros((6, vecs.shape[1]), f32)], axis=0)
        low = (center * gain_row).astype(bf16)
        for which, out in ((1, y_other), (0, y_mine)):
            here = slice(which * half, (which + 1) * half)
            out[0:half, :] = mm(low[here], out_w[...]) + mean[here] * gain_out
            out[half : half + 8, :] = extra
            for p in range(2):
                out[half + 2 + 2 * p : half + 4 + 2 * p, 0:rows] = jnp.where(
                    meta[0] == p, stat_rows, jnp.zeros_like(stat_rows)
                )


def join_rows(refs, odd, count):
    cols = []
    for ref in refs:
        half = ref.shape[1] // 2
        for p in range(2):
            rows = ref[2 + 2 * p : 4 + 2 * p, :]
            swapped = jnp.concatenate([rows[:, half:], rows[:, :half]], axis=1)
            rows = jnp.where(odd == p, rows, swapped)
            cols.append([rows[0:1], rows[1:2]])
    near = join_two(cols[0], cols[1], count)
    far = join_two(cols[2], cols[3], count)
    return join_two(near, far, 2 * count)


def middle_kernel(attn_width, meta, one, two, one_extra, two_extra, tok, bias, gain, shift,
                   h_out, branch_out, b_out, vec_out, stats):
    size = h_out.shape[0]
    step = pl.program_id(0)

    @pl.when(step == 0)
    def _():
        rows = stats.shape[0]
        extras = (one_extra.at[:, 0:rows], two_extra.at[:, 0:rows])
        mean, m2 = join_rows(extras, meta[0], attn_width // 4)
        inverse = lax.rsqrt(m2 * (1.0 / attn_width) + norm_eps)
        stats[...] = jnp.concatenate([as_column(mean), as_column(inverse)], axis=1)
        vec_out[...] = one_extra[...] + two_extra[...]

    at = pl.ds(pl.multiple_of(step * size, size), size)
    branch = stats[at, 1:2] * ((one[...] + two[...]) - stats[at, 0:1] * vec_out[0:1, :])
    branch_out[...] = branch
    h1 = tok[...].astype(f32) + (branch + vec_out[1:2, :]) + bias[...]
    h_out[...] = h1
    unit, _ = unit_rows(h1)
    b_out[...] = unit * gain[...] + shift[...]


def dw_kernel(meta, cot, weight, out, low):
    half = cot.shape[0] // 2

    @pl.when(pl.program_id(0) == 0)
    def _():
        for which in range(2):
            first = ((meta[0] + which) % 2) * half
            place = first + lax.broadcasted_iota(jnp.int32, (half, 1), 0)
            rows = cot[half_at(meta, which, half), :]
            low[which * half : (which + 1) * half, :] = jnp.where(
                place < meta[1], rows, jnp.zeros_like(rows)
            )

    out[...] = mm_nt(low[...], weight[...]).astype(bf16)


def first_kernel(meta, mine, other, weight, bias, gain, dw, g_out, slope_out, stat_out, low,
                 mean_s, m2_s, s1_s, s2_s):
    half = mine.shape[0]
    step = pl.program_id(0)
    span = weight.shape[1]

    @pl.when(step == 0)
    def _():
        low[0:half, :] = mine[...].astype(bf16)
        low[half:, :] = other[...].astype(bf16)
        for ref in (mean_s, m2_s, s1_s, s2_s):
            ref[...] = jnp.zeros_like(ref)

    done = step.astype(f32)
    share = 1.0 / (done + 1.0)
    u = mm(low[...], weight[...]) + bias[...]
    cdf = 0.5 + 0.5 * lax.erf(u * root_half)
    density = jnp.exp(-0.5 * (u * u)) * density_scale
    g = u * cdf
    slope_out[...] = (cdf + u * density).astype(bf16)
    g_out[...] = g.astype(bf16)
    scaled = dw[...].astype(f32) * gain[...]
    mean_c = row_mean(g)
    center = g - mean_c
    s1_c = row_sum(scaled)
    s2_c = row_sum(scaled * center)
    gap = mean_c - mean_s[...]
    mean_new = mean_s[...] + gap * share
    m2_s[...] += row_sum(center * center) + gap * gap * (span * done * share)
    s2_s[...] += s2_c + s1_s[...] * (mean_s[...] - mean_new) + s1_c * (mean_c - mean_new)
    s1_s[...] += s1_c
    mean_s[...] = mean_new

    @pl.when(step == pl.num_programs(0) - 1)
    def _():
        stat_out[...] = jnp.concatenate([mean_s[...], m2_s[...], s1_s[...], s2_s[...]], axis=1)


def hidden_stats(ref, odd, out, count, ff_width):
    mean, m2, s1, s2 = join_all(ref, odd, count)
    inverse = lax.rsqrt(m2 * (1.0 / ff_width) + norm_eps)
    out[...] = jnp.concatenate(
        [mean, inverse, s1 * (1.0 / ff_width), inverse * s2 * (1.0 / ff_width)], axis=1
    )


def hidden_rows(g, slope, dw, stats, gain, shift):
    inverse = stats[:, 1:2]
    unit = (g.astype(f32) - stats[:, 0:1]) * inverse
    w = (unit * gain + shift).astype(bf16)
    dw = dw.astype(f32)
    dg = inverse * (dw * gain - stats[:, 2:3] - unit * stats[:, 3:4])
    return w, (dg * slope.astype(f32)).astype(bf16), dw * unit, dw


def back_kernel(ff_width, span, meta, g, slope, dw, parts, gain, shift, weight, w_out, du_out, stats,
                sum_out, db_mine, db_other):
    half = db_mine.shape[0]

    @pl.when(pl.program_id(0) == 0)
    def _():
        hidden_stats(parts, meta[0], stats, ff_width // parts.shape[0], ff_width)
        for c in range(g.shape[1] // span):
            at = slice(c * span, (c + 1) * span)
            w, du, gain_part, dw_wide = hidden_rows(
                g[:, at], slope[:, at], dw[:, at], stats[...], gain[:, at], shift[:, at]
            )
            w_out[:, at] = w
            du_out[:, at] = du
            sum_out[:, at] = hidden_sums(du, gain_part, dw_wide)

    part = mm_nt(du_out[...], weight[...])
    db_mine[...] = part[0:half, :]
    db_other[...] = part[half:, :]


def hidden_sums(du, gain_part, dw_wide):
    return jnp.concatenate(
        [
            jnp.sum(du.astype(f32), axis=0, keepdims=True),
            jnp.sum(gain_part, axis=0, keepdims=True),
            jnp.sum(dw_wide, axis=0, keepdims=True),
            jnp.zeros((5, du.shape[1]), f32),
        ],
        axis=0,
    )


def pack_kernel(meta, *refs):
    sources, (out, buffer, sems) = refs[:8], refs[8:]
    where = meta[2] // 2
    inner = (where == 1) | (where == 2)
    half = buffer.shape[1]

    def loads(first):
        return [
            pltpu.make_async_copy(sources[2 * i + first], buffer.at[i], sems.at[i])
            for i in range(4)
        ]

    @pl.when(inner)
    def _():
        for copy in loads(0):
            copy.start()

    @pl.when(jnp.logical_not(inner))
    def _():
        for copy in loads(1):
            copy.start()

    stores = []
    for i, copy in enumerate(loads(0)):
        copy.wait()
        store = pltpu.make_async_copy(
            buffer.at[i], out.at[i * half : (i + 1) * half, :], sems.at[4 + i]
        )
        store.start()
        stores.append(store)
    for store in stores:
        store.wait()


def far_kernel(starts, lower, own, meta, *refs):
    groups = len(starts)
    count = 1 + max(source for pair in starts for source, _ in pair)
    b_src, d_src, refs = refs[:count], refs[count : 2 * count], refs[2 * count :]
    stat_refs, rest = refs[: 2 * groups], refs[2 * groups :]
    up_w, up_b, gain, shift, down_w = rest[:5]
    rest = rest[5:]
    if own:
        w_own, du_own, sum_own, *cols = rest[:7]
        rest = rest[7:]
        ins = ()
    else:
        ins, rest = rest[:3], rest[3:]
    (up_out, down_out, near_out), (b_low, d_low, stats, buffer, sem) = rest[:3], rest[3:]
    half = buffer.shape[1]
    rows = 2 * half
    block = up_out.shape[0]
    where = meta[2] // 2
    inner = (where == 1) | (where == 2)
    mine = pl.ds(pl.multiple_of(meta[2] * block, block), block)
    near = pl.ds(pl.multiple_of((meta[2] ^ 1) * block, block), block)

    @pl.when(pl.program_id(0) == 0)
    def _():
        copies = []
        for n, pair in enumerate(starts):
            for k, (refs_k, low) in enumerate(((b_src, b_low), (d_src, d_low))):
                for i, (source, first) in enumerate(pair):
                    slot = 4 * n + 2 * k + i
                    copy = pltpu.make_async_copy(
                        refs_k[source].at[first + k * lower : first + k * lower + half, :], buffer.at[slot], sem.at[slot]
                    )
                    copy.start()
                    copies.append((copy, low, n * rows + i * half, slot))
        for n in range(groups):
            stats[n * rows : (n + 1) * rows, :] = jnp.where(
                inner, stat_refs[2 * n][...], stat_refs[2 * n + 1][...]
            )
        for copy, low, at, slot in copies:
            copy.wait()
            low[at : at + half, :] = buffer[slot].astype(bf16)

    for n in range(groups):
        at = slice(n * rows, (n + 1) * rows)
        u = mm(b_low[at, :], up_w[...]) + up_b[...]
        cdf = 0.5 + 0.5 * lax.erf(u * root_half)
        density = jnp.exp(-0.5 * (u * u)) * density_scale
        dw = mm_nt(d_low[at, :], down_w[...])
        w, du, gain_part, dw_wide = hidden_rows(
            u * cdf, cdf + u * density, dw, stats[at, :], gain[...], shift[...]
        )
        terms = [
            mm_tn(b_low[at, mine], du),
            mm_tn(d_low[at, mine], w),
            mm_tn(b_low[at, near], du),
            mm_tn(d_low[at, near], w),
            hidden_sums(du, gain_part, dw_wide),
        ]
        totals = terms if n == 0 else [t + s for t, s in zip(totals, terms)]
    if own:
        terms = [
            mm_tn(cols[0][...], du_own[...]),
            mm_tn(cols[2][...], w_own[...]),
            mm_tn(cols[1][...], du_own[...]),
            mm_tn(cols[3][...], w_own[...]),
            sum_own[...],
        ]
    else:
        low, high = ins[2][0:block, :], ins[2][block : 2 * block, :]
        terms = [ins[0][...], ins[1][...], low, high, ins[2][2 * block :, :]]
    totals = [t + s for t, s in zip(totals, terms)]
    up_out[...] = totals[0]
    down_out[...] = totals[1]
    near_out[0:block, :] = totals[2]
    near_out[block : 2 * block, :] = totals[3]
    near_out[2 * block :, :] = totals[4]


def norm2_kernel(nb, meta, one, two, h1, dy, branch, vecs, gain, dh_out, sum_out, *sends):
    size, full = h1.shape
    db = one[...] + two[...]
    unit, inverse = unit_rows(h1[...])
    dh1 = dy[...] + unit_back(db, unit, inverse, gain[...])
    low = dh1.astype(bf16).astype(f32)
    dh_out[:, 0:full] = dh1
    lane = lax.broadcasted_iota(jnp.int32, (size, 128), 1)
    dh_out[:, full : full + 128] = jnp.where(
        lane == 0, row_sum(low * vecs[0:1]), row_sum(low * branch[...])
    )
    sums = jnp.concatenate(
        [
            jnp.sum(db * unit, axis=0, keepdims=True),
            jnp.sum(db, axis=0, keepdims=True),
            jnp.sum(dh1, axis=0, keepdims=True),
            jnp.sum(dy[...], axis=0, keepdims=True),
            jnp.zeros((4, full), f32),
        ],
        axis=0,
    )

    @pl.when(pl.program_id(0) == 0)
    def _():
        sum_out[...] = sums

    @pl.when(pl.program_id(0) > 0)
    def _():
        sum_out[...] += sums
    if sends:
        send_pieces(meta, dh_out, sends, full // nb)


def attend_back_kernel(attn_width, meta, dh_mine, dh_other, o_all, stats, sub_gain, sub_shift, out_w, q_all,
                       k_all, v_all, probs_all, table, dm_out, z_out, sum_out, dhl_out, do_all):
    rows, width = o_all.shape
    half = rows // 2
    full = out_w.shape[1]
    heads = width // HD
    step = pl.program_id(0)

    @pl.when(step == 0)
    def _():
        gain_row = spread(sub_gain, heads)
        dhl = jnp.concatenate(
            [dh_mine[:, 0:full].astype(bf16), dh_other[:, 0:full].astype(bf16)], axis=0
        )
        dhl_out[...] = dhl
        sums = jnp.concatenate([dh_mine[:, full:], dh_other[:, full:]], axis=0)
        dz = mm_nt(dhl, out_w[...])
        inverse = stats[:, 1:2]
        unit = (o_all[...] - stats[:, 0:1]) * inverse
        do = inverse * (
            dz * gain_row
            - sums[:, 0:1] * (1.0 / attn_width)
            - unit * (sums[:, 1:2] * (1.0 / attn_width))
        )
        do_all[...] = do.astype(bf16)
        z_out[...] = unit * gain_row + spread(sub_shift, heads)
        sum_out[0:1, :] = jnp.sum(dz * unit, axis=0, keepdims=True)
        sum_out[1:2, :] = jnp.sum(dz, axis=0, keepdims=True)
        sum_out[5:8, :] = jnp.zeros((3, width), f32)

    quad = pl.ds(pl.multiple_of(step * QUAD, QUAD), QUAD)
    do = do_all[:, quad]
    q, k, v = q_all[...], k_all[...], v_all[...]
    lane = lax.broadcasted_iota(jnp.int32, (1, PAIR), 1)
    grads = [[], [], []]
    for p in range(2):
        here = slice(p * PAIR, (p + 1) * PAIR)
        total = [None] * 3
        for h in range(2):
            mask = (lane // HD) == h

            def only(value):
                return jnp.where(mask, value[:, here], jnp.zeros_like(value[:, here]))

            probs = probs_all[p * 2 + h]
            do_h = only(do)
            dprobs = mm_nt(do_h, v[:, here])
            inner = row_sum(probs * dprobs)
            dscores = (probs * (dprobs - inner)).astype(bf16)
            parts = (
                mm(dscores, only(k)),
                mm_tn(dscores, only(q)),
                mm_tn(probs.astype(bf16), do_h),
            )
            total = [part if t is None else t + part for t, part in zip(total, parts)]
        for j in range(3):
            grads[j].append(total[j])
    for j in range(3):
        grad = jnp.concatenate(grads[j], axis=1)
        if j == 0:
            grad = grad * (1.0 / math.sqrt(HD))
        if j < 2:
            flipped = half_swap(grad)
            parts = []
            for which in range(2):
                at = half_at(meta, which, half)
                here = slice(which * half, (which + 1) * half)
                c = jnp.concatenate([table[2 * j, at, :]] * 2, axis=1)
                s = jnp.concatenate([table[2 * j + 1, at, :]] * 2, axis=1)
                parts.append(grad[here] * c - flipped[here] * s)
            grad = jnp.concatenate(parts, axis=0)
        dm_out[:, pl.ds(pl.multiple_of(j * width + step * QUAD, QUAD), QUAD)] = grad
        sum_out[2 + j : 3 + j, quad] = jnp.sum(
            grad.astype(bf16).astype(f32), axis=0, keepdims=True
        )


def tail_kernel(meta, dm, weight, w, down_w, mine, other, low):
    half = mine.shape[0] // 2
    width = weight.shape[2]

    @pl.when(pl.program_id(0) == 0)
    def _():
        low[...] = dm[...].astype(bf16)

    total = mm_nt(low[:, 0:width], weight[0])
    for j in (1, 2):
        total = total + mm_nt(low[:, j * width : (j + 1) * width], weight[j])
    part = mm(w[...], down_w[...])
    mine[0:half, :] = total[0:half, :]
    mine[half:, :] = part[0:half, :]
    other[0:half, :] = total[half:, :]
    other[half:, :] = part[half:, :]


def norm1_kernel(meta, one, two, h1, tok, dh, gain, bias, sum_in, out, sum_out):
    full = out.shape[1]
    step = pl.program_id(0)
    total = one[...] + two[...]

    @pl.when(step == 0)
    def _():
        sum_out[...] = sum_in[...]

    @pl.when(step < pl.num_programs(0) // 2)
    def _():
        unit, inverse = unit_rows(tok[...].astype(f32))
        out[...] = dh[:, 0:full] + unit_back(total, unit, inverse, gain[...])
        sum_out[4:5, :] += jnp.sum(total * unit, axis=0, keepdims=True)
        sum_out[5:6, :] += jnp.sum(total, axis=0, keepdims=True)

    @pl.when(step >= pl.num_programs(0) // 2)
    def _():
        out[...] = h1[...] + total + bias[...]


def place_kernel(meta, mine, other, out):
    tiles = pl.num_programs(0) // 2
    local = (pl.program_id(0) // tiles) == meta[0]
    out[...] = jnp.where(local, mine[...], other[...]).astype(bf16)


def add_kernel(count, meta, *refs):
    total = refs[0][...]
    for ref in refs[1:count]:
        total = total + ref[...]
    refs[count][...] = total


def join_kernel(meta, *refs):
    pieces, (out, buffer, sems) = refs[:3], refs[3:]
    half = buffer.shape[1]
    loads = [pltpu.make_async_copy(pieces[i], buffer.at[i], sems.at[i]) for i in range(3)]
    for copy in loads:
        copy.start()
    stores = []
    for i, copy in enumerate(loads):
        copy.wait()
        store = pltpu.make_async_copy(
            buffer.at[i], out.at[i * half : (i + 1) * half, :], sems.at[3 + i]
        )
        store.start()
        stores.append(store)
    for store in stores:
        store.wait()


def square_kernel(nb, meta, own, *refs):
    mine, other, sides, (own_out, mirror_out, left, right) = refs[:3], refs[3:6], refs[6:10], refs[10:]
    rows, full = own.shape
    half, block = rows // 2, full // nb
    for part, at in ((0, meta[2]), (1, meta[2] ^ 4)):
        cols = pl.ds(pl.multiple_of(at * block, block), block)
        left[0:rows, part * block : (part + 1) * block] = own[:, cols]
    for s in range(3):
        here = rows * (s + 1)
        left[here : here + half, :] = mine[s][...].astype(bf16)
        left[here + half : here + rows, :] = other[s][...].astype(bf16)
    for s in range(4):
        right[rows * s : rows * (s + 1), :] = sides[s][...].astype(bf16)
    for out, part in ((mirror_out, block), (own_out, 0)):
        out[...] = mm_tn(left[:, part : part + block], right[...])


def final_square_kernel(meta, one_own, one_got, two_own, two_got, m_out, o_out):
    width = m_out.shape[2]
    for j in range(3):
        cols = slice(j * width, (j + 1) * width)
        m_out[j] = one_own[:, cols] + one_got[:, cols]
    o_out[...] = (two_own[...] + two_got[...]).T


def final_hidden_kernel(meta, up_own, up_got, down_own, down_got, up_out, down_out):
    up_out[...] = up_own[...] + up_got[...]
    down_out[...] = (down_own[...] + down_got[...]).T


def make_local(nb, nm):
    pair = [(i, i ^ 1) for i in range(nm)]
    cross = [(i, i ^ 2) for i in range(nm)]
    full = nb == 8
    middle_link = [(2, 4), (3, 5), (4, 2), (5, 3)]
    outward_link = [(2, 0), (3, 1), (4, 6), (5, 7)]

    def to_core(value):
        return lax.ppermute(value, "mp", pair)

    def to_y(value):
        return lax.ppermute(value, "mp", cross)

    def to_batch(value, s):
        return lax.ppermute(value, "batch", [(i, i ^ s) for i in range(nb)])

    def to_middle(value):
        return lax.ppermute(value, "batch", middle_link)

    def outward(value):
        return lax.ppermute(value, "batch", outward_link)

    def local(
        tokens,
        lengths,
        cotangent,
        norm1_gain,
        norm1_shift,
        qkv_weight,
        qkv_bias,
        sub1_gain,
        sub1_shift,
        out_weight,
        out_bias,
        norm2_gain,
        norm2_shift,
        up_weight,
        up_bias,
        sub2_gain,
        sub2_shift,
        down_weight,
        down_bias,
    ):
        rows, D = tokens.shape
        half = rows // 2
        width = out_weight.shape[0]
        heads = width // HD
        hidden = up_weight.shape[1]
        attn_width = width * nm
        ff_width = hidden * nm
        block = D // nb
        span = 512
        chunks = hidden // span
        parts = D // span
        quads = heads // 4
        sends = 3 if full else 0
        tiles = 4
        index = lax.axis_index("batch")
        meta = jnp.stack([lax.axis_index("mp") % 2, lengths[0], index]).astype(jnp.int32)
        always = lengths[0] >= 0
        table = jnp.asarray(turn_tables(rows))
        weight = jnp.transpose(qkv_weight, (1, 0, 2))

        def segment(stage):
            def skip():
                return jax.tree.map(
                    lambda s: jnp.zeros(s.shape, s.dtype), jax.eval_shape(stage)
                )

            return lax.cond(always, stage, skip)

        def meet(*values):
            return lax.optimization_barrier(values)

        def line(vec):
            return vec.reshape(1, -1)

        def rolled(step):
            return lambda i, *_: (0, i) if step == 1 else (i, 0)

        half_shape = shape_of((half, D))
        half_tile = pl.BlockSpec((half // tiles, D), rolled(0))
        tok_mine = pl.BlockSpec((half // tiles, D), lambda i, m: (m[0] * tiles + i, 0))
        ext_spec, ext_shape = whole((half + 8, D)), shape_of((half + 8, D))
        dh_spec, dh_shape = whole((half, D + 128)), shape_of((half, D + 128))
        dh_tile = pl.BlockSpec((half // tiles, D + 128), rolled(0))
        row_spec = whole((1, D))
        wide_spec, wide_shape = whole((rows, width)), shape_of((rows, width))
        quad = pl.BlockSpec((rows, QUAD), rolled(1))
        quad_weight = pl.BlockSpec((3, D, QUAD), lambda i, *_: (0, 0, i))
        probs_spec = pl.BlockSpec((4, rows, rows), lambda i, *_: (i, 0, 0))
        table_spec = whole((4, rows, PAIR))
        wide = pl.BlockSpec((1, span), rolled(1))
        tall = pl.BlockSpec((D, span), rolled(1))
        flat = pl.BlockSpec((span, D), rolled(0))
        half_part = pl.BlockSpec((half, span), rolled(1))
        many = pl.BlockSpec((rows, span), rolled(1))
        low_hidden = shape_of((rows, hidden), bf16)
        low_rows = shape_of((rows, D), bf16)
        tiny2, tiny4 = shape_of((rows, 2)), shape_of((rows, 4))
        tile = pl.BlockSpec((block, span), rolled(1))
        sum_tile = pl.BlockSpec((8, span), rolled(1))
        gain2, shift2, bias2 = line(sub2_gain), line(sub2_shift), line(up_bias)

        dy = Order(meta).run(
            mask_kernel,
            (2,),
            [pl.BlockSpec((half // 2, D), lambda i, m: (m[0] * 2 + i, 0))],
            pl.BlockSpec((half // 2, D), rolled(0)),
            half_shape,
            (cotangent,),
        )
        if full:
            dy_e1, dy_m1 = to_batch(dy, 2), to_middle(dy)

        def attention():
            order = Order(meta)
            low_shape = shape_of((rows, width), bf16)
            a, q, k, v, probs, o, y_mine, y_other, *a_sent = order.run(
                functools.partial(attend_kernel, nb),
                (quads,),
                [whole((rows, D)), row_spec, row_spec, quad_weight, whole((3, heads, HD)),
                 whole((heads, HD)), whole((heads, HD)), whole((width, D)), table_spec],
                    [whole((rows, D)), quad, quad, quad, probs_spec, wide_spec, ext_spec, ext_spec]
                + [whole((half, 2 * block))] * sends,
                [low_rows, low_shape, low_shape, low_shape,
                 shape_of((heads, rows, rows)), wide_shape, ext_shape, ext_shape]
                + [shape_of((half, 2 * block))] * sends,
                (tokens, line(norm1_gain), line(norm1_shift), weight, qkv_bias, sub1_gain,
                 sub1_shift, out_weight, table),
                [pltpu.VMEM((rows, D), bf16), pltpu.VMEM((rows, width), f32)],
            )
            y_pair = y_mine + to_core(y_other)
            return a, q, k, v, probs, o, y_pair, a_sent

        a, q, k, v, probs, o, y_pair, a_sent = segment(attention)
        if full:
            dy_e1, dy_m1, y_pair, a_sent = meet(dy_e1, dy_m1, y_pair, a_sent)
            a_got = [None, to_batch(a_sent[1], 2), to_batch(a_sent[2], 3)]
            dy_f1, dy_m2 = outward(dy_m1), to_middle(dy_e1)

        def after_attention():
            order = Order(meta)
            y_cross = to_y(y_pair)
            dw, dyl = order.run(
                dw_kernel,
                (chunks,),
                [whole((rows, D)), flat],
                [many, whole((rows, D))],
                [low_hidden, low_rows],
                (cotangent, down_weight),
            )
            return dw, dyl, order.run(
                functools.partial(middle_kernel, attn_width),
                (tiles,),
                [half_tile, half_tile] + [pl.BlockSpec((8, D), lambda i, *_: (half // 8, 0))] * 2
                + [tok_mine] + [row_spec] * 3,
                [half_tile] * 3 + [whole((8, D)), whole((rows, 2))],
                [half_shape] * 3 + [shape_of((8, D)), tiny2],
                (y_pair, y_cross, y_pair, y_cross, tokens, line(out_bias), line(norm2_gain),
                 line(norm2_shift)),
            )

        dw, dyl, (h1, branch, b_mine, vecs, stats) = segment(after_attention)
        if full:
            dy_f1, dy_m2, b_mine, a_sent, a_got[1], a_got[2] = meet(
                dy_f1, dy_m2, b_mine, a_sent, a_got[1], a_got[2]
            )
            a_got[0] = to_batch(a_sent[0], 1)
            b_e1, b_m1 = to_batch(b_mine, 2), to_middle(b_mine)

        def hidden_first():
            order = Order(meta)
            dy_core = to_core(dy_e1) if full else ()
            g, slope, stats_g, b = order.run(
                first_kernel,
                (chunks,),
                [whole((half, D))] * 2 + [tall, wide, wide, many],
                [many, many, whole((rows, 4)), whole((rows, D))],
                [low_hidden, low_hidden, tiny4, low_rows],
                (b_mine, to_core(b_mine), up_weight, bias2, gain2, dw),
                [pltpu.VMEM((rows, 1), f32)] * 4,
            )
            return g, slope, lax.all_gather(stats_g, "mp"), b, dy_core

        g, slope, g_stats, b, dy_core = segment(hidden_first)
        if full:
            b_e1, b_m1, a_got, g, dy_core = meet(b_e1, b_m1, a_got, g, dy_core)
            b_f1, b_m2 = outward(b_m1), to_middle(b_e1)

        def hidden_back():
            order = Order(meta)
            b_core, a_core = (to_core(b_e1), [to_core(a_got[1])]) if full else ((), [])
            w, du, st, h_sum, db_mine, db_other = order.run(
                functools.partial(back_kernel, ff_width, span),
                (parts,),
                [whole((rows, hidden))] * 3 + [whole((nm, rows, 4))]
                + [whole((1, hidden))] * 2 + [pl.BlockSpec((span, hidden), rolled(0))],
                [whole((rows, hidden))] * 2 + [whole((rows, 4)), whole((8, hidden))]
                + [half_part] * 2,
                [low_hidden, low_hidden, tiny4, shape_of((8, hidden)), half_shape, half_shape],
                (g, slope, dw, g_stats, gain2, shift2, up_weight),
            )
            return w, du, st, h_sum, db_mine + to_core(db_other), b_core, a_core

        w, du, st, h_sum, db_pair, b_core, a_core = segment(hidden_back)
        if full:
            b_f1, b_m2, db_pair, b_core = meet(b_f1, b_m2, db_pair, b_core)
            st_near = to_batch(st, 2)
            st_near, dy_m2, b_m2, st = meet(st_near, dy_m2, b_m2, st)
            dy_f2, b_f2, st_six = outward(dy_m2), outward(b_m2), to_batch(st, 6)
        db_cross = to_y(db_pair)

        def far_pass(order, b_src, d_src, starts, lower, stats_in, own, wait=()):
            size = len(starts) * rows
            cols = [
                pl.BlockSpec((rows, block), lambda i, m: (0, m[2])),
                pl.BlockSpec((rows, block), lambda i, m: (0, m[2] ^ 1)),
            ] * 2
            near_tile = pl.BlockSpec((2 * block + 8, span), rolled(1))
            fresh = own[0].dtype == bf16
            if fresh:
                w_own, du_own, sum_own, b_own, d_own = own
                tail = (w_own, du_own, sum_own, b_own, b_own, d_own, d_own)
                specs = [many, many, sum_tile] + cols
            else:
                tail, specs = tuple(own), [tile, tile, near_tile]
            count = 4 * len(starts)
            sources = (*b_src, *d_src)
            return order.run(
                functools.partial(far_kernel, starts, lower, fresh),
                (chunks,),
                [pl.BlockSpec(memory_space=pl.ANY)] * len(sources)
                + [whole((rows, 4))] * len(stats_in)
                + [tall, wide, wide, wide, flat]
                + specs,
                [tile, tile, near_tile],
                [shape_of((block, hidden))] * 2 + [shape_of((2 * block + 8, hidden))],
                (*sources, *stats_in, up_weight, bias2, gain2, shift2, down_weight, *tail),
                [pltpu.VMEM((size, D), bf16)] * 2
                + [pltpu.VMEM((size, 4), f32), pltpu.VMEM((count, half, D), f32),
                   pltpu.SemaphoreType.DMA((count,))],
                wait=wait,
            )

        early = Order(meta, COVER)
        if full:
            sums = far_pass(
                early, [b_e1, b_core], [dy_e1, dy_core], (((0, 0), (1, 0)),), 0,
                (st_near, st_near), (w, du, h_sum, b, dyl),
            )
        dh_mine, d_sums, *dh_sent = early.run(
            functools.partial(norm2_kernel, nb),
            (tiles,),
            [half_tile] * 5 + [whole((8, D)), row_spec],
            [dh_tile, whole((8, D))]
            + [pl.BlockSpec((half // tiles, 2 * block), rolled(0))] * sends,
            [dh_shape, shape_of((8, D))] + [shape_of((half, 2 * block))] * sends,
            (db_pair, db_cross, h1, dy, branch, vecs, line(norm2_gain)),
        )
        if full:
            st_six, dy_f2, dh_mine, dh_sent, st = meet(st_six, dy_f2, dh_mine, dh_sent, st)
            st_far = (st_six, to_batch(st, 4))

        def attention_back():
            order = Order(meta)
            dh_other = to_core(dh_mine)
            a_late = [to_core(a_got[0]), to_core(a_got[2])] if full else ()
            dm, dv, h_sums, dhl = order.run(
                functools.partial(attend_back_kernel, attn_width),
                (quads,),
                [dh_spec, dh_spec, wide_spec, whole((rows, 2)), whole((heads, HD)),
                 whole((heads, HD)), whole((width, D)), quad, quad, quad, probs_spec, table_spec],
                [whole((rows, 3 * width)), wide_spec, whole((8, width)), whole((rows, D))],
                [shape_of((rows, 3 * width)), wide_shape, shape_of((8, width)), low_rows],
                (dh_mine, dh_other, o, stats, sub1_gain, sub1_shift, out_weight, q, k, v, probs,
                 table),
                [pltpu.VMEM((rows, width), bf16)],
            )
            return dm, dv, h_sums, dhl, a_late

        dm, dv, h_sums, dhl, a_late = segment(attention_back)
        main = Order(meta, COVER)
        if full:
            b_f2, st_far, dm, dv, dh_sent = meet(b_f2, st_far, dm, dv, dh_sent)
            dm_x, dm_z = to_batch(dm, 1), to_batch(dm, 2)
            dh_got = [None, to_batch(dh_sent[1], 2), None]

        both = pl.BlockSpec((rows, span), rolled(1))

        def prepare():
            order = Order(meta)
            packed = ()
            if full:
                far = order.run(
                    pack_kernel,
                    (1,),
                    [pl.BlockSpec(memory_space=pl.ANY)] * 8,
                    pl.BlockSpec(memory_space=pl.ANY),
                    shape_of((2 * rows, D)),
                    (b_m1, b_f1, b_m2, b_f2, dy_m1, dy_f1, dy_m2, dy_f2),
                    [pltpu.VMEM((4, half, D), f32), pltpu.SemaphoreType.DMA((8,))],
                )
                packed = [far, to_core(far)]
            tail_mine, tail_other = order.run(
                tail_kernel,
                (parts,),
                [whole((rows, 3 * width)),
                 pl.BlockSpec((3, span, width), lambda i, *_: (0, i, 0)),
                 whole((rows, hidden)), pl.BlockSpec((hidden, span), rolled(1))],
                [both] * 2,
                [shape_of((rows, D))] * 2,
                (dm, weight, w, down_weight),
                [pltpu.VMEM((rows, 3 * width), bf16)],
            )
            return packed, tail_mine + to_core(tail_other)

        packed, da_pair = segment(prepare)
        if full:
            dm_x, dm_z, packed, dv, dh_sent, da_pair = meet(dm_x, dm_z, packed, dv, dh_sent, da_pair)
            dv_x = to_batch(dv, 1)
            dm_d = to_batch(dm_x, 2)
            dh_got[0] = to_batch(dh_sent[0], 1)
            da_cross = to_y(da_pair)
            sums = far_pass(
                main, packed, packed, (((0, 0), (1, 0)), ((0, half), (1, half))), rows,
                (st_far[0], st_far[1], st_far[1], st_far[0]), sums,
            )

        if full:
            dv_x, sums = meet(dv_x, sums)
            near_got = to_batch(sums[2], 1)
            dm_d, dh_got[0], dh_got[1], dm, dv, dv_x, dh_sent = meet(
                dm_d, dh_got[0], dh_got[1], dm, dv, dv_x, dh_sent
            )
            dh_got[2] = to_batch(dh_sent[2], 3)
            dv_z, dv_d = to_batch(dv, 2), to_batch(dv_x, 2)
            a_join = [*a_got, a_late[0], *a_core, a_late[1]]

            def square(left, got, sides):
                def piece(array, s):
                    at = s if array.shape[0] > half else 0
                    return pl.BlockSpec((half, 2 * block), lambda i, *_: (at, 0))

                cut = sides[0].shape[1]
                return main.run(
                    functools.partial(square_kernel, nb),
                    (1,),
                    [whole((rows, D))] + [piece(got[i], i % 3) for i in range(6)]
                    + [whole((rows, cut))] * 4,
                    [whole((block, cut))] * 2,
                    [shape_of((block, cut))] * 2,
                    (left, *got, *sides),
                    [pltpu.VMEM((4 * rows, 2 * block), bf16), pltpu.VMEM((4 * rows, cut), bf16)],
                )

            one_own, one_mirror = square(a, a_join, [dm, dm_x, dm_z, dm_d])
            one_got = to_batch(one_mirror, 4)
        else:
            da_cross = to_y(da_pair)
        row_tile = pl.BlockSpec((half // tiles, D), rolled(0))
        row_mod = pl.BlockSpec((half // tiles, D), lambda i, *_: (i % tiles, 0))
        last = main.last

        def input_norm_back():
            order = Order(meta)
            order.last = last
            joined = ()
            if full:
                dh_all = Order(meta).run(
                    join_kernel,
                    (1,),
                    [pl.BlockSpec(memory_space=pl.ANY)] * 3,
                    pl.BlockSpec(memory_space=pl.ANY),
                    shape_of((3 * half, 2 * block)),
                    dh_got,
                    [pltpu.VMEM((3, half, 2 * block), f32), pltpu.SemaphoreType.DMA((6,))],
                )
                joined = [dh_all] * 3 + [to_core(dh_all)] * 3
            outs = order.run(
                norm1_kernel,
                (2 * tiles,),
                [row_tile, row_tile, row_mod,
                 pl.BlockSpec((half // tiles, D), lambda i, m: (m[0] * tiles + i % tiles, 0)),
                 pl.BlockSpec((half // tiles, D + 128), lambda i, *_: (i % tiles, 0)), row_spec,
                 row_spec, whole((8, D))],
                [row_tile, whole((8, D))],
                [shape_of((rows, D)), shape_of((8, D))],
                (da_pair, da_cross, h1, tokens, dh_mine, line(norm1_gain),
                 line(down_bias), d_sums),
            )
            return outs, joined

        (mine, d_sums), dh_join = segment(input_norm_back)
        if full:
            dv_z, dv_d, dh_join = meet(dv_z, dv_d, dh_join)
            two_own, two_mirror = square(dhl, dh_join, [dv, dv_x, dv_z, dv_d])
            two_got = to_batch(two_mirror, 4)

        def place():
            order = Order(meta)
            sums = d_sums + to_core(d_sums)
            other = to_core(mine)
            outs = [
                order.run(
                    place_kernel,
                    (2 * tiles,),
                    [pl.BlockSpec((half // tiles, D), functools.partial(
                        lambda first, i, *_: (first + i % tiles, 0), first))] * 2,
                    row_tile,
                    low_rows,
                    (mine, other),
                )
                for first in (tiles, 0)
            ]
            return (*outs, sums)

        result, tokens_grad, d_sums = segment(place)

        lanes = hidden // 128
        per = 128 // nb
        if not full:

            def scatter(value, axis):
                return lax.psum_scatter(value, "batch", scatter_dimension=axis, tiled=True)

            d_sums = scatter(d_sums, 1)
            h_sums = lax.psum(h_sums, "batch")
            h_parts = scatter(h_sum[:3].reshape(3, lanes, 128), 2)
            dm_low, z = dm.astype(bf16), dv
            grad_qkv = scatter(
                jnp.stack([mm_tn(a, dm_low[:, j * width : (j + 1) * width]) for j in range(3)], 1), 0
            )
            grad_out = scatter(mm_tn(z.astype(bf16), dhl), 1)
            grad_up = scatter(mm_tn(b, du), 0)
            grad_down = scatter(mm_tn(w, dyl), 1)
        else:
            comb = jnp.concatenate([d_sums, h_sums], axis=1)
            comb_x = to_batch(comb, 1)
            h_parts = (sums[2][2 * block :] + near_got[2 * block :])[:3]
            h_parts = lax.dynamic_slice_in_dim(
                h_parts.reshape(3, lanes, 128), index * per, per, 2
            )
            strip = hidden // 4
            grad_up, grad_down = main.run(
                final_hidden_kernel,
                (4,),
                [pl.BlockSpec((block, strip), rolled(1))] * 3
                + [pl.BlockSpec((block, strip), lambda i, *_: (1, i))],
                [pl.BlockSpec((block, strip), rolled(1)), pl.BlockSpec((strip, block), rolled(0))],
                [shape_of((block, hidden)), shape_of((hidden, block))],
                (sums[0], near_got, sums[1], near_got),
            )
            comb, comb_x, grad_up = meet(comb, comb_x, grad_up)

            def small_sums():
                total = comb + comb_x
                return total + to_batch(total, 2)

            comb = segment(small_sums)
            comb_far = to_batch(comb, 4)
            main.last = [comb]
            grad_qkv, grad_out = main.run(
                final_square_kernel,
                (1,),
                [whole((block, 3 * width))] * 2 + [whole((block, width))] * 2,
                [whole((3, block, width)), whole((width, block))],
                [shape_of((3, block, width)), shape_of((width, block))],
                (one_own, one_got, two_own, two_got),
            )
            comb = comb + comb_far
            d_sums = lax.dynamic_slice_in_dim(comb, index * block, block, 1)
            h_sums = comb[:, D:]
            grad_qkv = jnp.transpose(grad_qkv, (1, 0, 2))
        per = HD // nb

        def own_part(value, shape):
            return lax.dynamic_slice_in_dim(value.reshape(shape), index * per, per, len(shape) - 1)

        return (
            result,
            tokens_grad,
            d_sums[4],
            d_sums[5],
            grad_qkv,
            own_part(h_sums[2:5], (3, heads, HD)),
            own_part(h_sums[0], (heads, HD)),
            own_part(h_sums[1], (heads, HD)),
            grad_out,
            d_sums[2],
            d_sums[0],
            d_sums[1],
            grad_up,
            h_parts[0],
            h_parts[1],
            h_parts[2],
            grad_down,
            d_sums[3],
        )

    return local


def solution(mesh):
    in_specs = (
        P("batch", None),
        P("batch"),
        P("batch", None),
        P(),
        P(),
        P(None, None, "mp"),
        P(None, "mp", None),
        P("mp", None),
        P("mp", None),
        P("mp", None),
        P(),
        P(),
        P(),
        P(None, "mp"),
        P("mp"),
        P("mp"),
        P("mp"),
        P("mp", None),
        P(),
    )
    out_specs = (
        P("batch", None),
        P("batch", None),
        P("batch"),
        P("batch"),
        P("batch", None, "mp"),
        P(None, "mp", "batch"),
        P("mp", "batch"),
        P("mp", "batch"),
        P("mp", "batch"),
        P("batch"),
        P("batch"),
        P("batch"),
        P("batch", "mp"),
        P("mp", "batch"),
        P("mp", "batch"),
        P("mp", "batch"),
        P("mp", "batch"),
        P("batch"),
    )
    local = make_local(mesh.shape["batch"], mesh.shape["mp"])
    return jax.shard_map(local, mesh=mesh, in_specs=in_specs, out_specs=out_specs, check_vma=False)
```

```python
import functools
import math

import jax
import jax.numpy as jnp
import numpy as np
from jax import lax
from jax.experimental import pallas as pl
from jax.experimental.pallas import tpu as pltpu
from jax.sharding import PartitionSpec as P

HD = 64
QUAD = 4 * HD
PAIR = 2 * HD

norm_eps = 1e-05
rope_base = 10000.0
xpos_base = 512.0
masked_score = -1e30
root_half = 2.0**-0.5
density_scale = 1.0 / math.sqrt(2.0 * math.pi)
f32 = jnp.float32
bf16 = jnp.bfloat16
MIB = 1 << 20
COVER = 10**11


def dot(a, b, dims):
    return lax.dot_general(a, b, (dims, ((), ())), preferred_element_type=f32)


def mm(a, b):
    return dot(a, b, ((1,), (0,)))


def mm_nt(a, b):
    return dot(a, b, ((1,), (1,)))


def mm_tn(a, b):
    return dot(a, b, ((0,), (0,)))


def row_mean(value):
    return jnp.mean(value, axis=-1, keepdims=True)


def row_sum(value):
    return jnp.sum(value, axis=-1, keepdims=True)


def unit_rows(value):
    center = value - row_mean(value)
    inverse = lax.rsqrt(row_mean(center * center) + norm_eps)
    return center * inverse, inverse


def unit_back(grad, unit, inverse, gain):
    scaled = grad * gain
    return inverse * (scaled - row_mean(scaled) - unit * row_mean(scaled * unit))


def turn_tables(count):
    half = HD // 2
    places = np.arange(count, dtype=np.float64)[:, None]
    pair = np.arange(half, dtype=np.float64)[None, :]
    angles = places * rope_base ** (-2.0 * pair / HD)
    zeta = (2.0 * pair + 0.4 * HD) / (1.4 * HD)
    factor = zeta ** ((places - count // 2) / xpos_base)
    tables = []
    for scale in (factor, 1.0 / factor):
        tables.append(np.tile(np.cos(angles) * scale, (1, 4)))
        tables.append(np.tile(np.concatenate([-np.sin(angles), np.sin(angles)], 1), (1, 2))
                      * np.tile(scale, (1, 4)))
    return np.stack(tables).astype(np.float32)


def half_swap(value):
    lane = lax.broadcasted_iota(jnp.int32, value.shape, 1)
    return jnp.where(
        (lane & 32) == 0,
        pltpu.roll(value, value.shape[1] - 32, 1),
        pltpu.roll(value, 32, 1),
    )


def whole(shape):
    return pl.BlockSpec(shape, lambda *_: (0,) * len(shape))


def shape_of(shape, dtype=f32):
    return jax.ShapeDtypeStruct(shape, dtype)


def call(body, grid, ins, outs, shapes, scratch=(), tokens=0, cover=0):
    count = len(ins)

    def kernel(meta, *refs):
        body(meta, *refs[:count], *refs[count + tokens :])

    return pl.pallas_call(
        kernel,
        grid_spec=pltpu.PrefetchScalarGridSpec(
            num_scalar_prefetch=1,
            grid=grid,
            in_specs=list(ins) + [pl.BlockSpec(memory_space=pl.ANY)] * tokens,
            out_specs=outs,
            scratch_shapes=list(scratch),
        ),
        out_shape=shapes,
        compiler_params=pltpu.CompilerParams(
            dimension_semantics=("arbitrary",) * len(grid), vmem_limit_bytes=64 * MIB
        ),
        cost_estimate=pl.CostEstimate(flops=cover, bytes_accessed=0, transcendentals=0)
        if cover
        else None,
    )


class Order:
    def __init__(self, meta, cover=0):
        self.meta = meta
        self.last = []
        self.cover = cover

    def run(self, body, grid, ins, outs, shapes, args, scratch=(), wait=()):
        extra = list(wait) + self.last
        made = call(body, grid, ins, outs, shapes, scratch, len(extra), self.cover)(
            self.meta, *args, *extra
        )
        self.last = [made[0] if isinstance(made, (list, tuple)) else made]
        return made


def half_at(meta, which, half):
    return pl.ds(pl.multiple_of(((meta[0] + which) % 2) * half, half), half)


def spread(ref, count, first=0):
    return jnp.concatenate([ref[pl.ds(first + i, 1), :] for i in range(count)], axis=1)


def mask_kernel(meta, cot, mine):
    size = mine.shape[0]
    first = (meta[0] * pl.num_programs(0) + pl.program_id(0)) * size
    place = first + lax.broadcasted_iota(jnp.int32, (size, 1), 0)
    mine[...] = cot[...].astype(f32) * jnp.where(place < meta[1], 1.0, 0.0)


def send_pieces(meta, value, outs, block):
    for s, out in enumerate(outs):
        at = meta[2] ^ (s + 1)
        for part, where in ((0, at), (1, at ^ 4)):
            cols = pl.ds(pl.multiple_of(where * block, block), block)
            out[:, part * block : (part + 1) * block] = value[:, cols].astype(f32)


def flip_rows(value, half):
    return jnp.concatenate(
        [
            value[(i ^ 1) * half : ((i ^ 1) + 1) * half]
            for i in range(value.shape[0] // half)
        ],
        axis=0,
    )


def join_two(one, two, count):
    mean = 0.5 * (one[0] + two[0])
    gap = one[0] - two[0]
    joined = [mean, one[1] + two[1] + (0.5 * count) * gap * gap]
    if len(one) > 2:
        joined += [
            one[2] + two[2],
            one[3] + two[3] + one[2] * (one[0] - mean) + two[2] * (two[0] - mean),
        ]
    return joined


def join_all(ref, odd, count):
    cols = []
    for i in range(ref.shape[0]):
        value = ref[i]
        half = value.shape[0] // 2
        value = jnp.where(odd == i % 2, value, flip_rows(value, half))
        cols.append([value[:, c : c + 1] for c in range(4)])
    while len(cols) > 1:
        cols = [join_two(cols[i], cols[i + 1], count) for i in range(0, len(cols), 2)]
        count *= 2
    return cols[0]


def diagonal(count):
    return lax.broadcasted_iota(jnp.int32, (count, count), 0) == lax.broadcasted_iota(
        jnp.int32, (count, count), 1
    )


def as_row(column):
    return jnp.sum(jnp.where(diagonal(column.shape[0]), column, 0.0), axis=0, keepdims=True)


def as_column(row):
    return row_sum(jnp.where(diagonal(row.shape[1]), row, 0.0))


def attend_kernel(nb, meta, tok, gain, shift, weight, bias, sub_gain, sub_shift, out_w, table,
                  a_out, q_out, k_out, v_out, p_out, o_out, y_mine, y_other,
                  *rest):
    sends, (a_low, o_all) = rest[:-2], rest[-2:]
    rows, width = o_all.shape
    half = rows // 2
    step = pl.program_id(0)
    places = lax.broadcasted_iota(jnp.int32, (rows, 1), 0) ^ (meta[0] * half)
    keys = lax.broadcasted_iota(jnp.int32, (1, rows), 1) ^ (meta[0] * half)
    allowed = (keys <= places) & (keys < meta[1])

    @pl.when(step == 0)
    def _():
        for which in range(2):
            unit, _ = unit_rows(tok[half_at(meta, which, half), :].astype(f32))
            wide = unit * gain[...] + shift[...]
            a_low[which * half : (which + 1) * half, :] = wide.astype(bf16)
        a_out[...] = a_low[...]
        if sends:
            send_pieces(meta, a_low.at[0:half, :], sends, tok.shape[1] // nb)

    turned = []
    for j in range(3):
        m = mm(a_low[...], weight[j])
        m = m + jnp.concatenate(
            [bias[j, pl.ds(step * 4 + i, 1), :] for i in range(4)], axis=1
        )
        if j < 2:
            flipped = half_swap(m)
            parts = []
            for which in range(2):
                at = half_at(meta, which, half)
                here = slice(which * half, (which + 1) * half)
                c = jnp.concatenate([table[2 * j, at, :]] * 2, axis=1)
                s = jnp.concatenate([table[2 * j + 1, at, :]] * 2, axis=1)
                parts.append(m[here] * c + flipped[here] * s)
            m = jnp.concatenate(parts, axis=0)
        turned.append(m.astype(bf16))
    q, k, v = turned
    q = q * jnp.asarray(1.0 / math.sqrt(HD), bf16)
    q_out[...] = q
    k_out[...] = k
    v_out[...] = v
    lane = lax.broadcasted_iota(jnp.int32, (1, PAIR), 1)
    for p in range(2):
        here = slice(p * PAIR, (p + 1) * PAIR)
        total = None
        for h in range(2):
            mask = (lane // HD) == h
            scores = mm_nt(jnp.where(mask, q[:, here], jnp.zeros_like(q[:, here])), k[:, here])
            scores = jnp.where(allowed, scores, masked_score)
            weights = jnp.exp(scores - jnp.max(scores, axis=-1, keepdims=True))
            probs = weights * (1.0 / row_sum(weights))
            p_out[p * 2 + h] = probs
            part = mm(
                probs.astype(bf16), jnp.where(mask, v[:, here], jnp.zeros_like(v[:, here]))
            )
            total = part if total is None else total + part
        o_all[:, pl.ds(pl.multiple_of(step * QUAD + p * PAIR, PAIR), PAIR)] = total

    @pl.when(step == pl.num_programs(0) - 1)
    def _():
        o = o_all[...]
        o_out[...] = o
        mean = row_mean(o)
        center = o - mean
        stat_rows = jnp.concatenate([as_row(mean), as_row(row_sum(center * center))], axis=0)
        heads = width // HD
        gain_row, shift_row = spread(sub_gain, heads), spread(sub_shift, heads)
        pieces = []
        for row in (gain_row, shift_row):
            for _ in range(3):
                low = row.astype(bf16)
                pieces.append(low)
                row = row - low.astype(f32)
        vecs = mm(jnp.concatenate(pieces + [jnp.zeros((2, width), bf16)], axis=0), out_w[...])
        gain_out = vecs[0:1] + vecs[1:2] + vecs[2:3]
        shift_out = vecs[3:4] + vecs[4:5] + vecs[5:6]
        extra = jnp.concatenate([gain_out, shift_out, jnp.zeros((6, vecs.shape[1]), f32)], axis=0)
        low = (center * gain_row).astype(bf16)
        for which, out in ((1, y_other), (0, y_mine)):
            here = slice(which * half, (which + 1) * half)
            out[0:half, :] = mm(low[here], out_w[...]) + mean[here] * gain_out
            out[half : half + 8, :] = extra
            for p in range(2):
                out[half + 2 + 2 * p : half + 4 + 2 * p, 0:rows] = jnp.where(
                    meta[0] == p, stat_rows, jnp.zeros_like(stat_rows)
                )


def join_rows(refs, odd, count):
    cols = []
    for ref in refs:
        half = ref.shape[1] // 2
        for p in range(2):
            rows = ref[2 + 2 * p : 4 + 2 * p, :]
            swapped = jnp.concatenate([rows[:, half:], rows[:, :half]], axis=1)
            rows = jnp.where(odd == p, rows, swapped)
            cols.append([rows[0:1], rows[1:2]])
    near = join_two(cols[0], cols[1], count)
    far = join_two(cols[2], cols[3], count)
    return join_two(near, far, 2 * count)


def middle_kernel(attn_width, meta, one, two, one_extra, two_extra, tok, bias, gain, shift,
                   h_out, branch_out, b_out, vec_out, stats):
    size = h_out.shape[0]
    step = pl.program_id(0)

    @pl.when(step == 0)
    def _():
        rows = stats.shape[0]
        extras = (one_extra.at[:, 0:rows], two_extra.at[:, 0:rows])
        mean, m2 = join_rows(extras, meta[0], attn_width // 4)
        inverse = lax.rsqrt(m2 * (1.0 / attn_width) + norm_eps)
        stats[...] = jnp.concatenate([as_column(mean), as_column(inverse)], axis=1)
        vec_out[...] = one_extra[...] + two_extra[...]

    at = pl.ds(pl.multiple_of(step * size, size), size)
    branch = stats[at, 1:2] * ((one[...] + two[...]) - stats[at, 0:1] * vec_out[0:1, :])
    branch_out[...] = branch
    h1 = tok[...].astype(f32) + (branch + vec_out[1:2, :]) + bias[...]
    h_out[...] = h1
    unit, _ = unit_rows(h1)
    b_out[...] = unit * gain[...] + shift[...]


def dw_kernel(meta, cot, weight, out, low):
    half = cot.shape[0] // 2

    @pl.when(pl.program_id(0) == 0)
    def _():
        for which in range(2):
            first = ((meta[0] + which) % 2) * half
            place = first + lax.broadcasted_iota(jnp.int32, (half, 1), 0)
            rows = cot[half_at(meta, which, half), :]
            low[which * half : (which + 1) * half, :] = jnp.where(
                place < meta[1], rows, jnp.zeros_like(rows)
            )

    out[...] = mm_nt(low[...], weight[...]).astype(bf16)


def first_kernel(meta, mine, other, weight, bias, gain, dw, g_out, slope_out, stat_out, low,
                 mean_s, m2_s, s1_s, s2_s):
    half = mine.shape[0]
    step = pl.program_id(0)
    span = weight.shape[1]

    @pl.when(step == 0)
    def _():
        low[0:half, :] = mine[...].astype(bf16)
        low[half:, :] = other[...].astype(bf16)
        for ref in (mean_s, m2_s, s1_s, s2_s):
            ref[...] = jnp.zeros_like(ref)

    done = step.astype(f32)
    share = 1.0 / (done + 1.0)
    u = mm(low[...], weight[...]) + bias[...]
    cdf = 0.5 + 0.5 * lax.erf(u * root_half)
    density = jnp.exp(-0.5 * (u * u)) * density_scale
    g = u * cdf
    slope_out[...] = (cdf + u * density).astype(bf16)
    g_out[...] = g.astype(bf16)
    scaled = dw[...].astype(f32) * gain[...]
    mean_c = row_mean(g)
    center = g - mean_c
    s1_c = row_sum(scaled)
    s2_c = row_sum(scaled * center)
    gap = mean_c - mean_s[...]
    mean_new = mean_s[...] + gap * share
    m2_s[...] += row_sum(center * center) + gap * gap * (span * done * share)
    s2_s[...] += s2_c + s1_s[...] * (mean_s[...] - mean_new) + s1_c * (mean_c - mean_new)
    s1_s[...] += s1_c
    mean_s[...] = mean_new

    @pl.when(step == pl.num_programs(0) - 1)
    def _():
        stat_out[...] = jnp.concatenate([mean_s[...], m2_s[...], s1_s[...], s2_s[...]], axis=1)


def hidden_stats(ref, odd, out, count, ff_width):
    mean, m2, s1, s2 = join_all(ref, odd, count)
    inverse = lax.rsqrt(m2 * (1.0 / ff_width) + norm_eps)
    out[...] = jnp.concatenate(
        [mean, inverse, s1 * (1.0 / ff_width), inverse * s2 * (1.0 / ff_width)], axis=1
    )


def hidden_rows(g, slope, dw, stats, gain, shift):
    inverse = stats[:, 1:2]
    unit = (g.astype(f32) - stats[:, 0:1]) * inverse
    w = (unit * gain + shift).astype(bf16)
    dw = dw.astype(f32)
    dg = inverse * (dw * gain - stats[:, 2:3] - unit * stats[:, 3:4])
    return w, (dg * slope.astype(f32)).astype(bf16), dw * unit, dw


def back_kernel(ff_width, span, meta, g, slope, dw, parts, gain, shift, weight, w_out, du_out, stats,
                sum_out, db_mine, db_other):
    half = db_mine.shape[0]

    @pl.when(pl.program_id(0) == 0)
    def _():
        hidden_stats(parts, meta[0], stats, ff_width // parts.shape[0], ff_width)
        for c in range(g.shape[1] // span):
            at = slice(c * span, (c + 1) * span)
            w, du, gain_part, dw_wide = hidden_rows(
                g[:, at], slope[:, at], dw[:, at], stats[...], gain[:, at], shift[:, at]
            )
            w_out[:, at] = w
            du_out[:, at] = du
            sum_out[:, at] = hidden_sums(du, gain_part, dw_wide)

    part = mm_nt(du_out[...], weight[...])
    db_mine[...] = part[0:half, :]
    db_other[...] = part[half:, :]


def hidden_sums(du, gain_part, dw_wide):
    return jnp.concatenate(
        [
            jnp.sum(du.astype(f32), axis=0, keepdims=True),
            jnp.sum(gain_part, axis=0, keepdims=True),
            jnp.sum(dw_wide, axis=0, keepdims=True),
            jnp.zeros((5, du.shape[1]), f32),
        ],
        axis=0,
    )


def pack_kernel(meta, *refs):
    sources, (out, buffer, sems) = refs[:8], refs[8:]
    where = meta[2] // 2
    inner = (where == 1) | (where == 2)
    half = buffer.shape[1]

    def loads(first):
        return [
            pltpu.make_async_copy(sources[2 * i + first], buffer.at[i], sems.at[i])
            for i in range(4)
        ]

    @pl.when(inner)
    def _():
        for copy in loads(0):
            copy.start()

    @pl.when(jnp.logical_not(inner))
    def _():
        for copy in loads(1):
            copy.start()

    stores = []
    for i, copy in enumerate(loads(0)):
        copy.wait()
        store = pltpu.make_async_copy(
            buffer.at[i], out.at[i * half : (i + 1) * half, :], sems.at[4 + i]
        )
        store.start()
        stores.append(store)
    for store in stores:
        store.wait()


def far_kernel(starts, lower, own, meta, *refs):
    groups = len(starts)
    count = 1 + max(source for pair in starts for source, _ in pair)
    b_src, d_src, refs = refs[:count], refs[count : 2 * count], refs[2 * count :]
    stat_refs, rest = refs[: 2 * groups], refs[2 * groups :]
    up_w, up_b, gain, shift, down_w = rest[:5]
    rest = rest[5:]
    if own:
        w_own, du_own, sum_own, *cols = rest[:7]
        rest = rest[7:]
        ins = ()
    else:
        ins, rest = rest[:3], rest[3:]
    (up_out, down_out, near_out), (b_low, d_low, stats, buffer, sem) = rest[:3], rest[3:]
    half = buffer.shape[1]
    rows = 2 * half
    block = up_out.shape[0]
    where = meta[2] // 2
    inner = (where == 1) | (where == 2)
    mine = pl.ds(pl.multiple_of(meta[2] * block, block), block)
    near = pl.ds(pl.multiple_of((meta[2] ^ 1) * block, block), block)

    @pl.when(pl.program_id(0) == 0)
    def _():
        copies = []
        for n, pair in enumerate(starts):
            for k, (refs_k, low) in enumerate(((b_src, b_low), (d_src, d_low))):
                for i, (source, first) in enumerate(pair):
                    slot = 4 * n + 2 * k + i
                    copy = pltpu.make_async_copy(
                        refs_k[source].at[first + k * lower : first + k * lower + half, :], buffer.at[slot], sem.at[slot]
                    )
                    copy.start()
                    copies.append((copy, low, n * rows + i * half, slot))
        for n in range(groups):
            stats[n * rows : (n + 1) * rows, :] = jnp.where(
                inner, stat_refs[2 * n][...], stat_refs[2 * n + 1][...]
            )
        for copy, low, at, slot in copies:
            copy.wait()
            low[at : at + half, :] = buffer[slot].astype(bf16)

    for n in range(groups):
        at = slice(n * rows, (n + 1) * rows)
        u = mm(b_low[at, :], up_w[...]) + up_b[...]
        cdf = 0.5 + 0.5 * lax.erf(u * root_half)
        density = jnp.exp(-0.5 * (u * u)) * density_scale
        dw = mm_nt(d_low[at, :], down_w[...])
        w, du, gain_part, dw_wide = hidden_rows(
            u * cdf, cdf + u * density, dw, stats[at, :], gain[...], shift[...]
        )
        terms = [
            mm_tn(b_low[at, mine], du),
            mm_tn(d_low[at, mine], w),
            mm_tn(b_low[at, near], du),
            mm_tn(d_low[at, near], w),
            hidden_sums(du, gain_part, dw_wide),
        ]
        totals = terms if n == 0 else [t + s for t, s in zip(totals, terms)]
    if own:
        terms = [
            mm_tn(cols[0][...], du_own[...]),
            mm_tn(cols[2][...], w_own[...]),
            mm_tn(cols[1][...], du_own[...]),
            mm_tn(cols[3][...], w_own[...]),
            sum_own[...],
        ]
    else:
        low, high = ins[2][0:block, :], ins[2][block : 2 * block, :]
        terms = [ins[0][...], ins[1][...], low, high, ins[2][2 * block :, :]]
    totals = [t + s for t, s in zip(totals, terms)]
    up_out[...] = totals[0]
    down_out[...] = totals[1]
    near_out[0:block, :] = totals[2]
    near_out[block : 2 * block, :] = totals[3]
    near_out[2 * block :, :] = totals[4]


def norm2_kernel(nb, meta, one, two, h1, dy, branch, vecs, gain, dh_out, sum_out, *sends):
    size, full = h1.shape
    db = one[...] + two[...]
    unit, inverse = unit_rows(h1[...])
    dh1 = dy[...] + unit_back(db, unit, inverse, gain[...])
    low = dh1.astype(bf16).astype(f32)
    dh_out[:, 0:full] = dh1
    lane = lax.broadcasted_iota(jnp.int32, (size, 128), 1)
    dh_out[:, full : full + 128] = jnp.where(
        lane == 0, row_sum(low * vecs[0:1]), row_sum(low * branch[...])
    )
    sums = jnp.concatenate(
        [
            jnp.sum(db * unit, axis=0, keepdims=True),
            jnp.sum(db, axis=0, keepdims=True),
            jnp.sum(dh1, axis=0, keepdims=True),
            jnp.sum(dy[...], axis=0, keepdims=True),
            jnp.zeros((4, full), f32),
        ],
        axis=0,
    )

    @pl.when(pl.program_id(0) == 0)
    def _():
        sum_out[...] = sums

    @pl.when(pl.program_id(0) > 0)
    def _():
        sum_out[...] += sums
    if sends:
        send_pieces(meta, dh_out, sends, full // nb)


def attend_back_kernel(attn_width, meta, dh_mine, dh_other, o_all, stats, sub_gain, sub_shift, out_w, q_all,
                       k_all, v_all, probs_all, table, dm_out, z_out, sum_out, dhl_out, do_all):
    rows, width = o_all.shape
    half = rows // 2
    full = out_w.shape[1]
    heads = width // HD
    step = pl.program_id(0)

    @pl.when(step == 0)
    def _():
        gain_row = spread(sub_gain, heads)
        dhl = jnp.concatenate(
            [dh_mine[:, 0:full].astype(bf16), dh_other[:, 0:full].astype(bf16)], axis=0
        )
        dhl_out[...] = dhl
        sums = jnp.concatenate([dh_mine[:, full:], dh_other[:, full:]], axis=0)
        dz = mm_nt(dhl, out_w[...])
        inverse = stats[:, 1:2]
        unit = (o_all[...] - stats[:, 0:1]) * inverse
        do = inverse * (
            dz * gain_row
            - sums[:, 0:1] * (1.0 / attn_width)
            - unit * (sums[:, 1:2] * (1.0 / attn_width))
        )
        do_all[...] = do.astype(bf16)
        z_out[...] = unit * gain_row + spread(sub_shift, heads)
        sum_out[0:1, :] = jnp.sum(dz * unit, axis=0, keepdims=True)
        sum_out[1:2, :] = jnp.sum(dz, axis=0, keepdims=True)
        sum_out[5:8, :] = jnp.zeros((3, width), f32)

    quad = pl.ds(pl.multiple_of(step * QUAD, QUAD), QUAD)
    do = do_all[:, quad]
    q, k, v = q_all[...], k_all[...], v_all[...]
    lane = lax.broadcasted_iota(jnp.int32, (1, PAIR), 1)
    grads = [[], [], []]
    for p in range(2):
        here = slice(p * PAIR, (p + 1) * PAIR)
        total = [None] * 3
        for h in range(2):
            mask = (lane // HD) == h

            def only(value):
                return jnp.where(mask, value[:, here], jnp.zeros_like(value[:, here]))

            probs = probs_all[p * 2 + h]
            do_h = only(do)
            dprobs = mm_nt(do_h, v[:, here])
            inner = row_sum(probs * dprobs)
            dscores = (probs * (dprobs - inner)).astype(bf16)
            parts = (
                mm(dscores, only(k)),
                mm_tn(dscores, only(q)),
                mm_tn(probs.astype(bf16), do_h),
            )
            total = [part if t is None else t + part for t, part in zip(total, parts)]
        for j in range(3):
            grads[j].append(total[j])
    for j in range(3):
        grad = jnp.concatenate(grads[j], axis=1)
        if j == 0:
            grad = grad * (1.0 / math.sqrt(HD))
        if j < 2:
            flipped = half_swap(grad)
            parts = []
            for which in range(2):
                at = half_at(meta, which, half)
                here = slice(which * half, (which + 1) * half)
                c = jnp.concatenate([table[2 * j, at, :]] * 2, axis=1)
                s = jnp.concatenate([table[2 * j + 1, at, :]] * 2, axis=1)
                parts.append(grad[here] * c - flipped[here] * s)
            grad = jnp.concatenate(parts, axis=0)
        dm_out[:, pl.ds(pl.multiple_of(j * width + step * QUAD, QUAD), QUAD)] = grad
        sum_out[2 + j : 3 + j, quad] = jnp.sum(
            grad.astype(bf16).astype(f32), axis=0, keepdims=True
        )


def tail_kernel(meta, dm, weight, w, down_w, mine, other, low):
    half = mine.shape[0] // 2
    width = weight.shape[2]

    @pl.when(pl.program_id(0) == 0)
    def _():
        low[...] = dm[...].astype(bf16)

    total = mm_nt(low[:, 0:width], weight[0])
    for j in (1, 2):
        total = total + mm_nt(low[:, j * width : (j + 1) * width], weight[j])
    part = mm(w[...], down_w[...])
    mine[0:half, :] = total[0:half, :]
    mine[half:, :] = part[0:half, :]
    other[0:half, :] = total[half:, :]
    other[half:, :] = part[half:, :]


def norm1_kernel(meta, one, two, h1, tok, dh, gain, bias, sum_in, out, sum_out):
    full = out.shape[1]
    step = pl.program_id(0)
    total = one[...] + two[...]

    @pl.when(step == 0)
    def _():
        sum_out[...] = sum_in[...]

    @pl.when(step < pl.num_programs(0) // 2)
    def _():
        unit, inverse = unit_rows(tok[...].astype(f32))
        out[...] = dh[:, 0:full] + unit_back(total, unit, inverse, gain[...])
        sum_out[4:5, :] += jnp.sum(total * unit, axis=0, keepdims=True)
        sum_out[5:6, :] += jnp.sum(total, axis=0, keepdims=True)

    @pl.when(step >= pl.num_programs(0) // 2)
    def _():
        out[...] = h1[...] + total + bias[...]


def place_kernel(meta, mine, other, out):
    tiles = pl.num_programs(0) // 2
    local = (pl.program_id(0) // tiles) == meta[0]
    out[...] = jnp.where(local, mine[...], other[...]).astype(bf16)


def add_kernel(count, meta, *refs):
    total = refs[0][...]
    for ref in refs[1:count]:
        total = total + ref[...]
    refs[count][...] = total


def join_kernel(meta, *refs):
    pieces, (out, buffer, sems) = refs[:3], refs[3:]
    half = buffer.shape[1]
    loads = [pltpu.make_async_copy(pieces[i], buffer.at[i], sems.at[i]) for i in range(3)]
    for copy in loads:
        copy.start()
    stores = []
    for i, copy in enumerate(loads):
        copy.wait()
        store = pltpu.make_async_copy(
            buffer.at[i], out.at[i * half : (i + 1) * half, :], sems.at[3 + i]
        )
        store.start()
        stores.append(store)
    for store in stores:
        store.wait()


def square_kernel(nb, meta, own, *refs):
    mine, other, sides, (own_out, mirror_out, left, right) = refs[:3], refs[3:6], refs[6:10], refs[10:]
    rows, full = own.shape
    half, block = rows // 2, full // nb
    for part, at in ((0, meta[2]), (1, meta[2] ^ 4)):
        cols = pl.ds(pl.multiple_of(at * block, block), block)
        left[0:rows, part * block : (part + 1) * block] = own[:, cols]
    for s in range(3):
        here = rows * (s + 1)
        left[here : here + half, :] = mine[s][...].astype(bf16)
        left[here + half : here + rows, :] = other[s][...].astype(bf16)
    for s in range(4):
        right[rows * s : rows * (s + 1), :] = sides[s][...].astype(bf16)
    for out, part in ((mirror_out, block), (own_out, 0)):
        out[...] = mm_tn(left[:, part : part + block], right[...])


def final_square_kernel(meta, one_own, one_got, two_own, two_got, m_out, o_out):
    width = m_out.shape[2]
    for j in range(3):
        cols = slice(j * width, (j + 1) * width)
        m_out[j] = one_own[:, cols] + one_got[:, cols]
    o_out[...] = (two_own[...] + two_got[...]).T


def final_hidden_kernel(meta, up_own, up_got, down_own, down_got, up_out, down_out):
    up_out[...] = up_own[...] + up_got[...]
    down_out[...] = (down_own[...] + down_got[...]).T


def make_local(nb, nm):
    pair = [(i, i ^ 1) for i in range(nm)]
    cross = [(i, i ^ 2) for i in range(nm)]
    full = nb == 8
    middle_link = [(2, 4), (3, 5), (4, 2), (5, 3)]
    outward_link = [(2, 0), (3, 1), (4, 6), (5, 7)]

    def to_core(value):
        return lax.ppermute(value, "mp", pair)

    def to_y(value):
        return lax.ppermute(value, "mp", cross)

    def to_batch(value, s):
        return lax.ppermute(value, "batch", [(i, i ^ s) for i in range(nb)])

    def to_middle(value):
        return lax.ppermute(value, "batch", middle_link)

    def outward(value):
        return lax.ppermute(value, "batch", outward_link)

    def local(
        tokens,
        lengths,
        cotangent,
        norm1_gain,
        norm1_shift,
        qkv_weight,
        qkv_bias,
        sub1_gain,
        sub1_shift,
        out_weight,
        out_bias,
        norm2_gain,
        norm2_shift,
        up_weight,
        up_bias,
        sub2_gain,
        sub2_shift,
        down_weight,
        down_bias,
    ):
        rows, D = tokens.shape
        half = rows // 2
        width = out_weight.shape[0]
        heads = width // HD
        hidden = up_weight.shape[1]
        attn_width = width * nm
        ff_width = hidden * nm
        block = D // nb
        span = 512
        chunks = hidden // span
        parts = D // span
        quads = heads // 4
        sends = 3 if full else 0
        tiles = 4
        index = lax.axis_index("batch")
        meta = jnp.stack([lax.axis_index("mp") % 2, lengths[0], index]).astype(jnp.int32)
        always = lengths[0] >= 0
        table = jnp.asarray(turn_tables(rows))
        weight = jnp.transpose(qkv_weight, (1, 0, 2))

        def segment(stage):
            def skip():
                return jax.tree.map(
                    lambda s: jnp.zeros(s.shape, s.dtype), jax.eval_shape(stage)
                )

            return lax.cond(always, stage, skip)

        def meet(*values):
            return lax.optimization_barrier(values)

        def line(vec):
            return vec.reshape(1, -1)

        def rolled(step):
            return lambda i, *_: (0, i) if step == 1 else (i, 0)

        half_shape = shape_of((half, D))
        half_tile = pl.BlockSpec((half // tiles, D), rolled(0))
        tok_mine = pl.BlockSpec((half // tiles, D), lambda i, m: (m[0] * tiles + i, 0))
        ext_spec, ext_shape = whole((half + 8, D)), shape_of((half + 8, D))
        dh_spec, dh_shape = whole((half, D + 128)), shape_of((half, D + 128))
        dh_tile = pl.BlockSpec((half // tiles, D + 128), rolled(0))
        row_spec = whole((1, D))
        wide_spec, wide_shape = whole((rows, width)), shape_of((rows, width))
        quad = pl.BlockSpec((rows, QUAD), rolled(1))
        quad_weight = pl.BlockSpec((3, D, QUAD), lambda i, *_: (0, 0, i))
        probs_spec = pl.BlockSpec((4, rows, rows), lambda i, *_: (i, 0, 0))
        table_spec = whole((4, rows, PAIR))
        wide = pl.BlockSpec((1, span), rolled(1))
        tall = pl.BlockSpec((D, span), rolled(1))
        flat = pl.BlockSpec((span, D), rolled(0))
        half_part = pl.BlockSpec((half, span), rolled(1))
        many = pl.BlockSpec((rows, span), rolled(1))
        low_hidden = shape_of((rows, hidden), bf16)
        low_rows = shape_of((rows, D), bf16)
        tiny2, tiny4 = shape_of((rows, 2)), shape_of((rows, 4))
        tile = pl.BlockSpec((block, span), rolled(1))
        sum_tile = pl.BlockSpec((8, span), rolled(1))
        gain2, shift2, bias2 = line(sub2_gain), line(sub2_shift), line(up_bias)

        dy = Order(meta).run(
            mask_kernel,
            (2,),
            [pl.BlockSpec((half // 2, D), lambda i, m: (m[0] * 2 + i, 0))],
            pl.BlockSpec((half // 2, D), rolled(0)),
            half_shape,
            (cotangent,),
        )
        if full:
            dy_e1, dy_m1 = to_batch(dy, 2), to_middle(dy)

        def attention():
            order = Order(meta)
            low_shape = shape_of((rows, width), bf16)
            a, q, k, v, probs, o, y_mine, y_other, *a_sent = order.run(
                functools.partial(attend_kernel, nb),
                (quads,),
                [whole((rows, D)), row_spec, row_spec, quad_weight, whole((3, heads, HD)),
                 whole((heads, HD)), whole((heads, HD)), whole((width, D)), table_spec],
                    [whole((rows, D)), quad, quad, quad, probs_spec, wide_spec, ext_spec, ext_spec]
                + [whole((half, 2 * block))] * sends,
                [low_rows, low_shape, low_shape, low_shape,
                 shape_of((heads, rows, rows)), wide_shape, ext_shape, ext_shape]
                + [shape_of((half, 2 * block))] * sends,
                (tokens, line(norm1_gain), line(norm1_shift), weight, qkv_bias, sub1_gain,
                 sub1_shift, out_weight, table),
                [pltpu.VMEM((rows, D), bf16), pltpu.VMEM((rows, width), f32)],
            )
            y_pair = y_mine + to_core(y_other)
            return a, q, k, v, probs, o, y_pair, a_sent

        a, q, k, v, probs, o, y_pair, a_sent = segment(attention)
        if full:
            dy_e1, dy_m1, y_pair, a_sent = meet(dy_e1, dy_m1, y_pair, a_sent)
            a_got = [None, to_batch(a_sent[1], 2), to_batch(a_sent[2], 3)]
            dy_f1, dy_m2 = outward(dy_m1), to_middle(dy_e1)

        def after_attention():
            order = Order(meta)
            y_cross = to_y(y_pair)
            dw, dyl = order.run(
                dw_kernel,
                (chunks,),
                [whole((rows, D)), flat],
                [many, whole((rows, D))],
                [low_hidden, low_rows],
                (cotangent, down_weight),
            )
            return dw, dyl, order.run(
                functools.partial(middle_kernel, attn_width),
                (tiles,),
                [half_tile, half_tile] + [pl.BlockSpec((8, D), lambda i, *_: (half // 8, 0))] * 2
                + [tok_mine] + [row_spec] * 3,
                [half_tile] * 3 + [whole((8, D)), whole((rows, 2))],
                [half_shape] * 3 + [shape_of((8, D)), tiny2],
                (y_pair, y_cross, y_pair, y_cross, tokens, line(out_bias), line(norm2_gain),
                 line(norm2_shift)),
            )

        dw, dyl, (h1, branch, b_mine, vecs, stats) = segment(after_attention)
        if full:
            dy_f1, dy_m2, b_mine, a_sent, a_got[1], a_got[2] = meet(
                dy_f1, dy_m2, b_mine, a_sent, a_got[1], a_got[2]
            )
            a_got[0] = to_batch(a_sent[0], 1)
            b_e1, b_m1 = to_batch(b_mine, 2), to_middle(b_mine)

        def hidden_first():
            order = Order(meta)
            dy_core = to_core(dy_e1) if full else ()
            g, slope, stats_g, b = order.run(
                first_kernel,
                (chunks,),
                [whole((half, D))] * 2 + [tall, wide, wide, many],
                [many, many, whole((rows, 4)), whole((rows, D))],
                [low_hidden, low_hidden, tiny4, low_rows],
                (b_mine, to_core(b_mine), up_weight, bias2, gain2, dw),
                [pltpu.VMEM((rows, 1), f32)] * 4,
            )
            return g, slope, lax.all_gather(stats_g, "mp"), b, dy_core

        g, slope, g_stats, b, dy_core = segment(hidden_first)
        if full:
            b_e1, b_m1, a_got, g, dy_core = meet(b_e1, b_m1, a_got, g, dy_core)
            b_f1, b_m2 = outward(b_m1), to_middle(b_e1)

        def hidden_back():
            order = Order(meta)
            b_core, a_core = (to_core(b_e1), [to_core(a_got[1])]) if full else ((), [])
            w, du, st, h_sum, db_mine, db_other = order.run(
                functools.partial(back_kernel, ff_width, span),
                (parts,),
                [whole((rows, hidden))] * 3 + [whole((nm, rows, 4))]
                + [whole((1, hidden))] * 2 + [pl.BlockSpec((span, hidden), rolled(0))],
                [whole((rows, hidden))] * 2 + [whole((rows, 4)), whole((8, hidden))]
                + [half_part] * 2,
                [low_hidden, low_hidden, tiny4, shape_of((8, hidden)), half_shape, half_shape],
                (g, slope, dw, g_stats, gain2, shift2, up_weight),
            )
            return w, du, st, h_sum, db_mine + to_core(db_other), b_core, a_core

        w, du, st, h_sum, db_pair, b_core, a_core = segment(hidden_back)
        if full:
            b_f1, b_m2, db_pair, b_core = meet(b_f1, b_m2, db_pair, b_core)
            st_near = to_batch(st, 2)
            st_near, dy_m2, b_m2, st = meet(st_near, dy_m2, b_m2, st)
            dy_f2, b_f2, st_six = outward(dy_m2), outward(b_m2), to_batch(st, 6)
        db_cross = to_y(db_pair)

        def far_pass(order, b_src, d_src, starts, lower, stats_in, own, wait=()):
            size = len(starts) * rows
            cols = [
                pl.BlockSpec((rows, block), lambda i, m: (0, m[2])),
                pl.BlockSpec((rows, block), lambda i, m: (0, m[2] ^ 1)),
            ] * 2
            near_tile = pl.BlockSpec((2 * block + 8, span), rolled(1))
            fresh = own[0].dtype == bf16
            if fresh:
                w_own, du_own, sum_own, b_own, d_own = own
                tail = (w_own, du_own, sum_own, b_own, b_own, d_own, d_own)
                specs = [many, many, sum_tile] + cols
            else:
                tail, specs = tuple(own), [tile, tile, near_tile]
            count = 4 * len(starts)
            sources = (*b_src, *d_src)
            return order.run(
                functools.partial(far_kernel, starts, lower, fresh),
                (chunks,),
                [pl.BlockSpec(memory_space=pl.ANY)] * len(sources)
                + [whole((rows, 4))] * len(stats_in)
                + [tall, wide, wide, wide, flat]
                + specs,
                [tile, tile, near_tile],
                [shape_of((block, hidden))] * 2 + [shape_of((2 * block + 8, hidden))],
                (*sources, *stats_in, up_weight, bias2, gain2, shift2, down_weight, *tail),
                [pltpu.VMEM((size, D), bf16)] * 2
                + [pltpu.VMEM((size, 4), f32), pltpu.VMEM((count, half, D), f32),
                   pltpu.SemaphoreType.DMA((count,))],
                wait=wait,
            )

        early = Order(meta, COVER)
        if full:
            sums = far_pass(
                early, [b_e1, b_core], [dy_e1, dy_core], (((0, 0), (1, 0)),), 0,
                (st_near, st_near), (w, du, h_sum, b, dyl),
            )
        dh_mine, d_sums, *dh_sent = early.run(
            functools.partial(norm2_kernel, nb),
            (tiles,),
            [half_tile] * 5 + [whole((8, D)), row_spec],
            [dh_tile, whole((8, D))]
            + [pl.BlockSpec((half // tiles, 2 * block), rolled(0))] * sends,
            [dh_shape, shape_of((8, D))] + [shape_of((half, 2 * block))] * sends,
            (db_pair, db_cross, h1, dy, branch, vecs, line(norm2_gain)),
        )
        if full:
            st_six, dy_f2, dh_mine, dh_sent, st = meet(st_six, dy_f2, dh_mine, dh_sent, st)
            st_far = (st_six, to_batch(st, 4))

        def attention_back():
            order = Order(meta)
            dh_other = to_core(dh_mine)
            a_late = [to_core(a_got[0]), to_core(a_got[2])] if full else ()
            dm, dv, h_sums, dhl = order.run(
                functools.partial(attend_back_kernel, attn_width),
                (quads,),
                [dh_spec, dh_spec, wide_spec, whole((rows, 2)), whole((heads, HD)),
                 whole((heads, HD)), whole((width, D)), quad, quad, quad, probs_spec, table_spec],
                [whole((rows, 3 * width)), wide_spec, whole((8, width)), whole((rows, D))],
                [shape_of((rows, 3 * width)), wide_shape, shape_of((8, width)), low_rows],
                (dh_mine, dh_other, o, stats, sub1_gain, sub1_shift, out_weight, q, k, v, probs,
                 table),
                [pltpu.VMEM((rows, width), bf16)],
            )
            return dm, dv, h_sums, dhl, a_late

        dm, dv, h_sums, dhl, a_late = segment(attention_back)
        main = Order(meta, COVER)
        if full:
            b_f2, st_far, dm, dv, dh_sent = meet(b_f2, st_far, dm, dv, dh_sent)
            dm_x, dm_z = to_batch(dm, 1), to_batch(dm, 2)
            dh_got = [None, to_batch(dh_sent[1], 2), None]

        both = pl.BlockSpec((rows, span), rolled(1))

        def prepare():
            order = Order(meta)
            packed = ()
            if full:
                far = order.run(
                    pack_kernel,
                    (1,),
                    [pl.BlockSpec(memory_space=pl.ANY)] * 8,
                    pl.BlockSpec(memory_space=pl.ANY),
                    shape_of((2 * rows, D)),
                    (b_m1, b_f1, b_m2, b_f2, dy_m1, dy_f1, dy_m2, dy_f2),
                    [pltpu.VMEM((4, half, D), f32), pltpu.SemaphoreType.DMA((8,))],
                )
                packed = [far, to_core(far)]
            tail_mine, tail_other = order.run(
                tail_kernel,
                (parts,),
                [whole((rows, 3 * width)),
                 pl.BlockSpec((3, span, width), lambda i, *_: (0, i, 0)),
                 whole((rows, hidden)), pl.BlockSpec((hidden, span), rolled(1))],
                [both] * 2,
                [shape_of((rows, D))] * 2,
                (dm, weight, w, down_weight),
                [pltpu.VMEM((rows, 3 * width), bf16)],
            )
            return packed, tail_mine + to_core(tail_other)

        packed, da_pair = segment(prepare)
        if full:
            dm_x, dm_z, packed, dv, dh_sent, da_pair = meet(dm_x, dm_z, packed, dv, dh_sent, da_pair)
            dv_x = to_batch(dv, 1)
            dm_d = to_batch(dm_x, 2)
            dh_got[0] = to_batch(dh_sent[0], 1)
            da_cross = to_y(da_pair)
            sums = far_pass(
                main, packed, packed, (((0, 0), (1, 0)), ((0, half), (1, half))), rows,
                (st_far[0], st_far[1], st_far[1], st_far[0]), sums,
            )

        if full:
            dv_x, sums = meet(dv_x, sums)
            near_got = to_batch(sums[2], 1)
            dm_d, dh_got[0], dh_got[1], dm, dv, dv_x, dh_sent = meet(
                dm_d, dh_got[0], dh_got[1], dm, dv, dv_x, dh_sent
            )
            dh_got[2] = to_batch(dh_sent[2], 3)
            dv_z, dv_d = to_batch(dv, 2), to_batch(dv_x, 2)
            a_join = [*a_got, a_late[0], *a_core, a_late[1]]

            def square(left, got, sides):
                def piece(array, s):
                    at = s if array.shape[0] > half else 0
                    return pl.BlockSpec((half, 2 * block), lambda i, *_: (at, 0))

                cut = sides[0].shape[1]
                return main.run(
                    functools.partial(square_kernel, nb),
                    (1,),
                    [whole((rows, D))] + [piece(got[i], i % 3) for i in range(6)]
                    + [whole((rows, cut))] * 4,
                    [whole((block, cut))] * 2,
                    [shape_of((block, cut))] * 2,
                    (left, *got, *sides),
                    [pltpu.VMEM((4 * rows, 2 * block), bf16), pltpu.VMEM((4 * rows, cut), bf16)],
                )

            one_own, one_mirror = square(a, a_join, [dm, dm_x, dm_z, dm_d])
            one_got = to_batch(one_mirror, 4)
        else:
            da_cross = to_y(da_pair)
        row_tile = pl.BlockSpec((half // tiles, D), rolled(0))
        row_mod = pl.BlockSpec((half // tiles, D), lambda i, *_: (i % tiles, 0))
        last = main.last

        def input_norm_back():
            order = Order(meta)
            order.last = last
            joined = ()
            if full:
                dh_all = Order(meta).run(
                    join_kernel,
                    (1,),
                    [pl.BlockSpec(memory_space=pl.ANY)] * 3,
                    pl.BlockSpec(memory_space=pl.ANY),
                    shape_of((3 * half, 2 * block)),
                    dh_got,
                    [pltpu.VMEM((3, half, 2 * block), f32), pltpu.SemaphoreType.DMA((6,))],
                )
                joined = [dh_all] * 3 + [to_core(dh_all)] * 3
            outs = order.run(
                norm1_kernel,
                (2 * tiles,),
                [row_tile, row_tile, row_mod,
                 pl.BlockSpec((half // tiles, D), lambda i, m: (m[0] * tiles + i % tiles, 0)),
                 pl.BlockSpec((half // tiles, D + 128), lambda i, *_: (i % tiles, 0)), row_spec,
                 row_spec, whole((8, D))],
                [row_tile, whole((8, D))],
                [shape_of((rows, D)), shape_of((8, D))],
                (da_pair, da_cross, h1, tokens, dh_mine, line(norm1_gain),
                 line(down_bias), d_sums),
            )
            return outs, joined

        (mine, d_sums), dh_join = segment(input_norm_back)
        if full:
            dv_z, dv_d, dh_join = meet(dv_z, dv_d, dh_join)
            two_own, two_mirror = square(dhl, dh_join, [dv, dv_x, dv_z, dv_d])
            two_got = to_batch(two_mirror, 4)

        def place():
            order = Order(meta)
            sums = d_sums + to_core(d_sums)
            other = to_core(mine)
            outs = [
                order.run(
                    place_kernel,
                    (2 * tiles,),
                    [pl.BlockSpec((half // tiles, D), functools.partial(
                        lambda first, i, *_: (first + i % tiles, 0), first))] * 2,
                    row_tile,
                    low_rows,
                    (mine, other),
                )
                for first in (tiles, 0)
            ]
            return (*outs, sums)

        result, tokens_grad, d_sums = segment(place)

        lanes = hidden // 128
        per = 128 // nb
        if not full:

            def scatter(value, axis):
                return lax.psum_scatter(value, "batch", scatter_dimension=axis, tiled=True)

            d_sums = scatter(d_sums, 1)
            h_sums = lax.psum(h_sums, "batch")
            h_parts = scatter(h_sum[:3].reshape(3, lanes, 128), 2)
            dm_low, z = dm.astype(bf16), dv
            grad_qkv = scatter(
                jnp.stack([mm_tn(a, dm_low[:, j * width : (j + 1) * width]) for j in range(3)], 1), 0
            )
            grad_out = scatter(mm_tn(z.astype(bf16), dhl), 1)
            grad_up = scatter(mm_tn(b, du), 0)
            grad_down = scatter(mm_tn(w, dyl), 1)
        else:
            comb = jnp.concatenate([d_sums, h_sums], axis=1)
            comb_x = to_batch(comb, 1)
            h_parts = (sums[2][2 * block :] + near_got[2 * block :])[:3]
            h_parts = lax.dynamic_slice_in_dim(
                h_parts.reshape(3, lanes, 128), index * per, per, 2
            )
            strip = hidden // 4
            grad_up, grad_down = main.run(
                final_hidden_kernel,
                (4,),
                [pl.BlockSpec((block, strip), rolled(1))] * 3
                + [pl.BlockSpec((block, strip), lambda i, *_: (1, i))],
                [pl.BlockSpec((block, strip), rolled(1)), pl.BlockSpec((strip, block), rolled(0))],
                [shape_of((block, hidden)), shape_of((hidden, block))],
                (sums[0], near_got, sums[1], near_got),
            )
            comb, comb_x, grad_up, h_parts = meet(comb, comb_x, grad_up, h_parts)

            def small_sums():
                total = comb + comb_x
                return total + to_batch(total, 2)

            comb = segment(small_sums)
            comb_far = to_batch(comb, 4)
            main.last = [comb]
            grad_qkv, grad_out = main.run(
                final_square_kernel,
                (1,),
                [whole((block, 3 * width))] * 2 + [whole((block, width))] * 2,
                [whole((3, block, width)), whole((width, block))],
                [shape_of((3, block, width)), shape_of((width, block))],
                (one_own, one_got, two_own, two_got),
            )
            comb = comb + comb_far
            d_sums = lax.dynamic_slice_in_dim(comb, index * block, block, 1)
            h_sums = comb[:, D:]
            grad_qkv = jnp.transpose(grad_qkv, (1, 0, 2))
        per = HD // nb

        def own_part(value, shape):
            return lax.dynamic_slice_in_dim(value.reshape(shape), index * per, per, len(shape) - 1)

        return (
            result,
            tokens_grad,
            d_sums[4],
            d_sums[5],
            grad_qkv,
            own_part(h_sums[2:5], (3, heads, HD)),
            own_part(h_sums[0], (heads, HD)),
            own_part(h_sums[1], (heads, HD)),
            grad_out,
            d_sums[2],
            d_sums[0],
            d_sums[1],
            grad_up,
            h_parts[0],
            h_parts[1],
            h_parts[2],
            grad_down,
            d_sums[3],
        )

    return local


def solution(mesh):
    in_specs = (
        P("batch", None),
        P("batch"),
        P("batch", None),
        P(),
        P(),
        P(None, None, "mp"),
        P(None, "mp", None),
        P("mp", None),
        P("mp", None),
        P("mp", None),
        P(),
        P(),
        P(),
        P(None, "mp"),
        P("mp"),
        P("mp"),
        P("mp"),
        P("mp", None),
        P(),
    )
    out_specs = (
        P("batch", None),
        P("batch", None),
        P("batch"),
        P("batch"),
        P("batch", None, "mp"),
        P(None, "mp", "batch"),
        P("mp", "batch"),
        P("mp", "batch"),
        P("mp", "batch"),
        P("batch"),
        P("batch"),
        P("batch"),
        P("batch", "mp"),
        P("mp", "batch"),
        P("mp", "batch"),
        P("mp", "batch"),
        P("mp", "batch"),
        P("batch"),
    )
    local = make_local(mesh.shape["batch"], mesh.shape["mp"])
    return jax.shard_map(local, mesh=mesh, in_specs=in_specs, out_specs=out_specs, check_vma=False)
```
